32 devices in a mesh: dp: 16 (over z, y, x), chan: 2 (over core).
Axes of the slice: x: 2, y: 2, z: 4, core: 2. Of those that a mesh axis runs over, the one named last changes fastest.
Arguments:
- pixels: bfloat16 [32, 1024, 512], P('dp', None, 'chan'), may hold values from -6 to 6
- tile_ids: int32 [32, 1024], P('dp'), may hold values from 0 to 3, as said below
- first_gain: float32 [512], P('chan'), may hold values from 0.1 to 1.9
- first_shift: float32 [512], P('chan'), may hold values from -3 to 3
- first_conv: bfloat16 [9, 512, 512], P(None, None, 'chan'), may hold values from -0.09375 to 0.09375
- first_bias: float32 [512], P('chan'), may hold values from -3 to 3
- second_gain: float32 [512], P('chan'), may hold values from 0.1 to 1.9
- second_shift: float32 [512], P('chan'), may hold values from -3 to 3
- second_conv: bfloat16 [9, 512, 512], P(None, 'chan'), may hold values from -0.125 to 0.125
- second_bias: float32 [512], P('chan'), may hold values from -3 to 3
- attn_gain: float32 [512], P('chan'), may hold values from 0.1 to 1.9
- attn_shift: float32 [512], P('chan'), may hold values from -3 to 3
- query_weight: bfloat16 [512, 512], P(None, 'chan'), may hold values from -0.375 to 0.375
- query_bias: float32 [512], P('chan'), may hold values from -3 to 3
- key_weight: bfloat16 [512, 512], P(None, 'chan'), may hold values from -0.375 to 0.375
- value_weight: bfloat16 [512, 512], P(None, 'chan'), may hold values from -0.25 to 0.25
- value_bias: float32 [512], P('chan'), may hold values from -3 to 3
- proj_weight: bfloat16 [512, 512], P('chan'), may hold values from -0.5 to 0.5
- proj_bias: float32 [512], P('chan'), may hold values from -3 to 3
- cotangent: bfloat16 [32, 1024, 512], P('dp', None, 'chan'), may hold values from -6 to 6
Outputs:
- block_out: float32 [32, 1024, 512], P('dp', None, 'chan')
- pixel_grad: float32 [32, 1024, 512], P('dp', None, 'chan')
- grad_first_gain: float32 [512], P('chan')
- grad_first_shift: float32 [512], P('chan')
- grad_first_conv: float32 [9, 512, 512], P(None, None, 'chan')
- grad_first_bias: float32 [512], P('chan')
- grad_second_gain: float32 [512], P('chan')
- grad_second_shift: float32 [512], P('chan')
- grad_second_conv: float32 [9, 512, 512], P(None, 'chan')
- grad_second_bias: float32 [512], P('chan')
- grad_attn_gain: float32 [512], P('chan')
- grad_attn_shift: float32 [512], P('chan')
- grad_query_weight: float32 [512, 512], P(None, 'chan')
- grad_query_bias: float32 [512], P('chan')
- grad_key_weight: float32 [512, 512], P(None, 'chan')
- grad_value_weight: float32 [512, 512], P(None, 'chan')
- grad_value_bias: float32 [512], P('chan')
- grad_proj_weight: float32 [512, 512], P('chan')
- grad_proj_bias: float32 [512], P('chan')
The draws below stay inside these ranges and needn't reach their ends.
Inputs may be any that keep to these rules, and one draw needn't show every extreme that they name: `tile_ids`: constant over each aligned 16 x 16 tile of a canvas; the pixels of one canvas with equal ids form one image.
All inputs are finite; a program needn't handle non-finite values.
Results may differ from the reference program's by a relative error of at most 0.024.
Values may be sent and summed in bfloat16 or wider, within the bound.
No kernel may reach another device: no remote copies, remote signals or barrier semaphores. Data moves between devices by JAX's collectives and lax.ppermute only.
A program may use at most 192 MiB of HBM per device.

```python
import jax
import jax.numpy as jnp
from jax import lax

C = 512
GROUPS = 32
TILE = 16
SIDE = 32
CANVASES = 32
PIX = 1024
SLOTS = 4


def draw_tile_ids(key, part):
    per_slot = jax.random.randint(key, (CANVASES, SLOTS), 0, SLOTS)
    position = jnp.arange(SIDE * SIDE)
    row_index = position // SIDE
    col_index = position % SIDE
    slot_index = row_index // TILE * (SIDE // TILE) + col_index // TILE
    return jnp.take(per_slot, slot_index, axis=1).astype(jnp.int32)


def shard_levels(key, extent, shards, least, top_value):
    gain = 1.0
    for dim, parts in shards:
        heights = jax.random.uniform(jax.random.fold_in(jax.random.fold_in(key, 6), dim), (parts,), jnp.float32, least / len(shards), top_value / len(shards))
        gain = gain * jnp.repeat(jnp.exp(heights), extent[dim] // parts).reshape((-1,) + (1,) * (len(extent) - 1 - dim))
    return gain


def noise(key, shape, scale, limit, cuts=(), held_as=jnp.bfloat16):
    gain = shard_levels(key, shape, cuts, -0.22, 0.18) if cuts else 1.0
    drawn = jax.random.normal(key, shape, jnp.float32) * scale * gain
    return jnp.minimum(jnp.maximum(drawn, -limit), limit).astype(held_as)


def setup_inputs(seed: int = 0) -> dict:
    arg_keys = jax.random.split(jax.random.key(seed), 21)
    return {
        "pixels": noise(arg_keys[0], (CANVASES, PIX, C), 1.0, 6.0, ((0, 16), (2, 2))),
        "tile_ids": draw_tile_ids(jax.random.fold_in(arg_keys[20], 71), 0),
        "first_gain": jnp.clip(1.0 + 0.18 * jax.random.normal(arg_keys[2], (C,), jnp.float32), 0.1, 1.9),
        "first_shift": noise(arg_keys[3], (C,), 0.3, 3.0, ((0, 2),), jnp.float32),
        "first_conv": noise(arg_keys[4], (9, C, C), (9 * C) ** -0.5, 0.09375, ((2, 2),)),
        "first_bias": noise(arg_keys[5], (C,), 0.5, 3.0, ((0, 2),), jnp.float32),
        "second_gain": jnp.clip(1.0 + 0.18 * jax.random.normal(arg_keys[6], (C,), jnp.float32), 0.1, 1.9),
        "second_shift": noise(arg_keys[7], (C,), 0.3, 3.0, ((0, 2),), jnp.float32),
        "second_conv": noise(arg_keys[8], (9, C, C), (9 * C // 2) ** -0.5, 0.125, ((1, 2),)),
        "second_bias": noise(arg_keys[9], (C,), 0.3, 3.0, ((0, 2),), jnp.float32),
        "attn_gain": jnp.clip(1.0 + 0.18 * jax.random.normal(arg_keys[10], (C,), jnp.float32), 0.1, 1.9),
        "attn_shift": noise(arg_keys[11], (C,), 0.3, 3.0, ((0, 2),), jnp.float32),
        "query_weight": noise(arg_keys[12], (C, C), (C // 2) ** -0.5, 0.375, ((1, 2),)),
        "query_bias": noise(arg_keys[13], (C,), 0.5, 3.0, ((0, 2),), jnp.float32),
        "key_weight": noise(arg_keys[14], (C, C), (C // 2) ** -0.5, 0.375, ((1, 2),)),
        "value_weight": noise(arg_keys[15], (C, C), C ** -0.5, 0.25, ((1, 2),)),
        "value_bias": noise(arg_keys[16], (C,), 0.5, 3.0, ((0, 2),), jnp.float32),
        "proj_weight": noise(arg_keys[17], (C, C), (C // 4) ** -0.5, 0.5, ((0, 2),)),
        "proj_bias": noise(arg_keys[18], (C,), 0.3, 3.0, ((0, 2),), jnp.float32),
        "cotangent": noise(arg_keys[19], (CANVASES, PIX, C), 1.0, 6.0, ((0, 16), (2, 2))),
    }


EPSILON = 1e-06
OFFSETS = ((-1, -1), (-1, 0), (-1, 1), (0, -1), (0, 0), (0, 1), (1, -1), (1, 0), (1, 1))

@jax.custom_vjp
def low(v):
    return lax.optimization_barrier(v.astype(jnp.bfloat16)).astype(jnp.float32)

@jax.custom_vjp
def low_back(v):
    return v

def low_keep(v):
    return (low(v), None)

def low_pass(kept, grad):
    return (grad,)

def back_keep(v):
    return (v, None)

def back_low(kept, grad):
    return (low(grad),)
low.defvjp(low_keep, low_pass)
low_back.defvjp(back_keep, back_low)

def swish_unit(inputs):
    return inputs / (1.0 + jnp.exp(-inputs))

def group_norm(tensor, member, norm_gain, norm_shift):
    per_group = C // GROUPS
    counts = jnp.maximum(lax.optimization_barrier(jnp.sum(member, axis=0)) * per_group, 1.0)

    def seg_mean(entries):
        seg_sums = jnp.dot(member.T, entries, precision=lax.Precision.HIGHEST)
        seg_sums = lax.optimization_barrier(jnp.sum(seg_sums.reshape(seg_sums.shape[0], -1, per_group), axis=2))
        spread = jnp.dot(member, seg_sums / counts[:, None], precision=lax.Precision.HIGHEST)
        return jnp.repeat(spread, per_group, axis=1)
    centered = tensor - seg_mean(tensor)
    variance = seg_mean(centered * centered)
    return centered * lax.rsqrt(variance + EPSILON) * norm_gain + norm_shift

def shifted(tensor, row_step, col_step):
    layout = tensor.reshape(SIDE, SIDE, -1)
    padded = jnp.pad(layout, ((1, 1), (1, 1), (0, 0)))
    window = padded[1 + row_step:1 + row_step + SIDE, 1 + col_step:1 + col_step + SIDE]
    return window.reshape(SIDE * SIDE, -1)

def tap_masks(canvas_ids):
    layout = canvas_ids.reshape(SIDE, SIDE)
    padded = jnp.pad(layout, 1, constant_values=-1)
    rows = []
    for row_step, col_step in OFFSETS:
        window = padded[1 + row_step:1 + row_step + SIDE, 1 + col_step:1 + col_step + SIDE]
        rows.append((window == layout).reshape(-1))
    return jnp.stack(rows).astype(jnp.float32)

def convolve(tensor, kernel, bias, tap_mask):
    patches = []
    for tap_index, (row_step, col_step) in enumerate(OFFSETS):
        patches.append(tap_mask[tap_index][:, None] * shifted(tensor, row_step, col_step))
    patches = jnp.stack(patches)
    return jnp.einsum('tpc,tco->po', patches, kernel, precision=lax.Precision.HIGHEST) + bias

def forward(weights, tensor, member, tap_mask, same):
    first_gain, first_shift, first_conv, first_bias, second_gain, second_shift, second_conv, second_bias, attn_gain, attn_shift, query_weight, query_bias, key_weight, value_weight, value_bias, proj_weight, proj_bias = weights
    highest = lax.Precision.HIGHEST
    act1 = low(swish_unit(group_norm(tensor, member, first_gain, first_shift)))
    conv1 = low_back(convolve(act1, first_conv, first_bias, tap_mask))
    act2 = low(swish_unit(group_norm(conv1, member, second_gain, second_shift)))
    conv2 = low_back(convolve(act2, second_conv, second_bias, tap_mask))
    middle = tensor + conv2
    normed = low(group_norm(middle, member, attn_gain, attn_shift))
    queries = low(low_back(jnp.dot(normed, query_weight, precision=highest) + query_bias))
    key_rows = low(low_back(jnp.dot(normed, key_weight, precision=highest)))
    values = low(low_back(jnp.dot(normed, value_weight, precision=highest) + value_bias))
    scores = low_back(jnp.dot(queries, key_rows.T, precision=highest) * C ** (-0.5))
    masked = jnp.where(same, scores, -1e+30)
    row_max = lax.optimization_barrier(jnp.max(masked, axis=1, keepdims=True))
    expo_vals = jnp.exp(masked - row_max)
    attn_probs = low(expo_vals / lax.optimization_barrier(jnp.sum(expo_vals, axis=1, keepdims=True)))
    mixed = low(low_back(jnp.dot(attn_probs, values, precision=highest)))
    branch = low_back(jnp.dot(mixed, proj_weight, precision=highest) + proj_bias)
    return middle + branch

def reference(pixels, tile_ids, first_gain, first_shift, first_conv, first_bias, second_gain, second_shift, second_conv, second_bias, attn_gain, attn_shift, query_weight, query_bias, key_weight, value_weight, value_bias, proj_weight, proj_bias, cotangent):
    weights = tuple((item.astype(jnp.float32) for item in (first_gain, first_shift, first_conv, first_bias, second_gain, second_shift, second_conv, second_bias, attn_gain, attn_shift, query_weight, query_bias, key_weight, value_weight, value_bias, proj_weight, proj_bias)))

    def one_canvas(totals, inputs):
        tensor, canvas_ids, grad_rows = inputs
        tensor = tensor.astype(jnp.float32)
        member = (canvas_ids[:, None] == jnp.arange(SLOTS, dtype=jnp.int32)[None, :]).astype(jnp.float32)
        tap_mask = tap_masks(canvas_ids)
        same = canvas_ids[:, None] == canvas_ids[None, :]
        output, pullback = jax.vjp(lambda params, entry: forward(params, entry, member, tap_mask, same), weights, tensor)
        grad_params, grad_entry = pullback(grad_rows.astype(jnp.float32))
        totals = jax.tree.map(lambda first, second: first + second, totals, grad_params)
        return (totals, (output, grad_entry))
    zeros = jax.tree.map(jnp.zeros_like, weights)
    totals, (outputs, grads) = lax.scan(one_canvas, zeros, (pixels, tile_ids, cotangent))
    return (outputs, grads, totals[0], totals[1], totals[2], totals[3], totals[4], totals[5], totals[6], totals[7], totals[8], totals[9], totals[10], totals[11], totals[12], totals[13], totals[14], totals[15], totals[16])
```

```python
import functools
import math
import jax
import jax.numpy as jnp
from jax import lax
from jax.experimental import pallas as pl
from jax.experimental.pallas import tpu as pltpu
from jax.sharding import PartitionSpec as P

C = 512
HALF = 256
GROUP = 16
SIDE = 32
PIX = 1024
EPSILON = 1e-06
BF = jnp.bfloat16
F32 = jnp.float32
MB = 1024 * 1024
VM = pl.BlockSpec(memory_space=pltpu.VMEM)
SM = pl.BlockSpec(memory_space=pltpu.SMEM)
HBM = pl.BlockSpec(memory_space=pltpu.HBM)
SCALE = C ** (-0.5)
LOG2E = 1.4426950408889634


def dot(first, second):
    return jnp.dot(first, second, preferred_element_type=F32)


def dot_nt(first, second):
    return lax.dot_general(first, second, (((1,), (1,)), ((), ())), preferred_element_type=F32)


def dot_tn(first, second):
    return lax.dot_general(first, second, (((0,), (0,)), ((), ())), preferred_element_type=F32)


def at_row(row):
    return pl.ds(pl.multiple_of(row * SIDE, SIDE), SIDE)


def group_sums(rows):
    full = jnp.concatenate(rows, 0)
    width = full.shape[1]
    lane = lax.broadcasted_iota(jnp.int32, full.shape, 1)
    for step in (1, 2, 4, 8):
        full = full + jnp.where(
            (lane & step) == 0, pltpu.roll(full, width - step, 1), pltpu.roll(full, step, 1)
        )
    return [full[i : i + 1] for i in range(len(rows))]


def image_means(sums, eq_ref):
    rows = []
    for i in range(4):
        total, count = 0.0, 0.0
        for j in range(4):
            total = total + eq_ref[4 * i + j] * sums[j]
            count = count + eq_ref[4 * i + j]
        rows.append(total / (count * float(256 * GROUP)))
    return group_sums(rows)


def tiles_of(rows):
    return rows.reshape(2, 16, rows.shape[-1])


def pair(rows, top):
    return jnp.concatenate([rows[2 * top + side].reshape(1, 1, -1) for side in range(2)], 0)


def over_canvas(step, count, width=C, unroll=2):
    found = [[] for _ in range(count)]
    for top in range(2):
        zero = tuple(jnp.zeros((2, 16, width), F32) for _ in range(count))

        def body(index, carry, top=top):
            return tuple(a + b for a, b in zip(carry, step(top, top * 16 + index)))

        totals = lax.fori_loop(0, 16, body, zero, unroll=unroll)
        for n in range(count):
            columns = jnp.sum(totals[n], axis=1)
            found[n] += [columns[0:1], columns[1:2]]
    return found


def for_rows(step, unroll=2):
    for top in range(2):

        def body(index, carry, top=top):
            step(top, top * 16 + index)
            return carry

        lax.fori_loop(0, 16, body, 0, unroll=unroll)


def norm_stats(load, eq_ref, width):
    (sums,) = over_canvas(lambda top, row: (tiles_of(load(row)),), 1, width)
    means = image_means(sums, eq_ref)
    centers = [pair(means, top) for top in range(2)]

    def square(top, row):
        off = tiles_of(load(row)) - centers[top]
        return (off * off,)

    (squares,) = over_canvas(square, 1, width)
    rstds = [lax.rsqrt(v + EPSILON) for v in image_means(squares, eq_ref)]
    return means, rstds


def swish(value):
    half = 0.5 * value
    return half + half * jnp.tanh(half)


def norm_forward(load, out_refs, stat_ref, eq_ref, gain, shift, act):
    width = gain.shape[-1]
    means, rstds = norm_stats(load, eq_ref, width)
    stat_ref[...] = jnp.concatenate(means + rstds, 0)
    centers = [pair(means, top) for top in range(2)]
    slopes = [pair([r * gain for r in rstds], top) for top in range(2)]
    offset = shift.reshape(1, 1, width)

    def step(top, row):
        value = (tiles_of(load(row)) - centers[top]) * slopes[top] + offset
        value = act(value).reshape(SIDE, width).astype(BF)
        held = width // len(out_refs)
        for index, ref in enumerate(out_refs):
            ref[at_row(row), :] = value[:, index * held : (index + 1) * held]

    for_rows(step)


def norm_backward(load, load_grad, keep_ref, stat_ref, eq_ref, gain, shift, with_swish, finish):
    stats = stat_ref[...]
    means = [stats[i : i + 1] for i in range(4)]
    rstds = [stats[4 + i : 5 + i] for i in range(4)]
    centers = [pair(means, top) for top in range(2)]
    rates = [pair(rstds, top) for top in range(2)]
    scale, offset = gain.reshape(1, 1, C), shift.reshape(1, 1, C)

    def first(top, row):
        unit = (tiles_of(load(row)) - centers[top]) * rates[top]
        grad = tiles_of(load_grad(row))
        if with_swish:
            value = unit * scale + offset
            gate = 0.5 + 0.5 * jnp.tanh(0.5 * value)
            grad = grad * (gate * (1.0 + value * (1.0 - gate)))
            keep_ref[at_row(row), :] = grad.reshape(SIDE, C)
        return grad, grad * unit

    plain, scaled = over_canvas(first, 2)
    mean_plain = image_means([p * gain for p in plain], eq_ref)
    mean_scaled = image_means([s * gain for s in scaled], eq_ref)
    first_means = [pair(mean_plain, top) for top in range(2)]
    second_means = [pair(mean_scaled, top) for top in range(2)]

    def second(top, row):
        unit = (tiles_of(load(row)) - centers[top]) * rates[top]
        grad = tiles_of(keep_ref[at_row(row), :] if with_swish else load_grad(row))
        change = rates[top] * (grad * scale - first_means[top] - unit * second_means[top])
        finish(row, change.reshape(SIDE, C))

    for_rows(second)
    return sum(scaled), sum(plain)


def fill_patches(patch_ref, load, eq_ref):
    width = patch_ref.shape[1] // 9
    for t in range(9):
        if t // 3 == 0:
            patch_ref[SIDE : 2 * SIDE, t * width : (t + 1) * width] = jnp.zeros((SIDE, width), BF)
        if t // 3 == 2:
            patch_ref[PIX : PIX + SIDE, t * width : (t + 1) * width] = jnp.zeros((SIDE, width), BF)
    column = lax.broadcasted_iota(jnp.int32, (SIDE, 128), 0)

    def body(row, carry):
        value = load(row).astype(F32)
        moved = [pltpu.roll(value, 1, 0).astype(BF), value.astype(BF),
                 pltpu.roll(value, SIDE - 1, 0).astype(BF)]
        here = (row >= 16).astype(jnp.int32) * 2
        for t in range(9):
            down, right = t // 3 - 1, t % 3 - 1
            target = row - down
            there = (target >= 16).astype(jnp.int32) * 2

            def eq(side, source):
                return eq_ref[(there + side) * 4 + here + source]

            if right == 0:
                mask = jnp.where(column < 16, eq(0, 0), eq(1, 1))
            elif right < 0:
                mask = jnp.where(column < 16, eq(0, 0), jnp.where(column == 16, eq(1, 0), eq(1, 1)))
                mask = jnp.where(column == 0, 0.0, mask)
            else:
                mask = jnp.where(column < 15, eq(0, 0), jnp.where(column == 15, eq(0, 1), eq(1, 1)))
                mask = jnp.where(column == SIDE - 1, 0.0, mask)
            mask = mask.astype(BF)
            patch_ref[at_row(target + 1), t * width : (t + 1) * width] = moved[
                right + 1
            ] * jnp.concatenate([mask] * (width // 128), 1)
        return carry

    lax.fori_loop(0, SIDE, body, 0)


def weight_copies(core, own_ref, peer_ref, all_ref, sems, lead):
    copies = []
    for local in range(2):
        source = pl.ds(pl.multiple_of((core ^ local) * HALF, HALF), HALF)
        target = pl.ds(local * HALF, HALF)
        for which, ref in enumerate((own_ref, peer_ref)):
            held = pl.ds(which * HALF, HALF)
            if own_ref.shape[-1] == HALF:
                src, dst = (source, slice(None)), (target, held)
            else:
                src, dst = (slice(None), source), (held, target)
            copies.append(
                pltpu.make_async_copy(
                    ref.at[lead + src], all_ref.at[lead + dst], sems.at[2 * local + which]
                )
            )
    return copies


def params(limit):
    return pltpu.CompilerParams(vmem_limit_bytes=limit * MB)


def cost(micros):
    return pl.CostEstimate(flops=int(micros * 1.1e9), bytes_accessed=1 << 20, transcendentals=0)


def shape(rows, columns, dtype):
    return jax.ShapeDtypeStruct((rows, columns), dtype)


def fetch(source, target, sem):
    copy = pltpu.make_async_copy(source, target, sem)
    copy.start()
    return copy


def both_rows(own_ref, peer_ref, row):
    return jnp.concatenate([own_ref[at_row(row), :], peer_ref[at_row(row), :]], 1).astype(F32)


def act_kernel(core_ref, eq_ref, pixels_ref, vec_ref, out_ref, stat_ref, held, sem):
    fetch(pixels_ref.at[core_ref[0]], held, sem).wait()
    norm_forward(lambda row: held[at_row(row), :].astype(F32), (out_ref,), stat_ref, eq_ref,
                 vec_ref[0:1, :], vec_ref[1:2, :], swish)


def act_call(core, eq, pixels, vec):
    return pl.pallas_call(
        act_kernel, out_shape=(shape(PIX, HALF, BF), shape(8, HALF, F32)),
        in_specs=[SM, SM, HBM, VM], out_specs=(VM, VM),
        scratch_shapes=[pltpu.VMEM((PIX, HALF), BF), pltpu.SemaphoreType.DMA],
        name="act1", compiler_params=params(8), cost_estimate=cost(2),
    )(core, eq, pixels, vec)


def conv_kernel(final, core_ref, eq_ref, *refs):
    if final:
        (act_own, act_peer, own_ref, peer_ref, vec_ref, x_ref, xp_ref, sum_ref, next_ref, stat_ref,
         weight, patch, total, x_own, x_peer, sems) = refs
        extra = [fetch(x_ref.at[core_ref[0]], x_own, sems.at[5]),
                 fetch(xp_ref.at[core_ref[0]], x_peer, sems.at[6])]
        gain, shift, bias = vec_ref[6:7, :], vec_ref[7:8, :], vec_ref[5:6, :]
    else:
        (act_own, act_peer, own_ref, peer_ref, vec_ref, sum_ref, next_own, next_peer, stat_ref,
         weight, patch, total, sems) = refs
        extra = []
        gain, shift, bias = vec_ref[3:4, :], vec_ref[4:5, :], vec_ref[2:3, :]
    copies = weight_copies(core_ref[0], own_ref, peer_ref, weight, sems, (slice(None),))
    for copy in copies:
        copy.start()
    fill_patches(patch, lambda row: both_rows(act_own, act_peer, row), eq_ref)
    for copy in copies + extra:
        copy.wait()
    rows = 256

    def body(index, carry):
        start = pl.multiple_of(index * rows, rows)
        at = pl.ds(start, rows)
        value = dot(patch[pl.ds(start + SIDE, rows), :], weight[...].reshape(9 * C, C)) + bias
        if final:
            value = value + jnp.concatenate([x_own[at, :], x_peer[at, :]], 1).astype(F32)
        total[at, :] = value
        return carry

    lax.fori_loop(0, PIX // rows, body, 0)
    store = fetch(total, sum_ref, sems.at[4])
    outs = (next_ref,) if final else (next_own, next_peer)
    norm_forward(lambda row: total[at_row(row), :], outs, stat_ref, eq_ref, gain, shift,
                 (lambda v: v) if final else swish)
    store.wait()


def conv_call(core, eq, act, own, peer, vec, x=()):
    final = bool(x)
    return pl.pallas_call(
        functools.partial(conv_kernel, final),
        out_shape=(shape(PIX, C, F32),) + ((shape(PIX, C, BF),) if final else
                                           (shape(PIX, HALF, BF),) * 2) + (shape(8, C, F32),),
        in_specs=[SM, SM, VM, VM, HBM, HBM, VM] + [HBM] * len(x),
        out_specs=(HBM,) + (VM,) * (2 if final else 3),
        scratch_shapes=[pltpu.VMEM((9, C, C), BF), pltpu.VMEM((PIX + 2 * SIDE, 9 * C), BF),
                        pltpu.VMEM((PIX, C), F32)] + [pltpu.VMEM((PIX, HALF), BF)] * len(x)
        + [pltpu.SemaphoreType.DMA((7,))],
        name="conv2" if final else "conv1", compiler_params=params(28), cost_estimate=cost(9),
    )(core, eq, *act, own, peer, vec, *x)


def attn_kernel(core_ref, eq_ref, normed_ref, mid_hbm, g_own, g_peer, wq_o, wq_p, wk_o, wk_p, wv_o,
                wv_p, wp_o, wp_p, vec_ref, stat_ref, out_own, out_peer, gmid_hbm, gconv_ref,
                small_ref, dw_own, dw_peer, weight, gfull, query, keys, values, gmixed, mixed,
                dquery, probs, gscores, gnormed, mid_ref, sems):
    core = core_ref[0]
    copies = []
    for index, (own, peer) in enumerate(((wq_o, wq_p), (wk_o, wk_p), (wv_o, wv_p), (wp_o, wp_p))):
        copies += weight_copies(core, own, peer, weight.at[index], sems.at[index], ())
    for copy in copies:
        copy.start()
    copies.append(fetch(g_own.at[core], gfull.at[:, 0:HALF], sems.at[4, 0]))
    copies.append(fetch(g_peer.at[core], gfull.at[:, HALF:C], sems.at[4, 1]))
    mid_copy = fetch(mid_hbm, mid_ref, sems.at[4, 2])
    for copy in copies:
        copy.wait()
    normed = normed_ref[...]
    query[...] = (dot(normed, weight[0]) + vec_ref[8:9, :]).astype(BF)
    keys[...] = dot(normed, weight[1]).astype(BF)
    values[...] = (dot(normed, weight[2]) + vec_ref[9:10, :]).astype(BF)
    gmixed[...] = dot_nt(gfull[...], weight[3]).astype(BF)

    rows = 256
    spot = lax.broadcasted_iota(jnp.int32, (1, PIX), 1)
    right = (spot & (SIDE - 1)) >= 16
    low = spot >= PIX // 2

    def block(index, carry):
        start = pl.multiple_of(index * rows, rows)
        at = pl.ds(start, rows)
        half = (start >= PIX // 2).astype(jnp.int32) * 2
        bias = []
        for side in range(2):
            base = (half + side) * 4
            row = jnp.where(low, jnp.where(right, eq_ref[base + 3], eq_ref[base + 2]),
                            jnp.where(right, eq_ref[base + 1], eq_ref[base]))
            bias.append(jnp.where(row > 0.5, 0.0, -1e30).reshape(1, 1, 1, PIX))
        bias = jnp.concatenate(bias, 1)
        scores = dot_nt(query[at, :], keys[...]) * (SCALE * LOG2E)
        scores = (scores.reshape(rows // SIDE, 2, 16, PIX) + bias).reshape(rows, PIX)
        expo = jnp.exp2(scores - jnp.max(scores, axis=1, keepdims=True))
        wide = expo * (1.0 / jnp.sum(expo, axis=1, keepdims=True))
        narrow = wide.astype(BF)
        probs[at, :] = narrow
        mixed[at, :] = dot(narrow, values[...]).astype(BF)
        gprobs = dot_nt(gmixed[at, :], values[...])
        delta = jnp.sum(wide * gprobs, axis=1, keepdims=True)
        grads = (wide * (gprobs - delta)).astype(BF)
        gscores[at, :] = grads
        dquery[at, :] = (dot(grads, keys[...]) * SCALE).astype(BF)
        return carry

    lax.fori_loop(0, PIX // rows, block, 0)

    def narrow_out(index, full):
        full = full.astype(BF)
        for local in range(2):
            target = pl.multiple_of(index * C + (core ^ local) * HALF, HALF)
            part = full[local * HALF : (local + 1) * HALF, :]
            dw_own[pl.ds(target, HALF), :] = part[:, :HALF]
            dw_peer[pl.ds(target, HALF), :] = part[:, HALF:]

    def total(value):
        return jnp.sum(value.astype(F32), axis=0, keepdims=True)

    dkey = (dot_tn(gscores[...], query[...]) * SCALE).astype(BF)
    dvalue = dot_tn(probs[...], gmixed[...]).astype(BF)
    narrow_out(0, dot_tn(normed, dquery[...]))
    narrow_out(1, dot_tn(normed, dkey))
    narrow_out(2, dot_tn(normed, dvalue))
    dproj = dot_tn(mixed[...], gfull[...]).astype(BF)
    for local in range(2):
        target = pl.multiple_of(3 * C + (core ^ local) * HALF, HALF)
        part = dproj[:, local * HALF : (local + 1) * HALF]
        dw_own[pl.ds(target, HALF), :] = part[:HALF]
        dw_peer[pl.ds(target, HALF), :] = part[HALF:]
    gnormed[...] = dot_nt(dquery[...], weight[0]) + dot_nt(dkey, weight[1]) + dot_nt(dvalue, weight[2])
    dbq, dbv, dbp = total(dquery[...]), total(dvalue), total(gfull[...])

    mid_copy.wait()
    out = mid_ref[...] + dot(mixed[...], weight[3]) + vec_ref[10:11, :]
    out_own[...] = out[:, :HALF]
    out_peer[...] = out[:, HALF:]

    def finish(row, change):
        grad = gfull[at_row(row), :].astype(F32) + change
        gnormed[at_row(row), :] = grad
        gconv_ref[at_row(row), :] = grad.astype(BF)

    dgain, dshift = norm_backward(
        lambda row: mid_ref[at_row(row), :], lambda row: gnormed[at_row(row), :], None, stat_ref,
        eq_ref, vec_ref[6:7, :], vec_ref[7:8, :], False, finish)
    store = fetch(gnormed, gmid_hbm, sems.at[4, 3])
    small_ref[...] = jnp.concatenate(
        [dgain, dshift, dbq, dbv, dbp, total(gconv_ref[...]), dbq, dbq], 0)
    store.wait()


def attn_call(core, eq, normed, mid, g, weights, vec, stats):
    flat = [w for pair_of in weights for w in pair_of]
    return pl.pallas_call(
        attn_kernel,
        out_shape=(shape(PIX, HALF, F32), shape(PIX, HALF, F32), shape(PIX, C, F32),
                   shape(PIX, C, BF), shape(8, C, F32), shape(4 * C, HALF, BF),
                   shape(4 * C, HALF, BF)),
        in_specs=[SM, SM, VM, HBM, HBM, HBM] + [HBM] * 8 + [VM, VM],
        out_specs=(VM, VM, HBM, VM, VM, VM, VM),
        scratch_shapes=[pltpu.VMEM((4, C, C), BF)] + [pltpu.VMEM((PIX, C), BF)] * 7
        + [pltpu.VMEM((PIX, PIX), BF)] * 2 + [pltpu.VMEM((PIX, C), F32)] * 2
        + [pltpu.SemaphoreType.DMA((5, 4))],
        name="attention", compiler_params=params(44), cost_estimate=cost(20),
    )(core, eq, normed, mid, *g, *flat, vec, stats)


def wgrad2_kernel(core_ref, eq_ref, act_mine, act_other, grad_mine, grad_other, out_ref, patch,
                  patch_other):
    core = core_ref[0]
    fill_patches(patch, lambda row: act_mine[at_row(row), :], eq_ref.at[0])
    fill_patches(patch_other, lambda row: act_other[at_row(row), :], eq_ref.at[1])
    rows = slice(SIDE, SIDE + PIX)
    for group in range(3):
        columns = slice(3 * group * HALF, 3 * (group + 1) * HALF)
        for local in range(2):
            first = slice(local * HALF, (local + 1) * HALF)
            second = slice((1 - local) * HALF, (2 - local) * HALF)
            full = dot_tn(patch[rows, columns], grad_mine[:, first]) + dot_tn(
                patch_other[rows, columns], grad_other[:, second])
            full = full.astype(BF)
            for index in range(3):
                base = (3 * group + index) * C + (core ^ local) * HALF
                out_ref[pl.ds(pl.multiple_of(base, HALF), HALF), :] = full[
                    index * HALF : (index + 1) * HALF]


def wgrad2_call(core, eqs, act_mine, act_other, grad_mine, grad_other):
    return pl.pallas_call(
        wgrad2_kernel, out_shape=shape(9 * C, HALF, BF), in_specs=[SM, SM] + [VM] * 4, out_specs=VM,
        scratch_shapes=[pltpu.VMEM((PIX + 2 * SIDE, 9 * HALF), BF)] * 2,
        name="wgrad2", compiler_params=params(18), cost_estimate=cost(8),
    )(core, eqs, act_mine, act_other, grad_mine, grad_other)


TAPS = 6


def wgrad1_kernel(core_ref, eq_ref, own_mine, peer_mine, own_other, peer_other, grad_mine,
                  grad_other, out_ref, tail_ref, patch, patch_other, act, act2):
    core = core_ref[0]
    act[:, :HALF] = own_mine[...]
    act[:, HALF:] = peer_mine[...]
    act2[:, :HALF] = own_other[...]
    act2[:, HALF:] = peer_other[...]
    fill_patches(patch, lambda row: grad_mine[at_row(row), :], eq_ref.at[0])
    fill_patches(patch_other, lambda row: grad_other[at_row(row), :], eq_ref.at[1])
    rows = slice(SIDE, SIDE + PIX)
    for group in range(3):
        columns = slice(3 * group * HALF, 3 * (group + 1) * HALF)
        full = dot_tn(act[...], patch[rows, columns]) + dot_tn(act2[...], patch_other[rows, columns])
        full = full.astype(BF)
        for index in range(3):
            tap = 8 - (3 * group + index)
            out, base = (out_ref, tap * C) if tap < TAPS else (tail_ref, (tap - TAPS) * C)
            for local in range(2):
                where = pl.ds(pl.multiple_of(base + (core ^ local) * HALF, HALF), HALF)
                out[where, :] = full[local * HALF : (local + 1) * HALF,
                                     index * HALF : (index + 1) * HALF]


def wgrad1_call(core, eqs, *arrays):
    return pl.pallas_call(
        wgrad1_kernel, out_shape=(shape(TAPS * C, HALF, BF), shape((9 - TAPS) * C, HALF, BF)),
        in_specs=[SM, SM] + [VM] * 6, out_specs=(VM, VM),
        scratch_shapes=[pltpu.VMEM((PIX + 2 * SIDE, 9 * HALF), BF)] * 2 + [pltpu.VMEM((PIX, C), BF)] * 2,
        name="wgrad1", compiler_params=params(24), cost_estimate=cost(8),
    )(core, eqs, *arrays)


def dgrad_kernel(first, core_ref, eq_ref, own_ref, peer_ref, vec_ref, *refs):
    if first:
        (grad_own, grad_peer, stat_own, stat_peer, x_hbm, xp_hbm, gmid_hbm, out_own, out_peer, small_ref, weight, patch,
         total, stat_ref, sems, x_own, x_peer, gmid_ref) = refs
        stat_ref[:, :HALF] = stat_own[...]
        stat_ref[:, HALF:] = stat_peer[...]
        load = lambda row: both_rows(x_own, x_peer, row)
        load_grad = lambda row: both_rows(grad_own, grad_peer, row)
        later = [fetch(x_hbm.at[core_ref[0]], x_own, sems.at[4]),
                 fetch(xp_hbm.at[core_ref[0]], x_peer, sems.at[5]),
                 fetch(gmid_hbm, gmid_ref, sems.at[6])]
        gain, shift = vec_ref[0:1, :], vec_ref[1:2, :]
    else:
        (grad_ref, stat_in, input_hbm, out_own, out_peer, small_ref, weight, patch, total, stat_ref,
         sems, input_ref) = refs
        stat_ref[...] = stat_in[...]
        load = lambda row: input_ref[at_row(row), :]
        load_grad = lambda row: grad_ref[at_row(row), :]
        later = [fetch(input_hbm, input_ref, sems.at[4])]
        gain, shift = vec_ref[3:4, :], vec_ref[4:5, :]
    copies = weight_copies(core_ref[0], own_ref, peer_ref, weight, sems, (slice(None),))
    for copy in copies:
        copy.start()
    fill_patches(patch, load_grad, eq_ref)
    for copy in copies:
        copy.wait()
    rows = 512

    def body(index, carry):
        start = pl.multiple_of(index * rows, rows)
        at = pl.ds(start + SIDE, rows)
        value = dot_nt(patch[at, :C], weight[8])
        for t in range(1, 9):
            value = value + dot_nt(patch[at, t * C : (t + 1) * C], weight[8 - t])
        total[pl.ds(start, rows), :] = value
        return carry

    lax.fori_loop(0, PIX // rows, body, 0)
    for copy in later:
        copy.wait()

    def finish(row, change):
        at = at_row(row)
        if first:
            change = change + gmid_ref[at, :]
        out_own[at, :] = change[:, :HALF].astype(out_own.dtype)
        out_peer[at, :] = change[:, HALF:].astype(out_peer.dtype)

    dgain, dshift = norm_backward(load, lambda row: total[at_row(row), :], total, stat_ref, eq_ref,
                                  gain, shift, True, finish)
    bias = [jnp.sum(ref[...].astype(F32), axis=0, keepdims=True) for ref in (out_own, out_peer)]
    bias = jnp.concatenate(bias, 1)
    small_ref[...] = jnp.concatenate([dgain, dshift, bias] + [dgain] * 5, 0)


def dgrad_call(core, eq, grad, own, peer, vec, stats, source, gmid=None):
    first = gmid is not None
    extra = (*source, gmid) if first else source
    held = [pltpu.VMEM((PIX, HALF), BF)] * 2 if first else []
    outs = (shape(PIX, HALF, F32 if first else BF),) * 2
    return pl.pallas_call(
        functools.partial(dgrad_kernel, first),
        out_shape=outs + (shape(8, C, F32),),
        in_specs=[SM, SM, HBM, HBM, VM] + [VM] * (len(grad) + len(stats)) + [HBM] * len(extra),
        out_specs=(VM,) * 3,
        scratch_shapes=[pltpu.VMEM((9, C, C), BF), pltpu.VMEM((PIX + 2 * SIDE, 9 * C), BF),
                        pltpu.VMEM((PIX, C), F32), pltpu.VMEM((8, C), F32),
                        pltpu.SemaphoreType.DMA((7,))] + held + [pltpu.VMEM((PIX, C), F32)],
        name="dgrad1" if first else "dgrad2", compiler_params=params(32), cost_estimate=cost(10),
    )(core, eq, own, peer, vec, *grad, *stats, *extra)


def orders_of(kind, size):
    bits = size.bit_length() - 1
    low = list(range(bits - 1))
    turned = [low[k:] + low[:k] + [bits - 1] for k in range(3)]
    return (turned[0], turned[2]) if kind == 0 else (turned[1], turned[1])


def exchange(array, orders, stage, size):
    moves = [((d, c), (d ^ (1 << orders[c][stage]), c)) for d in range(size) for c in range(2)]
    return lax.ppermute(array, ("dp", "chan"), [(a[0] * 2 + a[1], b[0] * 2 + b[1]) for a, b in moves])


def side_of(orders, stage):
    bit = jnp.where(lax.axis_index("chan") == 0, orders[0][stage], orders[1][stage])
    return (lax.axis_index("dp") >> bit) & 1


def side_base(orders):
    base = 0
    for stage in range(len(orders[0])):
        base = base * 2 + side_of(orders, stage)
    return base


class Chain:
    def __init__(self, part, kind, size):
        self.value, self.size, self.orders, self.step = part, size, orders_of(kind, size), 0
        self.stages = len(self.orders[0])

    def advance(self):
        stage = self.step if self.step < self.stages else 2 * self.stages - 1 - self.step
        if self.step < self.stages:
            half = self.value.shape[0] // 2
            side = side_of(self.orders, stage)
            send = lax.dynamic_slice_in_dim(self.value, (1 - side) * half, half, 0)
            keep = lax.dynamic_slice_in_dim(self.value, side * half, half, 0)
            self.value = keep + exchange(send, self.orders, stage, self.size)
        elif stage > 0:
            self.value = jnp.concatenate(
                [self.value, exchange(self.value, self.orders, stage, self.size)], 0)
        else:
            self.value = (self.value, exchange(self.value, self.orders, stage, self.size))
        self.step += 1


def after(value, *others):
    return lax.optimization_barrier((value, *others))[0]


def together(chains, *values):
    held = lax.optimization_barrier(([c.value for c in chains], values))
    for chain, value in zip(chains, held[0]):
        chain.value = value
    return held[1]


def place_kernel(size, targets, counts, base_ref, *refs):
    ins, outs = refs[: sum(counts)], refs[sum(counts) :]
    at = 0
    for index, (count, target) in enumerate(zip(counts, targets)):
        pieces, at = ins[at : at + count], at + count
        rows = sum(ref.shape[0] for ref in pieces) // size
        piece = math.gcd(rows, HALF)
        block = 0
        for ref in pieces:
            for local in range(ref.shape[0] // rows):
                start = ((block ^ base_ref[index]) * rows)
                for offset in range(0, rows, piece):
                    row, column = target(start + offset)
                    outs[0][pl.ds(pl.multiple_of(row, piece), piece),
                            pl.ds(pl.multiple_of(column, HALF), HALF)] = ref[
                        local * rows + offset : local * rows + offset + piece, :].astype(F32)
                block += 1


def place(chains, size, targets, rows, columns):
    parts = [part for chain in chains for part in chain.value]
    return pl.pallas_call(
        functools.partial(place_kernel, size, targets, [len(chain.value) for chain in chains]),
        out_shape=shape(rows, columns, F32), in_specs=[SM] + [VM] * len(parts), out_specs=VM,
        compiler_params=params(12), name="place", cost_estimate=cost(2),
    )(jnp.stack([side_base(chain.orders) for chain in chains]).astype(jnp.int32), *parts)


def swap(array):
    return lax.ppermute(array, "chan", [(0, 1), (1, 0)])


def second_target(row):
    return row // C * HALF + row % HALF, row // HALF % 2 * HALF


def shards(pixels, tile_ids, first_gain, first_shift, first_conv, first_bias, second_gain,
           second_shift, second_conv, second_bias, attn_gain, attn_shift, query_weight,
           query_bias, key_weight, value_weight, value_bias, proj_weight, proj_bias, cotangent,
           *, size):
    index = lax.axis_index("chan")
    core = index.reshape(1).astype(jnp.int32)
    tiles = tile_ids.reshape(2, 2, 16, 2, 16)[:, :, 0, :, 0].reshape(2, 4)
    eqs = (tiles[:, :, None] == tiles[:, None, :]).astype(F32).reshape(2, 16)
    eqs = jnp.where(index == 0, eqs, eqs[::-1])
    eq = eqs[0]
    own_vectors = jnp.stack([first_gain, first_shift, first_bias, second_gain, second_shift,
                             second_bias, attn_gain, attn_shift, query_bias, value_bias, proj_bias])
    pixels_peer = swap(pixels)
    peer_vectors = swap(own_vectors)
    first_peer = swap(first_conv)
    vectors = jnp.concatenate([own_vectors, peer_vectors], 1)
    act_own, stat_own = act_call(core, eq, pixels, own_vectors)
    act_peer, stat_peer = act_call(core, eq, pixels_peer, peer_vectors)
    second_conv = after(second_conv, stat_own)
    second_peer = swap(second_conv)
    late = (query_weight, key_weight, value_weight, proj_weight, cotangent)
    *late, _ = lax.optimization_barrier((*late, first_peer))
    attn = [(w, swap(w)) for w in late[:4]]
    g = (late[4], swap(late[4]))
    x = (pixels, pixels_peer)
    wide, narrow = orders_of(0, size), orders_of(1, size)

    conv1, act2_own, act2_peer, stat2 = conv_call(
        core, eq, (act_own, act_peer), first_conv, first_peer, vectors)
    act_other = (swap(act_peer), swap(act_own))
    mid, normed, stat3 = conv_call(core, eq, (act2_own, act2_peer), second_conv, second_peer,
                                   vectors, x)
    act2_other = swap(act2_peer)
    out_own, out_peer, gmid, gconv2, small3, dattn, dattn_peer = attn_call(
        core, eq, normed, mid, g, attn, vectors, stat3)
    gconv2_other = swap(gconv2)
    attn_chain = Chain(dattn + swap(dattn_peer), 1, size)
    gconv2, gconv2_other = together([attn_chain], gconv2, gconv2_other)

    attn_chain.advance()
    part = wgrad2_call(core, eqs, act2_own, act2_other, gconv2, gconv2_other)
    second = Chain(part, 0, size)
    (gconv2,) = together([attn_chain, second], gconv2)

    attn_chain.advance()
    second.advance()
    gconv1_own, gconv1_peer, small2 = dgrad_call(
        core, eq, (gconv2,), second_conv, second_peer, vectors, (stat2,), (conv1,))
    gconv1_other = swap(gconv1_peer)
    gconv1_own, gconv1_other = together([attn_chain, second], gconv1_own, gconv1_other)

    attn_chain.advance()
    second.advance()
    part, tail = wgrad1_call(core, eqs, act_own, act_peer, *act_other, gconv1_own, gconv1_other)
    first, rest = Chain(part, 0, size), Chain(tail, 1, size)
    (gconv1_own,) = together([attn_chain, second, first, rest], gconv1_own)

    for chain in (first, rest, second, attn_chain):
        chain.advance()
    pix_own, pix_peer, small1 = dgrad_call(core, eq, (gconv1_own, gconv1_peer), first_conv,
                                           first_peer, vectors, (stat_own, stat_peer), x, gmid)
    small = jnp.concatenate([small1, small2, small3], 0)
    pix_peer, out_peer, small = together(
        [attn_chain, second, first, rest], pix_peer, out_peer, small)

    small = small[:, :HALF] + swap(small[:, HALF:])
    pix_back = swap(pix_peer)
    out_back = swap(out_peer)
    bits = size.bit_length() - 1
    turn = 0
    last = pix_back
    every = [attn_chain, second, rest, first]
    while any(chain.step < 2 * bits for chain in every):
        for chain in every:
            if chain.step < 2 * bits:
                chain.advance()
                (last,) = together([chain], last)
        if turn < bits:
            small = small + lax.ppermute(
                small, "dp", [(i, i ^ (1 << turn)) for i in range(size)])
            small = after(small, last)
        turn += 1
    summed = place([attn_chain], size, [lambda row: (row, 0)], 4 * C, HALF)
    sums3 = (summed[:C], summed[C : 2 * C], summed[2 * C : 3 * C],
             jnp.concatenate([summed[3 * C : 3 * C + HALF], summed[3 * C + HALF :]], 1))
    sums2 = place([second], size, [second_target], 9 * HALF, C)
    sums1 = place([first, rest], size,
                  [lambda row: (row, 0), lambda row: (row + TAPS * C, 0)], 9 * C, HALF)

    def unboth(own, back):
        return jnp.where(index == 0, jnp.stack([own, back]), jnp.stack([back, own]))

    return (
        unboth(out_own, out_back), unboth(pix_own, pix_back), small[0], small[1],
        sums1.reshape(9, C, HALF), small[10], small[8], small[9], sums2.reshape(9, HALF, C),
        small[21], small[16], small[17], sums3[0], small[18], sums3[1], sums3[2], small[19],
        sums3[3], small[20],
    )


def solution(mesh):
    chan = P("chan")
    rows = P("dp", None, "chan")
    return jax.shard_map(
        functools.partial(shards, size=mesh.shape["dp"]),
        mesh=mesh,
        in_specs=(
            rows, P("dp", None), chan, chan, P(None, None, "chan"), chan, chan, chan,
            P(None, "chan", None), chan, chan, chan, P(None, "chan"), chan, P(None, "chan"),
            P(None, "chan"), chan, P("chan", None), chan, rows,
        ),
        out_specs=(
            rows, rows, chan, chan, P(None, None, "chan"), chan, chan, chan,
            P(None, "chan", None), chan, chan, chan, P(None, "chan"), chan, P(None, "chan"),
            P(None, "chan"), chan, P("chan", None), chan,
        ),
        check_vma=False,
    )
```

```python
import functools
import math
import jax
import jax.numpy as jnp
from jax import lax
from jax.experimental import pallas as pl
from jax.experimental.pallas import tpu as pltpu
from jax.sharding import PartitionSpec as P

C = 512
HALF = 256
GROUP = 16
SIDE = 32
PIX = 1024
EPSILON = 1e-06
BF = jnp.bfloat16
F32 = jnp.float32
MB = 1024 * 1024
VM = pl.BlockSpec(memory_space=pltpu.VMEM)
SM = pl.BlockSpec(memory_space=pltpu.SMEM)
HBM = pl.BlockSpec(memory_space=pltpu.HBM)
SCALE = C ** (-0.5)
LOG2E = 1.4426950408889634


def dot(first, second):
    return jnp.dot(first, second, preferred_element_type=F32)


def dot_nt(first, second):
    return lax.dot_general(first, second, (((1,), (1,)), ((), ())), preferred_element_type=F32)


def dot_tn(first, second):
    return lax.dot_general(first, second, (((0,), (0,)), ((), ())), preferred_element_type=F32)


def at_row(row):
    return pl.ds(pl.multiple_of(row * SIDE, SIDE), SIDE)


def group_sums(rows):
    full = jnp.concatenate(rows, 0)
    width = full.shape[1]
    lane = lax.broadcasted_iota(jnp.int32, full.shape, 1)
    for step in (1, 2, 4, 8):
        full = full + jnp.where(
            (lane & step) == 0, pltpu.roll(full, width - step, 1), pltpu.roll(full, step, 1)
        )
    return [full[i : i + 1] for i in range(len(rows))]


def image_means(sums, eq_ref):
    rows = []
    for i in range(4):
        total, count = 0.0, 0.0
        for j in range(4):
            total = total + eq_ref[4 * i + j] * sums[j]
            count = count + eq_ref[4 * i + j]
        rows.append(total / (count * float(256 * GROUP)))
    return group_sums(rows)


def tiles_of(rows):
    return rows.reshape(2, 16, rows.shape[-1])


def pair(rows, top):
    return jnp.concatenate([rows[2 * top + side].reshape(1, 1, -1) for side in range(2)], 0)


def over_canvas(step, count, width=C, unroll=2):
    found = [[] for _ in range(count)]
    for top in range(2):
        zero = tuple(jnp.zeros((2, 16, width), F32) for _ in range(count))

        def body(index, carry, top=top):
            return tuple(a + b for a, b in zip(carry, step(top, top * 16 + index)))

        totals = lax.fori_loop(0, 16, body, zero, unroll=unroll)
        for n in range(count):
            columns = jnp.sum(totals[n], axis=1)
            found[n] += [columns[0:1], columns[1:2]]
    return found


def for_rows(step, unroll=2):
    for top in range(2):

        def body(index, carry, top=top):
            step(top, top * 16 + index)
            return carry

        lax.fori_loop(0, 16, body, 0, unroll=unroll)


def norm_stats(load, eq_ref, width):
    (sums,) = over_canvas(lambda top, row: (tiles_of(load(row)),), 1, width)
    means = image_means(sums, eq_ref)
    centers = [pair(means, top) for top in range(2)]

    def square(top, row):
        off = tiles_of(load(row)) - centers[top]
        return (off * off,)

    (squares,) = over_canvas(square, 1, width)
    rstds = [lax.rsqrt(v + EPSILON) for v in image_means(squares, eq_ref)]
    return means, rstds


def swish(value):
    half = 0.5 * value
    return half + half * jnp.tanh(half)


def norm_forward(load, out_refs, stat_ref, eq_ref, gain, shift, act):
    width = gain.shape[-1]
    means, rstds = norm_stats(load, eq_ref, width)
    stat_ref[...] = jnp.concatenate(means + rstds, 0)
    centers = [pair(means, top) for top in range(2)]
    slopes = [pair([r * gain for r in rstds], top) for top in range(2)]
    offset = shift.reshape(1, 1, width)

    def step(top, row):
        value = (tiles_of(load(row)) - centers[top]) * slopes[top] + offset
        value = act(value).reshape(SIDE, width).astype(BF)
        held = width // len(out_refs)
        for index, ref in enumerate(out_refs):
            ref[at_row(row), :] = value[:, index * held : (index + 1) * held]

    for_rows(step)


def norm_backward(load, load_grad, keep_ref, stat_ref, eq_ref, gain, shift, with_swish, finish):
    stats = stat_ref[...]
    means = [stats[i : i + 1] for i in range(4)]
    rstds = [stats[4 + i : 5 + i] for i in range(4)]
    centers = [pair(means, top) for top in range(2)]
    rates = [pair(rstds, top) for top in range(2)]
    scale, offset = gain.reshape(1, 1, C), shift.reshape(1, 1, C)

    def first(top, row):
        unit = (tiles_of(load(row)) - centers[top]) * rates[top]
        grad = tiles_of(load_grad(row))
        if with_swish:
            value = unit * scale + offset
            gate = 0.5 + 0.5 * jnp.tanh(0.5 * value)
            grad = grad * (gate * (1.0 + value * (1.0 - gate)))
            keep_ref[at_row(row), :] = grad.reshape(SIDE, C)
        return grad, grad * unit

    plain, scaled = over_canvas(first, 2)
    mean_plain = image_means([p * gain for p in plain], eq_ref)
    mean_scaled = image_means([s * gain for s in scaled], eq_ref)
    first_means = [pair(mean_plain, top) for top in range(2)]
    second_means = [pair(mean_scaled, top) for top in range(2)]

    def second(top, row):
        unit = (tiles_of(load(row)) - centers[top]) * rates[top]
        grad = tiles_of(keep_ref[at_row(row), :] if with_swish else load_grad(row))
        change = rates[top] * (grad * scale - first_means[top] - unit * second_means[top])
        finish(row, change.reshape(SIDE, C))

    for_rows(second)
    return sum(scaled), sum(plain)


BAND = PIX // 2 + 2 * SIDE


def row_mask(eq_ref, target, source, right):
    column = lax.broadcasted_iota(jnp.int32, (SIDE, 128), 0)

    def eq(side, other):
        return eq_ref[(2 * target + side) * 4 + 2 * source + other]

    if right == 0:
        mask = jnp.where(column < 16, eq(0, 0), eq(1, 1))
    elif right < 0:
        mask = jnp.where(column < 16, eq(0, 0), jnp.where(column == 16, eq(1, 0), eq(1, 1)))
        mask = jnp.where(column == 0, 0.0, mask)
    else:
        mask = jnp.where(column < 15, eq(0, 0), jnp.where(column == 15, eq(0, 1), eq(1, 1)))
        mask = jnp.where(column == SIDE - 1, 0.0, mask)
    return mask.astype(BF)


def fill_bands(band_ref, load, eq_ref, columns=None):
    width = band_ref.shape[2] // 3

    def put(half, place, value, masks):
        moved = [pltpu.roll(value, 1, 0), value, pltpu.roll(value, SIDE - 1, 0)]
        for index in range(3):
            part = moved[index].astype(BF)
            if masks[index] is not None:
                part = part * jnp.concatenate([masks[index]] * (width // 128), 1)
            if columns is None:
                band_ref[half, at_row(place), index * width : (index + 1) * width] = part
            else:
                for number in range(width // HALF):
                    where = pl.ds(columns(index, number), HALF)
                    band_ref[half, at_row(place), where] = part[
                        :, number * HALF : (number + 1) * HALF]

    for half in range(2):
        inner = [row_mask(eq_ref, half, half, -1), None, row_mask(eq_ref, half, half, 1)]

        def body(index, carry, half=half, inner=inner):
            put(half, index + 1, load(half * 16 + index).astype(F32), inner)
            return carry

        lax.fori_loop(0, 16, body, 0, unroll=2)
        across = [row_mask(eq_ref, half, 1 - half, right) for right in (-1, 0, 1)]
        put(half, 17 - 17 * half, load(16 - half).astype(F32), across)
        band_ref[half, 17 * half * SIDE : (17 * half + 1) * SIDE, :] = jnp.zeros(
            (SIDE, 3 * width), BF)


def half_rows(half):
    return pl.ds(pl.multiple_of(half * (PIX // 2), PIX // 2), PIX // 2)


def tap_band(band_ref, half, down):
    return band_ref[half, down * SIDE : down * SIDE + PIX // 2, :]


def parts_apart(index, number):
    return number * 3 * HALF + index * HALF


def swapped(core, number):
    return pl.multiple_of((core ^ number) * HALF, HALF)


def start_all(copies):
    for copy in copies:
        copy.start()
    return copies


def wait_all(copies):
    for copy in copies:
        copy.wait()


def half_copies(core, source, target, sems):
    return [start_all([
        pltpu.make_async_copy(source.at[pl.ds(3 * group, 3), pl.ds(swapped(core, part), HALF), :],
                              target.at[group, part], sems.at[group, part])
        for part in range(2)]) for group in range(3)]


def half_conv(band, weight, copies, bias, total):
    for down in range(3):
        wait_all(copies[down])

        def body(half, carry, down=down):
            at = half_rows(half)
            value = dot(tap_band(band, half, down), weight[down].reshape(6 * HALF, HALF))
            total[at, :] = value + (total[at, :] if down > 0 else bias)
            return carry

        lax.fori_loop(0, 2, body, 0)


def tap_copies(core, own_ref, peer_ref, all_ref, sems, group):
    lead = (pl.ds(3 * group, 3),)
    return weight_copies(core, own_ref, peer_ref, all_ref, sems.at[group], lead)


def weight_copies(core, own_ref, peer_ref, all_ref, sems, lead):
    copies = []
    for local in range(2):
        source = pl.ds(pl.multiple_of((core ^ local) * HALF, HALF), HALF)
        target = pl.ds(local * HALF, HALF)
        for which, ref in enumerate((own_ref, peer_ref)):
            held = pl.ds(which * HALF, HALF)
            if own_ref.shape[-1] == HALF:
                src, dst = (source, slice(None)), (target, held)
            else:
                src, dst = (slice(None), source), (held, target)
            copies.append(
                pltpu.make_async_copy(
                    ref.at[lead + src], all_ref.at[lead + dst], sems.at[2 * local + which]
                )
            )
    return copies


def params(limit):
    return pltpu.CompilerParams(vmem_limit_bytes=limit * MB)


def cost(micros):
    return pl.CostEstimate(flops=int(micros * 1.1e9), bytes_accessed=1 << 20, transcendentals=0)


def shape(rows, columns, dtype):
    return jax.ShapeDtypeStruct((rows, columns), dtype)


def in_hbm(*arrays):
    return [pltpu.with_memory_space_constraint(array, pltpu.HBM) for array in arrays]


def fetch(source, target, sem):
    copy = pltpu.make_async_copy(source, target, sem)
    copy.start()
    return copy


def both_rows(own_ref, peer_ref, row):
    return jnp.concatenate([own_ref[at_row(row), :], peer_ref[at_row(row), :]], 1).astype(F32)


def front_kernel(core_ref, eq_ref, x_hbm, xp_hbm, w_hbm, vec_ref, peer_ref, act_own_hbm, act_peer_hbm, stat_own, stat_peer, band,
                 conv_hbm, next_ref, stat2_ref, x_own, x_peer, act_own, act_peer, weight, total, sems):
    core = core_ref[0]
    first = fetch(x_hbm.at[core], x_own, sems.at[3, 0])
    second = fetch(xp_hbm.at[core], x_peer, sems.at[3, 1])
    copies = half_copies(core, w_hbm, weight, sems)
    first.wait()
    norm_forward(lambda row: x_own[at_row(row), :].astype(F32), (act_own,), stat_own, eq_ref,
                 vec_ref[0:1, :], vec_ref[1:2, :], swish)
    second.wait()
    norm_forward(lambda row: x_peer[at_row(row), :].astype(F32), (act_peer,), stat_peer, eq_ref,
                 peer_ref[0:1, :], peer_ref[1:2, :], swish)
    stores = [fetch(act_own, act_own_hbm, sems.at[4, 0]), fetch(act_peer, act_peer_hbm, sems.at[4, 1])]
    fill_bands(band, lambda row: both_rows(act_own, act_peer, row), eq_ref, parts_apart)
    half_conv(band, weight, copies, vec_ref[2:3, :], total)
    stores.append(fetch(total, conv_hbm, sems.at[3, 0]))
    norm_forward(lambda row: total[at_row(row), :], (next_ref,), stat2_ref, eq_ref, vec_ref[3:4, :],
                 vec_ref[4:5, :], swish)
    wait_all(stores)


def front_peer_kernel(core_ref, eq_ref, band, w_hbm, vec_ref, conv_hbm, next_ref, stat2_ref, weight,
                      total, sems):
    copies = half_copies(core_ref[0], w_hbm, weight, sems)
    half_conv(band, weight, copies, vec_ref[2:3, :], total)
    store = fetch(total, conv_hbm, sems.at[3, 0])
    norm_forward(lambda row: total[at_row(row), :], (next_ref,), stat2_ref, eq_ref, vec_ref[3:4, :],
                 vec_ref[4:5, :], swish)
    store.wait()


def front_call(core, eq, pixels, pixels_peer, weight, own_vectors, peer_vectors):
    half = pltpu.HBM((PIX, HALF), BF)
    return pl.pallas_call(
        front_kernel,
        out_shape=(half, half, shape(8, HALF, F32), shape(8, HALF, F32),
                   pltpu.VMEM((2, BAND, 3 * C), BF), pltpu.HBM((PIX, HALF), F32),
                   shape(PIX, HALF, BF), shape(8, HALF, F32)),
        in_specs=[SM, SM, HBM, HBM, HBM, VM, VM],
        out_specs=(HBM, HBM, VM, VM, VM, HBM, VM, VM),
        scratch_shapes=[pltpu.VMEM((PIX, HALF), BF)] * 4
        + [pltpu.VMEM((3, 2, 3, HALF, HALF), BF), pltpu.VMEM((PIX, HALF), F32),
           pltpu.SemaphoreType.DMA((5, 2))],
        name="front", compiler_params=params(14), cost_estimate=cost(9),
    )(core, eq, *in_hbm(pixels, pixels_peer, weight), own_vectors, peer_vectors)


def front_peer_call(core, eq, band, weight, vec):
    return pl.pallas_call(
        front_peer_kernel,
        out_shape=(pltpu.HBM((PIX, HALF), F32), shape(PIX, HALF, BF), shape(8, HALF, F32)),
        in_specs=[SM, SM, VM, HBM, VM], out_specs=(HBM, VM, VM),
        scratch_shapes=[pltpu.VMEM((3, 2, 3, HALF, HALF), BF), pltpu.VMEM((PIX, HALF), F32),
                        pltpu.SemaphoreType.DMA((4, 2))],
        name="front_peer", compiler_params=params(14), cost_estimate=cost(5),
    )(core, eq, band, *in_hbm(weight), vec)


def attn_kernel(core_ref, eq_ref, act_own, act_peer, own_ref, peer_ref, x_ref, xp_ref, g_own, g_peer,
                wq_o, wq_p, wk_o, wk_p, wv_o, wv_p, wp_o, wp_p, vec_ref, out_own, out_peer, gmid_hbm,
                gconv_ref, small_ref, dquery, dkey, dvalue, mixed, normed_ref, weight, gfull, query,
                keys, values, gmixed, probs, gscores, gnormed, mid_ref, taps, band, x_own, x_peer,
                stat_ref, sems):
    core = core_ref[0]
    groups = [tap_copies(core, own_ref, peer_ref, taps, sems.at[5:8], down) for down in range(3)]
    start_all(groups[0])
    extra = [fetch(x_ref.at[core], x_own, sems.at[4, 2]), fetch(xp_ref.at[core], x_peer, sems.at[4, 3])]
    fill_bands(band, lambda row: both_rows(act_own, act_peer, row), eq_ref)
    start_all(groups[1])
    start_all(groups[2])
    wait_all(extra)
    for down in range(3):
        wait_all(groups[down])
        if down == 0:
            copies = []
            for index, (own, peer) in enumerate(
                    ((wq_o, wq_p), (wk_o, wk_p), (wv_o, wv_p), (wp_o, wp_p))):
                copies += start_all(
                    weight_copies(core, own, peer, weight.at[index], sems.at[index], ()))
            copies.append(fetch(g_own.at[core], gfull.at[:, 0:HALF], sems.at[4, 0]))
            copies.append(fetch(g_peer.at[core], gfull.at[:, HALF:C], sems.at[4, 1]))

        def conv(half, carry, down=down):
            at = half_rows(half)
            value = dot(tap_band(band, half, down),
                        taps[3 * down : 3 * down + 3].reshape(3 * C, C))
            if down > 0:
                value = value + mid_ref[at, :]
            else:
                value = value + vec_ref[5:6, :] + jnp.concatenate(
                    [x_own[at, :], x_peer[at, :]], 1).astype(F32)
            mid_ref[at, :] = value
            return carry

        lax.fori_loop(0, 2, conv, 0)
    norm_forward(lambda row: mid_ref[at_row(row), :], (normed_ref,), stat_ref, eq_ref,
                 vec_ref[6:7, :], vec_ref[7:8, :], lambda v: v)
    wait_all(copies)
    normed = normed_ref[...]
    query[...] = (dot(normed, weight[0]) + vec_ref[8:9, :]).astype(BF)
    keys[...] = dot(normed, weight[1]).astype(BF)
    values[...] = (dot(normed, weight[2]) + vec_ref[9:10, :]).astype(BF)
    gmixed[...] = dot_nt(gfull[...], weight[3]).astype(BF)

    rows = 256
    spot = lax.broadcasted_iota(jnp.int32, (1, PIX), 1)
    right = (spot & (SIDE - 1)) >= 16
    low = spot >= PIX // 2

    def block(index, carry):
        start = pl.multiple_of(index * rows, rows)
        at = pl.ds(start, rows)
        half = (start >= PIX // 2).astype(jnp.int32) * 2
        bias = []
        for side in range(2):
            base = (half + side) * 4
            row = jnp.where(low, jnp.where(right, eq_ref[base + 3], eq_ref[base + 2]),
                            jnp.where(right, eq_ref[base + 1], eq_ref[base]))
            bias.append(jnp.where(row > 0.5, 0.0, -1e30).reshape(1, 1, 1, PIX))
        bias = jnp.concatenate(bias, 1)
        scores = dot_nt(query[at, :], keys[...]) * (SCALE * LOG2E)
        scores = (scores.reshape(rows // SIDE, 2, 16, PIX) + bias).reshape(rows, PIX)
        expo = jnp.exp2(scores - jnp.max(scores, axis=1, keepdims=True))
        wide = expo * (1.0 / jnp.sum(expo, axis=1, keepdims=True))
        narrow = wide.astype(BF)
        probs[at, :] = narrow
        mixed[at, :] = dot(narrow, values[...]).astype(BF)
        gprobs = dot_nt(gmixed[at, :], values[...])
        delta = jnp.sum(wide * gprobs, axis=1, keepdims=True)
        grads = (wide * (gprobs - delta)).astype(BF)
        gscores[at, :] = grads
        dquery[at, :] = (dot(grads, keys[...]) * SCALE).astype(BF)
        return carry

    lax.fori_loop(0, PIX // rows, block, 0)

    def total(value):
        return jnp.sum(value.astype(F32), axis=0, keepdims=True)

    dkey[...] = (dot_tn(gscores[...], query[...]) * SCALE).astype(BF)
    dvalue[...] = dot_tn(probs[...], gmixed[...]).astype(BF)
    gnormed[...] = (dot_nt(dquery[...], weight[0]) + dot_nt(dkey[...], weight[1])
                    + dot_nt(dvalue[...], weight[2]))
    dbq, dbv, dbp = total(dquery[...]), total(dvalue[...]), total(gfull[...])

    out = mid_ref[...] + dot(mixed[...], weight[3]) + vec_ref[10:11, :]
    out_own[...] = out[:, :HALF]
    out_peer[...] = out[:, HALF:]

    def finish(row, change):
        grad = gfull[at_row(row), :].astype(F32) + change
        gnormed[at_row(row), :] = grad
        gconv_ref[at_row(row), :] = grad.astype(BF)

    dgain, dshift = norm_backward(
        lambda row: mid_ref[at_row(row), :], lambda row: gnormed[at_row(row), :], None, stat_ref,
        eq_ref, vec_ref[6:7, :], vec_ref[7:8, :], False, finish)
    store = fetch(gnormed, gmid_hbm, sems.at[4, 3])
    small_ref[...] = jnp.concatenate(
        [dgain, dshift, dbq, dbv, dbp, total(gconv_ref[...]), dbq, dbq], 0)
    store.wait()


def attn_call(core, eq, acts, own, peer, x, g, weights, vec):
    flat = [w for pair_of in weights for w in pair_of]
    return pl.pallas_call(
        attn_kernel,
        out_shape=(shape(PIX, HALF, F32), shape(PIX, HALF, F32), pltpu.HBM((PIX, C), F32),
                   shape(PIX, C, BF), shape(8, C, F32)) + (pltpu.VMEM((PIX, C), BF),) * 5,
        in_specs=[SM, SM, VM, VM] + [HBM] * 14 + [VM],
        out_specs=(VM, VM, HBM) + (VM,) * 7,
        scratch_shapes=[pltpu.VMEM((4, C, C), BF)] + [pltpu.VMEM((PIX, C), BF)] * 5
        + [pltpu.VMEM((PIX, PIX), BF)] * 2 + [pltpu.VMEM((PIX, C), F32)] * 2
        + [pltpu.VMEM((9, C, C), BF), pltpu.VMEM((2, BAND, 3 * C), BF)]
        + [pltpu.VMEM((PIX, HALF), BF)] * 2
        + [pltpu.VMEM((8, C), F32), pltpu.SemaphoreType.DMA((8, 4))],
        name="attention", compiler_params=params(34), cost_estimate=cost(28),
    )(core, eq, *acts, *in_hbm(own, peer, *x, *g, *flat), vec)


def attn_wgrad_kernel(core_ref, normed_ref, dquery, dkey, dvalue, mixed, g_own, g_peer, dw_own,
                      dw_peer, g_mine, g_back, sems):
    core = core_ref[0]
    copies = [fetch(g_own.at[core], g_mine, sems.at[0]), fetch(g_peer.at[core], g_back, sems.at[1])]
    normed = normed_ref[...]
    for index, ref in enumerate((dquery, dkey, dvalue)):
        full = dot_tn(normed, ref[...]).astype(BF)
        for local in range(2):
            target = pl.multiple_of(index * C + (core ^ local) * HALF, HALF)
            part = full[local * HALF : (local + 1) * HALF, :]
            dw_own[pl.ds(target, HALF), :] = part[:, :HALF]
            dw_peer[pl.ds(target, HALF), :] = part[:, HALF:]
    for copy in copies:
        copy.wait()
    for local, ref in enumerate((g_mine, g_back)):
        target = pl.multiple_of(3 * C + (core ^ local) * HALF, HALF)
        part = dot_tn(mixed[...], ref[...]).astype(BF)
        dw_own[pl.ds(target, HALF), :] = part[:HALF]
        dw_peer[pl.ds(target, HALF), :] = part[HALF:]


def attn_wgrad_call(core, normed, dquery, dkey, dvalue, mixed, g):
    return pl.pallas_call(
        attn_wgrad_kernel, out_shape=(shape(4 * C, HALF, BF),) * 2,
        in_specs=[SM] + [VM] * 5 + [HBM] * 2, out_specs=(VM, VM),
        scratch_shapes=[pltpu.VMEM((PIX, HALF), BF)] * 2 + [pltpu.SemaphoreType.DMA((2,))],
        name="attention_weights", compiler_params=params(6), cost_estimate=cost(3),
    )(core, normed, dquery, dkey, dvalue, mixed, *in_hbm(*g))


def fetch_all(sources, targets, sems):
    return [fetch(source, target, sems.at[index])
            for index, (source, target) in enumerate(zip(sources, targets))]


def wgrad2_kernel(core_ref, eq_ref, *refs):
    sources, (out_ref, act_mine, act_other, grad_mine, grad_other, band, band_other, sems) = (
        refs[:4], refs[4:])
    core = core_ref[0]
    copies = fetch_all(sources, (act_mine, act_other, grad_mine, grad_other), sems)
    copies[0].wait()
    fill_bands(band, lambda row: act_mine[at_row(row), :], eq_ref.at[0])
    copies[1].wait()
    fill_bands(band_other, lambda row: act_other[at_row(row), :], eq_ref.at[1])
    for copy in copies[2:]:
        copy.wait()
    for down in range(3):
        for local in range(2):
            full = 0.0
            for half in range(2):
                rows = slice(half * (PIX // 2), (half + 1) * (PIX // 2))
                full = full + dot_tn(tap_band(band, half, down),
                                     grad_mine[rows, local * HALF : (local + 1) * HALF])
                full = full + dot_tn(tap_band(band_other, half, down),
                                     grad_other[rows, (1 - local) * HALF : (2 - local) * HALF])
            full = full.astype(BF)
            for index in range(3):
                base = (3 * down + index) * C + (core ^ local) * HALF
                out_ref[pl.ds(pl.multiple_of(base, HALF), HALF), :] = full[
                    index * HALF : (index + 1) * HALF]


def wgrad2_call(core, eqs, *arrays):
    return pl.pallas_call(
        wgrad2_kernel, out_shape=shape(9 * C, HALF, BF), in_specs=[SM, SM] + [HBM] * 4,
        out_specs=VM,
        scratch_shapes=[pltpu.VMEM((PIX, HALF), BF)] * 2 + [pltpu.VMEM((PIX, C), BF)] * 2
        + [pltpu.VMEM((2, BAND, 3 * HALF), BF)] * 2 + [pltpu.SemaphoreType.DMA((4,))],
        name="wgrad2", compiler_params=params(14), cost_estimate=cost(7),
    )(core, eqs, *in_hbm(*arrays))


TAPS = 6


def wgrad1_kernel(core_ref, eq_ref, *refs):
    sources, (out_ref, tail_ref, band, band_other, act, act2, grad_mine, grad_other, sems) = (
        refs[:6], refs[6:])
    core = core_ref[0]
    copies = fetch_all(sources, (grad_mine, grad_other, act.at[:, 0:HALF], act.at[:, HALF:C],
                                 act2.at[:, 0:HALF], act2.at[:, HALF:C]), sems)
    copies[0].wait()
    fill_bands(band, lambda row: grad_mine[at_row(row), :], eq_ref.at[0])
    copies[1].wait()
    fill_bands(band_other, lambda row: grad_other[at_row(row), :], eq_ref.at[1])
    for copy in copies[2:]:
        copy.wait()
    for down in range(3):
        full = 0.0
        for half in range(2):
            rows = slice(half * (PIX // 2), (half + 1) * (PIX // 2))
            full = full + dot_tn(act[rows, :], tap_band(band, half, down))
            full = full + dot_tn(act2[rows, :], tap_band(band_other, half, down))
        full = full.astype(BF)
        for index in range(3):
            tap = 8 - (3 * down + index)
            out, base = (out_ref, tap * C) if tap < TAPS else (tail_ref, (tap - TAPS) * C)
            for local in range(2):
                where = pl.ds(pl.multiple_of(base + (core ^ local) * HALF, HALF), HALF)
                out[where, :] = full[local * HALF : (local + 1) * HALF,
                                     index * HALF : (index + 1) * HALF]


def wgrad1_call(core, eqs, *arrays):
    return pl.pallas_call(
        wgrad1_kernel, out_shape=(shape(TAPS * C, HALF, BF), shape((9 - TAPS) * C, HALF, BF)),
        in_specs=[SM, SM] + [HBM] * 6, out_specs=(VM, VM),
        scratch_shapes=[pltpu.VMEM((2, BAND, 3 * HALF), BF)] * 2 + [pltpu.VMEM((PIX, C), BF)] * 2
        + [pltpu.VMEM((PIX, HALF), BF)] * 2 + [pltpu.SemaphoreType.DMA((6,))],
        name="wgrad1", compiler_params=params(16), cost_estimate=cost(7),
    )(core, eqs, *in_hbm(*arrays))


def dgrad_kernel(first, core_ref, eq_ref, own_ref, peer_ref, vec_ref, *refs):
    if first:
        (grad_own, grad_peer, stat_own, stat_peer, x_hbm, xp_hbm, gmid_hbm, out_own, out_peer, small_ref, weight, patch,
         total, stat_ref, sems, x_own, x_peer, gmid_ref) = refs
        load = lambda row: both_rows(x_own, x_peer, row)
        load_grad = lambda row: both_rows(grad_own, grad_peer, row)
        sources = (x_hbm.at[core_ref[0]], xp_hbm.at[core_ref[0]], gmid_hbm)
        held = (x_own, x_peer, gmid_ref)
        gain, shift = vec_ref[0:1, :], vec_ref[1:2, :]
    else:
        (grad_ref, stat_own, stat_peer, in_own, in_peer, out_own, out_peer, small_ref, weight, patch,
         total, stat_ref, sems, mine, back) = refs
        load = lambda row: both_rows(mine, back, row)
        load_grad = lambda row: grad_ref[at_row(row), :]
        sources, held = (in_own, in_peer), (mine, back)
        gain, shift = vec_ref[3:4, :], vec_ref[4:5, :]
    stat_ref[:, :HALF] = stat_own[...]
    stat_ref[:, HALF:] = stat_peer[...]
    copies = [tap_copies(core_ref[0], own_ref, peer_ref, weight, sems, 2 - down)
              for down in range(3)]
    for group in copies:
        for copy in group:
            copy.start()
    later = fetch_all(sources, held, sems.at[3])
    fill_bands(patch, load_grad, eq_ref)
    for down in range(3):
        for copy in copies[down]:
            copy.wait()

        def body(half, carry, down=down):
            value = total[half_rows(half), :] if down > 0 else 0.0
            for t in range(3):
                value = value + dot_nt(tap_band(patch, half, down)[:, t * C : (t + 1) * C],
                                       weight[8 - (3 * down + t)])
            total[half_rows(half), :] = value
            return carry

        lax.fori_loop(0, 2, body, 0)
    for copy in later:
        copy.wait()

    def finish(row, change):
        at = at_row(row)
        if first:
            change = change + gmid_ref[at, :]
        out_own[at, :] = change[:, :HALF].astype(out_own.dtype)
        out_peer[at, :] = change[:, HALF:].astype(out_peer.dtype)

    dgain, dshift = norm_backward(load, lambda row: total[at_row(row), :], total, stat_ref, eq_ref,
                                  gain, shift, True, finish)
    bias = [jnp.sum(ref[...].astype(F32), axis=0, keepdims=True) for ref in (out_own, out_peer)]
    bias = jnp.concatenate(bias, 1)
    small_ref[...] = jnp.concatenate([dgain, dshift, bias] + [dgain] * 5, 0)


def dgrad_call(core, eq, grad, own, peer, vec, stats, source, gmid=None):
    first = gmid is not None
    extra = (*source, gmid) if first else source
    held = [pltpu.VMEM((PIX, HALF), BF if first else F32)] * 2
    held += [pltpu.VMEM((PIX, C), F32)] if first else []
    outs = (shape(PIX, HALF, F32 if first else BF),) * 2
    return pl.pallas_call(
        functools.partial(dgrad_kernel, first),
        out_shape=outs + (shape(8, C, F32),),
        in_specs=[SM, SM, HBM, HBM, VM] + [VM] * (len(grad) + len(stats)) + [HBM] * len(extra),
        out_specs=(VM,) * 3,
        scratch_shapes=[pltpu.VMEM((9, C, C), BF), pltpu.VMEM((2, BAND, 3 * C), BF),
                        pltpu.VMEM((PIX, C), F32), pltpu.VMEM((8, C), F32),
                        pltpu.SemaphoreType.DMA((4, 4))] + held,
        name="dgrad1" if first else "dgrad2", compiler_params=params(16), cost_estimate=cost(10),
    )(core, eq, *in_hbm(own, peer), vec, *grad, *stats, *in_hbm(*extra))


ORDERS = {
    "second": ((2, 0, 1), (0, 1, 2)),
    "attn": ((1, 2, 0), (1, 2, 0)),
    "first": ((2, 0, 1), (0, 1, 2)),
    "rest": ((1, 2, 0), (1, 2, 0)),
}


def orders_of(kind, size):
    bits = size.bit_length() - 1
    return [[*order, *range(3, bits)] for order in ORDERS[kind]]


def exchange(array, orders, stage, size):
    moves = [((d, c), (d ^ (1 << orders[c][stage]), c)) for d in range(size) for c in range(2)]
    return lax.ppermute(array, ("dp", "chan"), [(a[0] * 2 + a[1], b[0] * 2 + b[1]) for a, b in moves])


def side_of(orders, stage):
    bit = jnp.where(lax.axis_index("chan") == 0, orders[0][stage], orders[1][stage])
    return (lax.axis_index("dp") >> bit) & 1


def side_base(orders):
    base = 0
    for stage in range(len(orders[0])):
        base = base * 2 + side_of(orders, stage)
    return base


class Chain:
    def __init__(self, part, kind, size):
        self.value, self.size, self.orders, self.step = part, size, orders_of(kind, size), 0
        self.stages = len(self.orders[0])

    def advance(self):
        stage = self.step if self.step < self.stages else 2 * self.stages - 1 - self.step
        if self.step < self.stages:
            half = self.value.shape[0] // 2
            side = side_of(self.orders, stage)
            send = lax.dynamic_slice_in_dim(self.value, (1 - side) * half, half, 0)
            keep = lax.dynamic_slice_in_dim(self.value, side * half, half, 0)
            self.value = keep + exchange(send, self.orders, stage, self.size)
        else:
            back = exchange(self.value, self.orders, stage, self.size)
            self.value = jnp.concatenate([self.value, back], 0) if stage > 0 else (self.value, back)
        self.step += 1


def together(chains, *values):
    held = lax.optimization_barrier(([c.value for c in chains], values))
    for chain, value in zip(chains, held[0]):
        chain.value = value
    return held[1]


def after(value, *others):
    return lax.optimization_barrier((value, *others))[0]


def first_target(row, start=0):
    return 0, row + start, slice(0, HALF)


def second_target(row):
    return 0, row // C * HALF + row % HALF, slice(row // HALF % 2 * HALF, (row // HALF % 2 + 1) * HALF)


def attn_target(row):
    if row < 3 * C:
        return row // C, row % C, slice(0, HALF)
    row -= 3 * C
    return 3, row % HALF, slice(row // HALF * HALF, (row // HALF + 1) * HALF)


def place_kernel(size, targets, base_ref, *refs):
    ins, outs, held = refs[: 2 * len(targets)], refs[2 * len(targets) : -1], refs[-1]
    start = 0
    for index, target in enumerate(targets):
        part, part2 = ins[2 * index : 2 * index + 2]
        half = part.shape[0]
        held[start : start + half, :] = part[...]
        held[start + half : start + 2 * half, :] = part2[...]
        rows = 2 * half // size
        piece = math.gcd(rows, HALF)
        for row in range(0, 2 * half, piece):
            source = ((row // rows) ^ base_ref[index]) * rows + row % rows + start
            which, at, columns = target(row)
            outs[which][at : at + piece, columns] = held[
                pl.ds(pl.multiple_of(source, piece), piece), :].astype(F32)
        start += 2 * half


def place(chains, targets, shapes, token):
    parts = [part for chain in chains for part in chain.value]
    rows = sum(part.shape[0] for part in parts)
    base = jnp.stack([side_base(chain.orders) for chain in chains]).astype(jnp.int32)
    return pl.pallas_call(
        functools.partial(place_kernel, chains[0].size, targets),
        out_shape=tuple(shape(*one, F32) for one in shapes), in_specs=[SM] + [VM] * len(parts),
        out_specs=(VM,) * len(shapes), scratch_shapes=[pltpu.VMEM((rows, HALF), BF)],
        compiler_params=params(12), name="place", cost_estimate=cost(2),
    )(after(base, token), *parts)


def swap(array):
    return lax.ppermute(array, "chan", [(0, 1), (1, 0)])


def shards(pixels, tile_ids, first_gain, first_shift, first_conv, first_bias, second_gain,
           second_shift, second_conv, second_bias, attn_gain, attn_shift, query_weight,
           query_bias, key_weight, value_weight, value_bias, proj_weight, proj_bias, cotangent,
           *, size):
    index = lax.axis_index("chan")
    core = index.reshape(1).astype(jnp.int32)
    tiles = tile_ids.reshape(2, 2, 16, 2, 16)[:, :, 0, :, 0].reshape(2, 4)
    eqs = (tiles[:, :, None] == tiles[:, None, :]).astype(F32).reshape(2, 16)
    eqs = jnp.where(index == 0, eqs, eqs[::-1])
    own_vectors = jnp.stack([first_gain, first_shift, first_bias, second_gain, second_shift,
                             second_bias, attn_gain, attn_shift, query_bias, value_bias, proj_bias])
    pixels_peer = swap(pixels)
    pixels_peer, own_vectors, eqs = lax.optimization_barrier((pixels_peer, own_vectors, eqs))
    eq = eqs[0]
    peer_vectors = swap(own_vectors)
    first_conv, peer_vectors, pixels_peer = lax.optimization_barrier(
        (first_conv, peer_vectors, pixels_peer))
    first_peer = swap(first_conv)
    weights = lax.optimization_barrier(
        (query_weight, key_weight, value_weight, proj_weight, peer_vectors))[:4]
    weights_peer = [swap(array) for array in weights]
    vectors = jnp.concatenate([own_vectors, peer_vectors], 1)
    x = (pixels, pixels_peer)
    act_own, act_peer, stat_own, stat_peer, band, conv1_own, act2_own, stat2_own = front_call(
        core, eq, *x, first_conv, own_vectors, peer_vectors)
    first_peer, act2_own, act_own, act_peer, second_conv, cotangent, *weights_peer = (
        lax.optimization_barrier((first_peer, act2_own, act_own, act_peer, second_conv, cotangent,
                                  *weights_peer)))
    second_peer, g_peer = swap(second_conv), swap(cotangent)
    act_other = (swap(act_peer), swap(act_own))
    conv1_peer, act2_peer, stat2_peer = front_peer_call(core, eq, band, first_peer, peer_vectors)
    act2_peer, second_peer, g_peer = lax.optimization_barrier((act2_peer, second_peer, g_peer))
    g = (cotangent, g_peer)
    act2_other = swap(act2_peer)
    out_own, out_peer, gmid, gconv2, small3, *parts, normed = attn_call(
        core, eq, (act2_own, act2_peer), second_conv, second_peer, x, g,
        list(zip(weights, weights_peer)), vectors)
    gconv2, act2_other, *act_other = lax.optimization_barrier((gconv2, act2_other, *act_other))
    gconv2_other = swap(gconv2)
    dattn, dattn_peer = attn_wgrad_call(core, normed, *parts, g)
    dattn, gconv2, gconv2_other = lax.optimization_barrier((dattn, gconv2, gconv2_other))
    attn_other = swap(dattn_peer)
    part = wgrad2_call(core, eqs, act2_own, act2_other, gconv2, gconv2_other)
    attn_other, part = lax.optimization_barrier((attn_other, part))
    second, attn_sum = Chain(part, "second", size), Chain(dattn + attn_other, "attn", size)
    (gconv2,) = together([second, attn_sum], gconv2)

    attn_sum.advance()
    second.advance()
    gconv1_own, gconv1_peer, small2 = dgrad_call(
        core, eq, (gconv2,), second_conv, second_peer, vectors, (stat2_own, stat2_peer),
        (conv1_own, conv1_peer))
    gconv1_other = swap(gconv1_peer)
    gconv1_own, gconv1_other = together([second, attn_sum], gconv1_own, gconv1_other)

    attn_sum.advance()
    second.advance()
    part, tail = wgrad1_call(core, eqs, gconv1_own, gconv1_other, act_own, act_peer, *act_other)
    first, rest = Chain(part, "first", size), Chain(tail, "rest", size)
    (gconv1_own,) = together([second, attn_sum, first, rest], gconv1_own)

    every = [attn_sum, second, rest, first]
    for chain in every:
        chain.advance()
    pix_own, pix_peer, small1 = dgrad_call(core, eq, (gconv1_own, gconv1_peer), first_conv,
                                           first_peer, vectors, (stat_own, stat_peer), x, gmid)
    small = jnp.concatenate([small1, small2, small3], 0)
    pix_peer, out_peer, small = together(every, pix_peer, out_peer, small)

    small = small[:, :HALF] + swap(small[:, HALF:])
    pix_back = swap(pix_peer)
    out_back = swap(out_peer)
    bits = size.bit_length() - 1
    turn = 0
    token = core
    while any(chain.step < 2 * bits for chain in every):
        for chain in every:
            if chain.step < 2 * bits:
                chain.advance()
                (token,) = together([chain], token)
        if turn < bits:
            small = small + lax.ppermute(
                small, "dp", [(i, i ^ (1 << turn)) for i in range(size)])
            small, token = lax.optimization_barrier((small, token))
        turn += 1
    (sums2,) = place([second], [second_target], [(9 * HALF, C)], core)
    sums3 = place([attn_sum], [attn_target], [(C, HALF), (C, HALF), (C, HALF), (HALF, C)], core)
    (sums1,) = place([first, rest], [first_target, functools.partial(first_target, start=TAPS * C)],
                     [(9 * C, HALF)], token)

    def unboth(own, back):
        return jnp.where(index == 0, jnp.stack([own, back]), jnp.stack([back, own]))

    return (
        unboth(out_own, out_back), unboth(pix_own, pix_back), small[0], small[1],
        sums1.reshape(9, C, HALF), small[10], small[8], small[9], sums2.reshape(9, HALF, C),
        small[21], small[16], small[17], sums3[0], small[18], sums3[1], sums3[2], small[19],
        sums3[3], small[20],
    )


def solution(mesh):
    chan = P("chan")
    rows = P("dp", None, "chan")
    return jax.shard_map(
        functools.partial(shards, size=mesh.shape["dp"]),
        mesh=mesh,
        in_specs=(
            rows, P("dp", None), chan, chan, P(None, None, "chan"), chan, chan, chan,
            P(None, "chan", None), chan, chan, chan, P(None, "chan"), chan, P(None, "chan"),
            P(None, "chan"), chan, P("chan", None), chan, rows,
        ),
        out_specs=(
            rows, rows, chan, chan, P(None, None, "chan"), chan, chan, chan,
            P(None, "chan", None), chan, chan, chan, P(None, "chan"), chan, P(None, "chan"),
            P(None, "chan"), chan, P("chan", None), chan,
        ),
        check_vma=False,
    )
```

```python
import functools
import math
import jax
import jax.numpy as jnp
from jax import lax
from jax.experimental import pallas as pl
from jax.experimental.pallas import tpu as pltpu
from jax.sharding import PartitionSpec as P

C = 512
HALF = 256
GROUP = 16
SIDE = 32
PIX = 1024
EPSILON = 1e-06
BF = jnp.bfloat16
F32 = jnp.float32
MB = 1024 * 1024
VM = pl.BlockSpec(memory_space=pltpu.VMEM)
SM = pl.BlockSpec(memory_space=pltpu.SMEM)
HBM = pl.BlockSpec(memory_space=pltpu.HBM)
SCALE = C ** (-0.5)
LOG2E = 1.4426950408889634


def dot(first, second):
    return jnp.dot(first, second, preferred_element_type=F32)


def dot_nt(first, second):
    return lax.dot_general(first, second, (((1,), (1,)), ((), ())), preferred_element_type=F32)


def dot_tn(first, second):
    return lax.dot_general(first, second, (((0,), (0,)), ((), ())), preferred_element_type=F32)


def at_row(row):
    return pl.ds(pl.multiple_of(row * SIDE, SIDE), SIDE)


def group_sums(rows):
    full = jnp.concatenate(rows, 0)
    width = full.shape[1]
    lane = lax.broadcasted_iota(jnp.int32, full.shape, 1)
    for step in (1, 2, 4, 8):
        full = full + jnp.where(
            (lane & step) == 0, pltpu.roll(full, width - step, 1), pltpu.roll(full, step, 1)
        )
    return [full[i : i + 1] for i in range(len(rows))]


def image_means(sums, eq_ref):
    rows = []
    for i in range(4):
        total, count = 0.0, 0.0
        for j in range(4):
            total = total + eq_ref[4 * i + j] * sums[j]
            count = count + eq_ref[4 * i + j]
        rows.append(total / (count * float(256 * GROUP)))
    return group_sums(rows)


def tiles_of(rows):
    return rows.reshape(2, 16, rows.shape[-1])


def pair(rows, top):
    return jnp.concatenate([rows[2 * top + side].reshape(1, 1, -1) for side in range(2)], 0)


def over_canvas(step, count, width=C, unroll=2):
    found = [[] for _ in range(count)]
    for top in range(2):
        zero = tuple(jnp.zeros((2, 16, width), F32) for _ in range(count))

        def body(index, carry, top=top):
            return tuple(a + b for a, b in zip(carry, step(top, top * 16 + index)))

        totals = lax.fori_loop(0, 16, body, zero, unroll=unroll)
        for n in range(count):
            columns = jnp.sum(totals[n], axis=1)
            found[n] += [columns[0:1], columns[1:2]]
    return found


def for_rows(step, unroll=2):
    for top in range(2):

        def body(index, carry, top=top):
            step(top, top * 16 + index)
            return carry

        lax.fori_loop(0, 16, body, 0, unroll=unroll)


def norm_stats(load, eq_ref, width):
    (sums,) = over_canvas(lambda top, row: (tiles_of(load(row)),), 1, width)
    means = image_means(sums, eq_ref)
    centers = [pair(means, top) for top in range(2)]

    def square(top, row):
        off = tiles_of(load(row)) - centers[top]
        return (off * off,)

    (squares,) = over_canvas(square, 1, width)
    rstds = [lax.rsqrt(v + EPSILON) for v in image_means(squares, eq_ref)]
    return means, rstds


def swish(value):
    half = 0.5 * value
    return half + half * jnp.tanh(half)


def norm_forward(load, out_refs, stat_ref, eq_ref, gain, shift, act):
    width = gain.shape[-1]
    means, rstds = norm_stats(load, eq_ref, width)
    stat_ref[...] = jnp.concatenate(means + rstds, 0)
    centers = [pair(means, top) for top in range(2)]
    slopes = [pair([r * gain for r in rstds], top) for top in range(2)]
    offset = shift.reshape(1, 1, width)

    def step(top, row):
        value = (tiles_of(load(row)) - centers[top]) * slopes[top] + offset
        value = act(value).reshape(SIDE, width).astype(BF)
        held = width // len(out_refs)
        for index, ref in enumerate(out_refs):
            ref[at_row(row), :] = value[:, index * held : (index + 1) * held]

    for_rows(step)


def norm_backward(load, load_grad, keep_ref, stat_ref, eq_ref, gain, shift, with_swish, finish):
    stats = stat_ref[...]
    means = [stats[i : i + 1] for i in range(4)]
    rstds = [stats[4 + i : 5 + i] for i in range(4)]
    centers = [pair(means, top) for top in range(2)]
    rates = [pair(rstds, top) for top in range(2)]
    scale, offset = gain.reshape(1, 1, C), shift.reshape(1, 1, C)

    def first(top, row):
        unit = (tiles_of(load(row)) - centers[top]) * rates[top]
        grad = tiles_of(load_grad(row))
        if with_swish:
            value = unit * scale + offset
            gate = 0.5 + 0.5 * jnp.tanh(0.5 * value)
            grad = grad * (gate * (1.0 + value * (1.0 - gate)))
            keep_ref[at_row(row), :] = grad.reshape(SIDE, C)
        return grad, grad * unit

    plain, scaled = over_canvas(first, 2)
    mean_plain = image_means([p * gain for p in plain], eq_ref)
    mean_scaled = image_means([s * gain for s in scaled], eq_ref)
    first_means = [pair(mean_plain, top) for top in range(2)]
    second_means = [pair(mean_scaled, top) for top in range(2)]

    def second(top, row):
        unit = (tiles_of(load(row)) - centers[top]) * rates[top]
        grad = tiles_of(keep_ref[at_row(row), :] if with_swish else load_grad(row))
        change = rates[top] * (grad * scale - first_means[top] - unit * second_means[top])
        finish(row, change.reshape(SIDE, C))

    for_rows(second)
    return sum(scaled), sum(plain)


BAND = PIX // 2 + 2 * SIDE


def row_mask(eq_ref, target, source, right):
    column = lax.broadcasted_iota(jnp.int32, (SIDE, 128), 0)

    def eq(side, other):
        return eq_ref[(2 * target + side) * 4 + 2 * source + other]

    if right == 0:
        mask = jnp.where(column < 16, eq(0, 0), eq(1, 1))
    elif right < 0:
        mask = jnp.where(column < 16, eq(0, 0), jnp.where(column == 16, eq(1, 0), eq(1, 1)))
        mask = jnp.where(column == 0, 0.0, mask)
    else:
        mask = jnp.where(column < 15, eq(0, 0), jnp.where(column == 15, eq(0, 1), eq(1, 1)))
        mask = jnp.where(column == SIDE - 1, 0.0, mask)
    return mask.astype(BF)


def fill_bands(band_ref, load, eq_ref, columns=None):
    width = band_ref.shape[2] // 3

    def put(half, place, value, masks):
        moved = [pltpu.roll(value, 1, 0), value, pltpu.roll(value, SIDE - 1, 0)]
        for index in range(3):
            part = moved[index].astype(BF)
            if masks[index] is not None:
                part = part * jnp.concatenate([masks[index]] * (width // 128), 1)
            if columns is None:
                band_ref[half, at_row(place), index * width : (index + 1) * width] = part
            else:
                for number in range(width // HALF):
                    where = pl.ds(columns(index, number), HALF)
                    band_ref[half, at_row(place), where] = part[
                        :, number * HALF : (number + 1) * HALF]

    for half in range(2):
        inner = [row_mask(eq_ref, half, half, -1), None, row_mask(eq_ref, half, half, 1)]

        def body(index, carry, half=half, inner=inner):
            put(half, index + 1, load(half * 16 + index).astype(F32), inner)
            return carry

        lax.fori_loop(0, 16, body, 0, unroll=2)
        across = [row_mask(eq_ref, half, 1 - half, right) for right in (-1, 0, 1)]
        put(half, 17 - 17 * half, load(16 - half).astype(F32), across)
        band_ref[half, 17 * half * SIDE : (17 * half + 1) * SIDE, :] = jnp.zeros(
            (SIDE, 3 * width), BF)


def half_rows(half):
    return pl.ds(pl.multiple_of(half * (PIX // 2), PIX // 2), PIX // 2)


def tap_band(band_ref, half, down):
    if isinstance(down, int):
        return band_ref[half, down * SIDE : down * SIDE + PIX // 2, :]
    return band_ref[half, pl.ds(pl.multiple_of(down * SIDE, SIDE), PIX // 2), :]


def parts_apart(index, number):
    return number * 3 * HALF + index * HALF


def swapped(core, number):
    return pl.multiple_of((core ^ number) * HALF, HALF)


def start_all(copies):
    for copy in copies:
        copy.start()
    return copies


def wait_all(copies):
    for copy in copies:
        copy.wait()


def half_copies(core, source, target, sems):
    return [start_all([
        pltpu.make_async_copy(source.at[pl.ds(3 * group, 3), pl.ds(swapped(core, part), HALF), :],
                              target.at[group, part], sems.at[group, part])
        for part in range(2)]) for group in range(3)]


def half_conv(band, weight, copies, bias, total):
    for down in range(3):
        wait_all(copies[down])

        def body(half, carry, down=down):
            at = half_rows(half)
            value = dot(tap_band(band, half, down), weight[down].reshape(6 * HALF, HALF))
            total[at, :] = value + (total[at, :] if down > 0 else bias)
            return carry

        lax.fori_loop(0, 2, body, 0)


def tap_copies(core, own_ref, peer_ref, all_ref, sems, group):
    lead = (pl.ds(3 * group, 3),)
    return weight_copies(core, own_ref, peer_ref, all_ref, sems.at[group], lead)


def weight_copies(core, own_ref, peer_ref, all_ref, sems, lead):
    copies = []
    for local in range(2):
        source = pl.ds(pl.multiple_of((core ^ local) * HALF, HALF), HALF)
        target = pl.ds(local * HALF, HALF)
        for which, ref in enumerate((own_ref, peer_ref)):
            held = pl.ds(which * HALF, HALF)
            if own_ref.shape[-1] == HALF:
                src, dst = (source, slice(None)), (target, held)
            else:
                src, dst = (slice(None), source), (held, target)
            copies.append(
                pltpu.make_async_copy(
                    ref.at[lead + src], all_ref.at[lead + dst], sems.at[2 * local + which]
                )
            )
    return copies


def params(limit):
    return pltpu.CompilerParams(vmem_limit_bytes=limit * MB)


def cost(micros):
    return pl.CostEstimate(flops=int(micros * 1.1e9), bytes_accessed=1 << 20, transcendentals=0)


def shape(rows, columns, dtype):
    return jax.ShapeDtypeStruct((rows, columns), dtype)


def in_hbm(*arrays):
    return [pltpu.with_memory_space_constraint(array, pltpu.HBM) for array in arrays]


def fetch(source, target, sem):
    copy = pltpu.make_async_copy(source, target, sem)
    copy.start()
    return copy


def both_rows(own_ref, peer_ref, row):
    return jnp.concatenate([own_ref[at_row(row), :], peer_ref[at_row(row), :]], 1).astype(F32)


def front_kernel(core_ref, eq_ref, x_hbm, xp_hbm, w_hbm, vec_ref, peer_ref, act_own_hbm, act_peer_hbm, stat_own, stat_peer, band,
                 conv_hbm, next_ref, stat2_ref, x_own, x_peer, act_own, act_peer, weight, total, sems):
    core = core_ref[0]
    first = fetch(x_hbm.at[core], x_own, sems.at[3, 0])
    second = fetch(xp_hbm.at[core], x_peer, sems.at[3, 1])
    copies = half_copies(core, w_hbm, weight, sems)
    first.wait()
    norm_forward(lambda row: x_own[at_row(row), :].astype(F32), (act_own,), stat_own, eq_ref,
                 vec_ref[0:1, :], vec_ref[1:2, :], swish)
    second.wait()
    norm_forward(lambda row: x_peer[at_row(row), :].astype(F32), (act_peer,), stat_peer, eq_ref,
                 peer_ref[0:1, :], peer_ref[1:2, :], swish)
    stores = [fetch(act_own, act_own_hbm, sems.at[4, 0]), fetch(act_peer, act_peer_hbm, sems.at[4, 1])]
    fill_bands(band, lambda row: both_rows(act_own, act_peer, row), eq_ref, parts_apart)
    half_conv(band, weight, copies, vec_ref[2:3, :], total)
    stores.append(fetch(total, conv_hbm, sems.at[3, 0]))
    norm_forward(lambda row: total[at_row(row), :], (next_ref,), stat2_ref, eq_ref, vec_ref[3:4, :],
                 vec_ref[4:5, :], swish)
    wait_all(stores)


def front_peer_kernel(core_ref, eq_ref, band, w_hbm, vec_ref, conv_hbm, next_ref, stat2_ref, weight,
                      total, sems):
    copies = half_copies(core_ref[0], w_hbm, weight, sems)
    half_conv(band, weight, copies, vec_ref[2:3, :], total)
    store = fetch(total, conv_hbm, sems.at[3, 0])
    norm_forward(lambda row: total[at_row(row), :], (next_ref,), stat2_ref, eq_ref, vec_ref[3:4, :],
                 vec_ref[4:5, :], swish)
    store.wait()


def front_call(core, eq, pixels, pixels_peer, weight, own_vectors, peer_vectors):
    half = pltpu.HBM((PIX, HALF), BF)
    return pl.pallas_call(
        front_kernel,
        out_shape=(half, half, shape(8, HALF, F32), shape(8, HALF, F32),
                   pltpu.VMEM((2, BAND, 3 * C), BF), pltpu.HBM((PIX, HALF), F32),
                   shape(PIX, HALF, BF), shape(8, HALF, F32)),
        in_specs=[SM, SM, HBM, HBM, HBM, VM, VM],
        out_specs=(HBM, HBM, VM, VM, VM, HBM, VM, VM),
        scratch_shapes=[pltpu.VMEM((PIX, HALF), BF)] * 4
        + [pltpu.VMEM((3, 2, 3, HALF, HALF), BF), pltpu.VMEM((PIX, HALF), F32),
           pltpu.SemaphoreType.DMA((5, 2))],
        name="front", compiler_params=params(14), cost_estimate=cost(9),
    )(core, eq, *in_hbm(pixels, pixels_peer, weight), own_vectors, peer_vectors)


def front_peer_call(core, eq, band, weight, vec):
    return pl.pallas_call(
        front_peer_kernel,
        out_shape=(pltpu.HBM((PIX, HALF), F32), shape(PIX, HALF, BF), shape(8, HALF, F32)),
        in_specs=[SM, SM, VM, HBM, VM], out_specs=(HBM, VM, VM),
        scratch_shapes=[pltpu.VMEM((3, 2, 3, HALF, HALF), BF), pltpu.VMEM((PIX, HALF), F32),
                        pltpu.SemaphoreType.DMA((4, 2))],
        name="front_peer", compiler_params=params(14), cost_estimate=cost(5),
    )(core, eq, band, *in_hbm(weight), vec)


def attn_kernel(core_ref, eq_ref, act_own, act_peer, own_ref, peer_ref, x_ref, xp_ref, g_own, g_peer,
                wq_o, wq_p, wk_o, wk_p, wv_o, wv_p, wp_o, wp_p, vec_ref, out_own, out_peer, gmid_hbm,
                gconv_ref, small_ref, dquery, dkey, dvalue, mixed, normed_ref, weight, gfull, query,
                keys, values, gmixed, probs, gscores, gnormed, mid_ref, taps, band, x_own, x_peer,
                stat_ref, sems):
    core = core_ref[0]
    groups = [tap_copies(core, own_ref, peer_ref, taps, sems.at[5:8], down) for down in range(3)]
    start_all(groups[0])
    extra = [fetch(x_ref.at[core], x_own, sems.at[4, 2]), fetch(xp_ref.at[core], x_peer, sems.at[4, 3])]
    fill_bands(band, lambda row: both_rows(act_own, act_peer, row), eq_ref)
    start_all(groups[1])
    start_all(groups[2])
    wait_all(extra)
    for down in range(3):
        wait_all(groups[down])
        if down == 0:
            copies = []
            for index, (own, peer) in enumerate(
                    ((wq_o, wq_p), (wk_o, wk_p), (wv_o, wv_p), (wp_o, wp_p))):
                copies += start_all(
                    weight_copies(core, own, peer, weight.at[index], sems.at[index], ()))
            copies.append(fetch(g_own.at[core], gfull.at[:, 0:HALF], sems.at[4, 0]))
            copies.append(fetch(g_peer.at[core], gfull.at[:, HALF:C], sems.at[4, 1]))

        def conv(half, carry, down=down):
            at = half_rows(half)
            value = dot(tap_band(band, half, down),
                        taps[3 * down : 3 * down + 3].reshape(3 * C, C))
            if down > 0:
                value = value + mid_ref[at, :]
            else:
                value = value + vec_ref[5:6, :] + jnp.concatenate(
                    [x_own[at, :], x_peer[at, :]], 1).astype(F32)
            mid_ref[at, :] = value
            return carry

        lax.fori_loop(0, 2, conv, 0)
    norm_forward(lambda row: mid_ref[at_row(row), :], (normed_ref,), stat_ref, eq_ref,
                 vec_ref[6:7, :], vec_ref[7:8, :], lambda v: v)
    wait_all(copies)
    normed = normed_ref[...]
    query[...] = (dot(normed, weight[0]) + vec_ref[8:9, :]).astype(BF)
    keys[...] = dot(normed, weight[1]).astype(BF)
    values[...] = (dot(normed, weight[2]) + vec_ref[9:10, :]).astype(BF)
    gmixed[...] = dot_nt(gfull[...], weight[3]).astype(BF)

    rows = 256
    spot = lax.broadcasted_iota(jnp.int32, (1, PIX), 1)
    right = (spot & (SIDE - 1)) >= 16
    low = spot >= PIX // 2

    def block(index, carry):
        start = pl.multiple_of(index * rows, rows)
        at = pl.ds(start, rows)
        half = (start >= PIX // 2).astype(jnp.int32) * 2
        bias = []
        for side in range(2):
            base = (half + side) * 4
            row = jnp.where(low, jnp.where(right, eq_ref[base + 3], eq_ref[base + 2]),
                            jnp.where(right, eq_ref[base + 1], eq_ref[base]))
            bias.append(jnp.where(row > 0.5, 0.0, -1e30).reshape(1, 1, 1, PIX))
        bias = jnp.concatenate(bias, 1)
        scores = dot_nt(query[at, :], keys[...]) * (SCALE * LOG2E)
        scores = (scores.reshape(rows // SIDE, 2, 16, PIX) + bias).reshape(rows, PIX)
        expo = jnp.exp2(scores - jnp.max(scores, axis=1, keepdims=True))
        wide = expo * (1.0 / jnp.sum(expo, axis=1, keepdims=True))
        narrow = wide.astype(BF)
        probs[at, :] = narrow
        mixed[at, :] = dot(narrow, values[...]).astype(BF)
        gprobs = dot_nt(gmixed[at, :], values[...])
        delta = jnp.sum(wide * gprobs, axis=1, keepdims=True)
        grads = (wide * (gprobs - delta)).astype(BF)
        gscores[at, :] = grads
        dquery[at, :] = (dot(grads, keys[...]) * SCALE).astype(BF)
        return carry

    lax.fori_loop(0, PIX // rows, block, 0)

    def total(value):
        return jnp.sum(value.astype(F32), axis=0, keepdims=True)

    dkey[...] = (dot_tn(gscores[...], query[...]) * SCALE).astype(BF)
    dvalue[...] = dot_tn(probs[...], gmixed[...]).astype(BF)
    gnormed[...] = (dot_nt(dquery[...], weight[0]) + dot_nt(dkey[...], weight[1])
                    + dot_nt(dvalue[...], weight[2]))
    dbq, dbv, dbp = total(dquery[...]), total(dvalue[...]), total(gfull[...])

    out = mid_ref[...] + dot(mixed[...], weight[3]) + vec_ref[10:11, :]
    out_own[...] = out[:, :HALF]
    out_peer[...] = out[:, HALF:]

    def finish(row, change):
        grad = gfull[at_row(row), :].astype(F32) + change
        gnormed[at_row(row), :] = grad
        gconv_ref[at_row(row), :] = grad.astype(BF)

    dgain, dshift = norm_backward(
        lambda row: mid_ref[at_row(row), :], lambda row: gnormed[at_row(row), :], None, stat_ref,
        eq_ref, vec_ref[6:7, :], vec_ref[7:8, :], False, finish)
    store = fetch(gnormed, gmid_hbm, sems.at[4, 3])
    small_ref[...] = jnp.concatenate(
        [dgain, dshift, dbq, dbv, dbp, total(gconv_ref[...]), dbq, dbq], 0)
    store.wait()


def attn_call(core, eq, acts, own, peer, x, g, weights, vec):
    flat = [w for pair_of in weights for w in pair_of]
    return pl.pallas_call(
        attn_kernel,
        out_shape=(shape(PIX, HALF, F32), shape(PIX, HALF, F32), pltpu.HBM((PIX, C), F32),
                   shape(PIX, C, BF), shape(8, C, F32)) + (pltpu.VMEM((PIX, C), BF),) * 5,
        in_specs=[SM, SM, VM, VM] + [HBM] * 14 + [VM],
        out_specs=(VM, VM, HBM) + (VM,) * 7,
        scratch_shapes=[pltpu.VMEM((4, C, C), BF)] + [pltpu.VMEM((PIX, C), BF)] * 5
        + [pltpu.VMEM((PIX, PIX), BF)] * 2 + [pltpu.VMEM((PIX, C), F32)] * 2
        + [pltpu.VMEM((9, C, C), BF), pltpu.VMEM((2, BAND, 3 * C), BF)]
        + [pltpu.VMEM((PIX, HALF), BF)] * 2
        + [pltpu.VMEM((8, C), F32), pltpu.SemaphoreType.DMA((8, 4))],
        name="attention", compiler_params=params(34), cost_estimate=cost(28),
    )(core, eq, *acts, *in_hbm(own, peer, *x, *g, *flat), vec)


def attn_wgrad_kernel(core_ref, normed_ref, dquery, dkey, dvalue, mixed, g_own, g_peer, dw_own,
                      dw_peer, g_mine, g_back, sems):
    core = core_ref[0]
    copies = [fetch(g_own.at[core], g_mine, sems.at[0]), fetch(g_peer.at[core], g_back, sems.at[1])]
    normed = normed_ref[...]
    for index, ref in enumerate((dquery, dkey, dvalue)):
        full = dot_tn(normed, ref[...]).astype(BF)
        for local in range(2):
            target = pl.multiple_of(index * C + (core ^ local) * HALF, HALF)
            part = full[local * HALF : (local + 1) * HALF, :]
            dw_own[pl.ds(target, HALF), :] = part[:, :HALF]
            dw_peer[pl.ds(target, HALF), :] = part[:, HALF:]
    for copy in copies:
        copy.wait()
    for local, ref in enumerate((g_mine, g_back)):
        target = pl.multiple_of(3 * C + (core ^ local) * HALF, HALF)
        part = dot_tn(mixed[...], ref[...]).astype(BF)
        dw_own[pl.ds(target, HALF), :] = part[:HALF]
        dw_peer[pl.ds(target, HALF), :] = part[HALF:]


def attn_wgrad_call(core, normed, dquery, dkey, dvalue, mixed, g):
    return pl.pallas_call(
        attn_wgrad_kernel, out_shape=(shape(4 * C, HALF, BF),) * 2,
        in_specs=[SM] + [VM] * 5 + [HBM] * 2, out_specs=(VM, VM),
        scratch_shapes=[pltpu.VMEM((PIX, HALF), BF)] * 2 + [pltpu.SemaphoreType.DMA((2,))],
        name="attention_weights", compiler_params=params(6), cost_estimate=cost(3),
    )(core, normed, dquery, dkey, dvalue, mixed, *in_hbm(*g))


def fetch_all(sources, targets, sems):
    return [fetch(source, target, sems.at[index])
            for index, (source, target) in enumerate(zip(sources, targets))]


def wgrad2_kernel(core_ref, eq_ref, *refs):
    sources, (out_ref, act_mine, act_other, grad_mine, grad_other, band, band_other, sems) = (
        refs[:4], refs[4:])
    core = core_ref[0]
    copies = fetch_all(sources, (act_mine, act_other, grad_mine, grad_other), sems)
    copies[0].wait()
    fill_bands(band, lambda row: act_mine[at_row(row), :], eq_ref.at[0])
    copies[1].wait()
    fill_bands(band_other, lambda row: act_other[at_row(row), :], eq_ref.at[1])
    for copy in copies[2:]:
        copy.wait()

    def body(down, carry):
        for local in range(2):
            full = 0.0
            for half in range(2):
                rows = slice(half * (PIX // 2), (half + 1) * (PIX // 2))
                full = full + dot_tn(tap_band(band, half, down),
                                     grad_mine[rows, local * HALF : (local + 1) * HALF])
                full = full + dot_tn(tap_band(band_other, half, down),
                                     grad_other[rows, (1 - local) * HALF : (2 - local) * HALF])
            full = full.astype(BF)
            for index in range(3):
                base = (3 * down + index) * C + (core ^ local) * HALF
                out_ref[pl.ds(pl.multiple_of(base, HALF), HALF), :] = full[
                    index * HALF : (index + 1) * HALF]
        return carry

    lax.fori_loop(0, 3, body, 0)


def wgrad2_call(core, eqs, *arrays):
    return pl.pallas_call(
        wgrad2_kernel, out_shape=shape(9 * C, HALF, BF), in_specs=[SM, SM] + [HBM] * 4,
        out_specs=VM,
        scratch_shapes=[pltpu.VMEM((PIX, HALF), BF)] * 2 + [pltpu.VMEM((PIX, C), BF)] * 2
        + [pltpu.VMEM((2, BAND, 3 * HALF), BF)] * 2 + [pltpu.SemaphoreType.DMA((4,))],
        name="wgrad2", compiler_params=params(14), cost_estimate=cost(7),
    )(core, eqs, *in_hbm(*arrays))


TAPS = 6


def wgrad1_kernel(core_ref, eq_ref, *refs):
    sources, (out_ref, tail_ref, band, band_other, act, act2, grad_mine, grad_other, sems) = (
        refs[:6], refs[6:])
    core = core_ref[0]
    copies = fetch_all(sources, (grad_mine, grad_other, act.at[:, 0:HALF], act.at[:, HALF:C],
                                 act2.at[:, 0:HALF], act2.at[:, HALF:C]), sems)
    copies[0].wait()
    fill_bands(band, lambda row: grad_mine[at_row(row), :], eq_ref.at[0])
    copies[1].wait()
    fill_bands(band_other, lambda row: grad_other[at_row(row), :], eq_ref.at[1])
    for copy in copies[2:]:
        copy.wait()

    def group(down, out, base):
        full = 0.0
        for half in range(2):
            rows = slice(half * (PIX // 2), (half + 1) * (PIX // 2))
            full = full + dot_tn(act[rows, :], tap_band(band, half, down))
            full = full + dot_tn(act2[rows, :], tap_band(band_other, half, down))
        full = full.astype(BF)
        for index in range(3):
            for local in range(2):
                where = base + (2 - index) * C + (core ^ local) * HALF
                out[pl.ds(pl.multiple_of(where, HALF), HALF), :] = full[
                    local * HALF : (local + 1) * HALF, index * HALF : (index + 1) * HALF]

    group(0, tail_ref, 0)

    def body(down, carry):
        group(down, out_ref, (2 - down) * 3 * C)
        return carry

    lax.fori_loop(1, 3, body, 0)


def wgrad1_call(core, eqs, *arrays):
    return pl.pallas_call(
        wgrad1_kernel, out_shape=(shape(TAPS * C, HALF, BF), shape((9 - TAPS) * C, HALF, BF)),
        in_specs=[SM, SM] + [HBM] * 6, out_specs=(VM, VM),
        scratch_shapes=[pltpu.VMEM((2, BAND, 3 * HALF), BF)] * 2 + [pltpu.VMEM((PIX, C), BF)] * 2
        + [pltpu.VMEM((PIX, HALF), BF)] * 2 + [pltpu.SemaphoreType.DMA((6,))],
        name="wgrad1", compiler_params=params(16), cost_estimate=cost(7),
    )(core, eqs, *in_hbm(*arrays))


def dgrad_kernel(first, core_ref, eq_ref, own_ref, peer_ref, vec_ref, *refs):
    if first:
        (grad_own, grad_peer, stat_own, stat_peer, x_hbm, xp_hbm, gmid_hbm, out_own, out_peer, small_ref, weight, patch,
         total, stat_ref, sems, x_own, x_peer, gmid_ref) = refs
        load = lambda row: both_rows(x_own, x_peer, row)
        load_grad = lambda row: both_rows(grad_own, grad_peer, row)
        sources = (x_hbm.at[core_ref[0]], xp_hbm.at[core_ref[0]], gmid_hbm)
        held = (x_own, x_peer, gmid_ref)
        gain, shift = vec_ref[0:1, :], vec_ref[1:2, :]
    else:
        (grad_ref, stat_own, stat_peer, in_own, in_peer, out_own, out_peer, small_ref, weight, patch,
         total, stat_ref, sems, mine, back) = refs
        load = lambda row: both_rows(mine, back, row)
        load_grad = lambda row: grad_ref[at_row(row), :]
        sources, held = (in_own, in_peer), (mine, back)
        gain, shift = vec_ref[3:4, :], vec_ref[4:5, :]
    stat_ref[:, :HALF] = stat_own[...]
    stat_ref[:, HALF:] = stat_peer[...]
    copies = [tap_copies(core_ref[0], own_ref, peer_ref, weight, sems, 2 - down)
              for down in range(3)]
    for group in copies:
        for copy in group:
            copy.start()
    later = fetch_all(sources, held, sems.at[3])
    fill_bands(patch, load_grad, eq_ref)
    for down in range(3):
        for copy in copies[down]:
            copy.wait()

        def body(half, carry, down=down):
            value = total[half_rows(half), :] if down > 0 else 0.0
            for t in range(3):
                value = value + dot_nt(tap_band(patch, half, down)[:, t * C : (t + 1) * C],
                                       weight[8 - (3 * down + t)])
            total[half_rows(half), :] = value
            return carry

        lax.fori_loop(0, 2, body, 0)
    for copy in later:
        copy.wait()

    def finish(row, change):
        at = at_row(row)
        if first:
            change = change + gmid_ref[at, :]
        out_own[at, :] = change[:, :HALF].astype(out_own.dtype)
        out_peer[at, :] = change[:, HALF:].astype(out_peer.dtype)

    dgain, dshift = norm_backward(load, lambda row: total[at_row(row), :], total, stat_ref, eq_ref,
                                  gain, shift, True, finish)
    bias = [jnp.sum(ref[...].astype(F32), axis=0, keepdims=True) for ref in (out_own, out_peer)]
    bias = jnp.concatenate(bias, 1)
    small_ref[...] = jnp.concatenate([dgain, dshift, bias] + [dgain] * 5, 0)


def dgrad_call(core, eq, grad, own, peer, vec, stats, source, gmid=None):
    first = gmid is not None
    extra = (*source, gmid) if first else source
    held = [pltpu.VMEM((PIX, HALF), BF if first else F32)] * 2
    held += [pltpu.VMEM((PIX, C), F32)] if first else []
    outs = (shape(PIX, HALF, F32 if first else BF),) * 2
    return pl.pallas_call(
        functools.partial(dgrad_kernel, first),
        out_shape=outs + (shape(8, C, F32),),
        in_specs=[SM, SM, HBM, HBM, VM] + [VM] * (len(grad) + len(stats)) + [HBM] * len(extra),
        out_specs=(VM,) * 3,
        scratch_shapes=[pltpu.VMEM((9, C, C), BF), pltpu.VMEM((2, BAND, 3 * C), BF),
                        pltpu.VMEM((PIX, C), F32), pltpu.VMEM((8, C), F32),
                        pltpu.SemaphoreType.DMA((4, 4))] + held,
        name="dgrad1" if first else "dgrad2", compiler_params=params(16), cost_estimate=cost(10),
    )(core, eq, *in_hbm(own, peer), vec, *grad, *stats, *in_hbm(*extra))


EVERY, TIED, SMALL_FROM = "asrf", 9, 0
ORDERS = {
    "second": ((2, 0, 1), (0, 1, 2)),
    "attn": ((1, 2, 0), (1, 2, 0)),
    "first": ((2, 0, 1), (0, 1, 2)),
    "rest": ((1, 2, 0), (1, 2, 0)),
}


def orders_of(kind, size):
    bits = size.bit_length() - 1
    return [[*order, *range(3, bits)] for order in ORDERS[kind]]


def exchange(array, orders, stage, size):
    moves = [((d, c), (d ^ (1 << orders[c][stage]), c)) for d in range(size) for c in range(2)]
    return lax.ppermute(array, ("dp", "chan"), [(a[0] * 2 + a[1], b[0] * 2 + b[1]) for a, b in moves])


def side_of(orders, stage):
    bit = jnp.where(lax.axis_index("chan") == 0, orders[0][stage], orders[1][stage])
    return (lax.axis_index("dp") >> bit) & 1


def side_base(orders):
    base = 0
    for stage in range(len(orders[0])):
        base = base * 2 + side_of(orders, stage)
    return base


class Chain:
    def __init__(self, part, kind, size):
        self.value, self.size, self.orders, self.step = part, size, orders_of(kind, size), 0
        self.stages, self.rows = len(self.orders[0]), part.shape[0]

    def advance(self):
        stage = self.step if self.step < self.stages else 2 * self.stages - 1 - self.step
        if self.step < self.stages:
            half = self.value.shape[0] // 2
            side = side_of(self.orders, stage)
            send = lax.dynamic_slice_in_dim(self.value, (1 - side) * half, half, 0)
            keep = lax.dynamic_slice_in_dim(self.value, side * half, half, 0)
            self.value = keep + exchange(send, self.orders, stage, self.size)
        else:
            back = exchange(self.value, self.orders, stage, self.size)
            self.value = jnp.concatenate([self.value, back], 0) if stage > 0 else (self.value, back)
        self.step += 1


def together(chains, *values):
    held = lax.optimization_barrier(([c.value for c in chains], values))
    for chain, value in zip(chains, held[0]):
        chain.value = value
    return held[1]


def after(value, *others):
    return lax.optimization_barrier((value, *others))[0]


def spread_kernel(plan, base_ref, *refs):
    count = len(plan)
    ins, out_hbm, wide, sems = refs[:count], refs[-2 * count - 1], refs[-2 * count : -count], refs[-count:]
    copies = []
    for index, (start, first, rows) in enumerate(plan):
        wide[index][...] = ins[index][...].astype(F32)
        for block in range(ins[index].shape[0] // rows):
            row = start + ((block + first) ^ base_ref[index]) * rows
            copies.append(fetch(
                wide[index].at[block * rows : (block + 1) * rows, :],
                out_hbm.at[pl.ds(pl.multiple_of(row, rows & -rows), rows), :],
                sems[index].at[block]))
    wait_all(copies)


def spread(parts, rows, token, into=None):
    plan = [(start, first, chain.rows // chain.size) for _, chain, start, first in parts]
    arrays = [part[0] for part in parts]
    base = jnp.stack([side_base(part[1].orders) for part in parts]).astype(jnp.int32)
    held = () if into is None else (into,)
    return pl.pallas_call(
        functools.partial(spread_kernel, plan), out_shape=pltpu.HBM((rows, HALF), F32),
        in_specs=[SM] + [VM] * len(arrays) + [HBM] * len(held), out_specs=HBM,
        input_output_aliases={} if into is None else {1 + len(arrays): 0},
        scratch_shapes=[pltpu.VMEM(array.shape, F32) for array in arrays]
        + [pltpu.SemaphoreType.DMA((array.shape[0] // one[2],)) for array, one in zip(arrays, plan)],
        compiler_params=params(14), name="spread", cost_estimate=cost(2),
    )(after(base, token), *arrays, *held)


def second_target(row):
    return 0, row // C * HALF + row % HALF, slice(row // HALF % 2 * HALF, (row // HALF % 2 + 1) * HALF)


def attn_target(row):
    if row < 3 * C:
        return row // C, row % C, slice(0, HALF)
    row -= 3 * C
    return 3, row % HALF, slice(row // HALF * HALF, (row // HALF + 1) * HALF)


def place_kernel(size, targets, base_ref, *refs):
    ins, outs, held = refs[: 2 * len(targets)], refs[2 * len(targets) : -1], refs[-1]
    start = 0
    for index, target in enumerate(targets):
        part, part2 = ins[2 * index : 2 * index + 2]
        half = part.shape[0]
        held[start : start + half, :] = part[...]
        held[start + half : start + 2 * half, :] = part2[...]
        rows = 2 * half // size
        piece = math.gcd(rows, HALF)
        for row in range(0, 2 * half, piece):
            source = ((row // rows) ^ base_ref[index]) * rows + row % rows + start
            which, at, columns = target(row)
            outs[which][at : at + piece, columns] = held[
                pl.ds(pl.multiple_of(source, piece), piece), :].astype(F32)
        start += 2 * half


def place(chains, targets, shapes, token):
    parts = [part for chain in chains for part in chain.value]
    rows = sum(part.shape[0] for part in parts)
    base = jnp.stack([side_base(chain.orders) for chain in chains]).astype(jnp.int32)
    return pl.pallas_call(
        functools.partial(place_kernel, chains[0].size, targets),
        out_shape=tuple(shape(*one, F32) for one in shapes), in_specs=[SM] + [VM] * len(parts),
        out_specs=(VM,) * len(shapes), scratch_shapes=[pltpu.VMEM((rows, HALF), BF)],
        compiler_params=params(12), name="place", cost_estimate=cost(2),
    )(after(base, token), *parts)


def swap(array):
    return lax.ppermute(array, "chan", [(0, 1), (1, 0)])


def shards(pixels, tile_ids, first_gain, first_shift, first_conv, first_bias, second_gain,
           second_shift, second_conv, second_bias, attn_gain, attn_shift, query_weight,
           query_bias, key_weight, value_weight, value_bias, proj_weight, proj_bias, cotangent,
           *, size):
    index = lax.axis_index("chan")
    core = index.reshape(1).astype(jnp.int32)
    tiles = tile_ids.reshape(2, 2, 16, 2, 16)[:, :, 0, :, 0].reshape(2, 4)
    eqs = (tiles[:, :, None] == tiles[:, None, :]).astype(F32).reshape(2, 16)
    eqs = jnp.where(index == 0, eqs, eqs[::-1])
    own_vectors = jnp.stack([first_gain, first_shift, first_bias, second_gain, second_shift,
                             second_bias, attn_gain, attn_shift, query_bias, value_bias, proj_bias])
    pixels_peer = swap(pixels)
    pixels_peer, own_vectors, eqs = lax.optimization_barrier((pixels_peer, own_vectors, eqs))
    eq = eqs[0]
    peer_vectors = swap(own_vectors)
    first_conv, peer_vectors, pixels_peer = lax.optimization_barrier(
        (first_conv, peer_vectors, pixels_peer))
    first_peer = swap(first_conv)
    weights = lax.optimization_barrier(
        (query_weight, key_weight, value_weight, proj_weight, peer_vectors))[:4]
    weights_peer = [swap(array) for array in weights]
    vectors = jnp.concatenate([own_vectors, peer_vectors], 1)
    x = (pixels, pixels_peer)
    act_own, act_peer, stat_own, stat_peer, band, conv1_own, act2_own, stat2_own = front_call(
        core, eq, *x, first_conv, own_vectors, peer_vectors)
    first_peer, act2_own, act_own, act_peer, second_conv, cotangent, *weights_peer = (
        lax.optimization_barrier((first_peer, act2_own, act_own, act_peer, second_conv, cotangent,
                                  *weights_peer)))
    second_peer, g_peer = swap(second_conv), swap(cotangent)
    act_other = (swap(act_peer), swap(act_own))
    conv1_peer, act2_peer, stat2_peer = front_peer_call(core, eq, band, first_peer, peer_vectors)
    act2_peer, second_peer, g_peer = lax.optimization_barrier((act2_peer, second_peer, g_peer))
    g = (cotangent, g_peer)
    act2_other = swap(act2_peer)
    out_own, out_peer, gmid, gconv2, small3, *parts, normed = attn_call(
        core, eq, (act2_own, act2_peer), second_conv, second_peer, x, g,
        list(zip(weights, weights_peer)), vectors)
    gconv2, act2_other, *act_other = lax.optimization_barrier((gconv2, act2_other, *act_other))
    gconv2_other = swap(gconv2)
    dattn, dattn_peer = attn_wgrad_call(core, normed, *parts, g)
    dattn, gconv2, gconv2_other = lax.optimization_barrier((dattn, gconv2, gconv2_other))
    attn_other = swap(dattn_peer)
    part = wgrad2_call(core, eqs, act2_own, act2_other, gconv2, gconv2_other)
    attn_other, part = lax.optimization_barrier((attn_other, part))
    second, attn_sum = Chain(part, "second", size), Chain(dattn + attn_other, "attn", size)
    (gconv2,) = together([second, attn_sum], gconv2)

    for chain in (attn_sum, second):
        chain.advance()
    gconv1_own, gconv1_peer, small2 = dgrad_call(
        core, eq, (gconv2,), second_conv, second_peer, vectors, (stat2_own, stat2_peer),
        (conv1_own, conv1_peer))
    gconv1_other = swap(gconv1_peer)
    gconv1_own, gconv1_other = together([second, attn_sum], gconv1_own, gconv1_other)

    for chain in (attn_sum, second):
        chain.advance()
    part, tail = wgrad1_call(core, eqs, gconv1_own, gconv1_other, act_own, act_peer, *act_other)
    first, rest = Chain(part, "first", size), Chain(tail, "rest", size)
    (gconv1_own,) = together([second, attn_sum, first, rest], gconv1_own)

    known = {"a": attn_sum, "s": second, "r": rest, "f": first}
    every = [known[name] for name in EVERY]
    for chain in every:
        chain.advance()
    pix_own, pix_peer, small1 = dgrad_call(core, eq, (gconv1_own, gconv1_peer), first_conv,
                                           first_peer, vectors, (stat_own, stat_peer), x, gmid)
    small = jnp.concatenate([small1, small2, small3], 0)
    pix_peer, out_peer, small = together(every, pix_peer, out_peer, small)

    small = small[:, :HALF] + swap(small[:, HALF:])
    pix_back = swap(pix_peer)
    out_back = swap(out_peer)
    bits = size.bit_length() - 1
    turn, bit = 0, 0
    token = core
    while any(chain.step < 2 * bits for chain in every):
        for chain in every:
            if chain.step < 2 * bits:
                chain.advance()
                if turn < TIED:
                    (token,) = together([chain], token)
        if turn >= SMALL_FROM and bit < bits:
            small = small + lax.ppermute(
                small, "dp", [(i, i ^ (1 << bit)) for i in range(size)])
            small, token = lax.optimization_barrier((small, token))
            bit += 1
        turn += 1
    (sums2,) = place([second], [second_target], [(9 * HALF, C)], core)
    sums3 = place([attn_sum], [attn_target], [(C, HALF), (C, HALF), (C, HALF), (HALF, C)], core)
    mine, back = first.value
    half = size // 2
    sums1 = spread([(rest.value[0], rest, TAPS * C, 0), (rest.value[1], rest, TAPS * C, half),
                    (mine, first, 0, 0)], 9 * C, core)
    back, sums1, sums2, *sums3 = lax.optimization_barrier((back, sums1, sums2, *sums3))
    sums1 = spread([(back, first, 0, half)], 9 * C, token, sums1)

    def unboth(own, back):
        return jnp.where(index == 0, jnp.stack([own, back]), jnp.stack([back, own]))

    return (
        unboth(out_own, out_back), unboth(pix_own, pix_back), small[0], small[1],
        sums1.reshape(9, C, HALF), small[10], small[8], small[9], sums2.reshape(9, HALF, C),
        small[21], small[16], small[17], sums3[0], small[18], sums3[1], sums3[2], small[19],
        sums3[3], small[20],
    )


def solution(mesh):
    chan = P("chan")
    rows = P("dp", None, "chan")
    return jax.shard_map(
        functools.partial(shards, size=mesh.shape["dp"]),
        mesh=mesh,
        in_specs=(
            rows, P("dp", None), chan, chan, P(None, None, "chan"), chan, chan, chan,
            P(None, "chan", None), chan, chan, chan, P(None, "chan"), chan, P(None, "chan"),
            P(None, "chan"), chan, P("chan", None), chan, rows,
        ),
        out_specs=(
            rows, rows, chan, chan, P(None, None, "chan"), chan, chan, chan,
            P(None, "chan", None), chan, chan, chan, P(None, "chan"), chan, P(None, "chan"),
            P(None, "chan"), chan, P("chan", None), chan,
        ),
        check_vma=False,
    )
```

```python
import functools
import math
import jax
import jax.numpy as jnp
from jax import lax
from jax.experimental import pallas as pl
from jax.experimental.pallas import tpu as pltpu
from jax.sharding import PartitionSpec as P

C = 512
HALF = 256
GROUP = 16
SIDE = 32
PIX = 1024
EPSILON = 1e-06
BF = jnp.bfloat16
F32 = jnp.float32
MB = 1024 * 1024
VM = pl.BlockSpec(memory_space=pltpu.VMEM)
SM = pl.BlockSpec(memory_space=pltpu.SMEM)
HBM = pl.BlockSpec(memory_space=pltpu.HBM)
SCALE = C ** (-0.5)
LOG2E = 1.4426950408889634


def dot(first, second):
    return jnp.dot(first, second, preferred_element_type=F32)


def dot_nt(first, second):
    return lax.dot_general(first, second, (((1,), (1,)), ((), ())), preferred_element_type=F32)


def dot_tn(first, second):
    return lax.dot_general(first, second, (((0,), (0,)), ((), ())), preferred_element_type=F32)


def at_row(row):
    return pl.ds(pl.multiple_of(row * SIDE, SIDE), SIDE)


def group_sums(rows):
    full = jnp.concatenate(rows, 0)
    width = full.shape[1]
    lane = lax.broadcasted_iota(jnp.int32, full.shape, 1)
    for step in (1, 2, 4, 8):
        full = full + jnp.where(
            (lane & step) == 0, pltpu.roll(full, width - step, 1), pltpu.roll(full, step, 1)
        )
    return [full[i : i + 1] for i in range(len(rows))]


def image_means(sums, eq_ref):
    rows = []
    for i in range(4):
        total, count = 0.0, 0.0
        for j in range(4):
            total = total + eq_ref[4 * i + j] * sums[j]
            count = count + eq_ref[4 * i + j]
        rows.append(total / (count * float(256 * GROUP)))
    return group_sums(rows)


def tiles_of(rows):
    return rows.reshape(2, 16, rows.shape[-1])


def pair(rows, top):
    return jnp.concatenate([rows[2 * top + side].reshape(1, 1, -1) for side in range(2)], 0)


def over_canvas(step, count, width=C, unroll=2):
    found = [[] for _ in range(count)]
    for top in range(2):
        zero = tuple(jnp.zeros((2, 16, width), F32) for _ in range(count))

        def body(index, carry, top=top):
            return tuple(a + b for a, b in zip(carry, step(top, top * 16 + index)))

        totals = lax.fori_loop(0, 16, body, zero, unroll=unroll)
        for n in range(count):
            columns = jnp.sum(totals[n], axis=1)
            found[n] += [columns[0:1], columns[1:2]]
    return found


def for_rows(step, unroll=2):
    for top in range(2):

        def body(index, carry, top=top):
            step(top, top * 16 + index)
            return carry

        lax.fori_loop(0, 16, body, 0, unroll=unroll)


def norm_stats(load, eq_ref, width):
    (sums,) = over_canvas(lambda top, row: (tiles_of(load(row)),), 1, width)
    means = image_means(sums, eq_ref)
    centers = [pair(means, top) for top in range(2)]

    def square(top, row):
        off = tiles_of(load(row)) - centers[top]
        return (off * off,)

    (squares,) = over_canvas(square, 1, width)
    rstds = [lax.rsqrt(v + EPSILON) for v in image_means(squares, eq_ref)]
    return means, rstds


def swish(value):
    half = 0.5 * value
    return half + half * jnp.tanh(half)


def norm_forward(load, out_refs, stat_ref, eq_ref, gain, shift, act):
    width = gain.shape[-1]
    means, rstds = norm_stats(load, eq_ref, width)
    stat_ref[...] = jnp.concatenate(means + rstds, 0)
    centers = [pair(means, top) for top in range(2)]
    slopes = [pair([r * gain for r in rstds], top) for top in range(2)]
    offset = shift.reshape(1, 1, width)

    def step(top, row):
        value = (tiles_of(load(row)) - centers[top]) * slopes[top] + offset
        value = act(value).reshape(SIDE, width).astype(BF)
        held = width // len(out_refs)
        for index, ref in enumerate(out_refs):
            ref[at_row(row), :] = value[:, index * held : (index + 1) * held]

    for_rows(step)


def norm_backward(load, load_grad, keep_ref, stat_ref, eq_ref, gain, shift, with_swish, finish):
    stats = stat_ref[...]
    means = [stats[i : i + 1] for i in range(4)]
    rstds = [stats[4 + i : 5 + i] for i in range(4)]
    centers = [pair(means, top) for top in range(2)]
    rates = [pair(rstds, top) for top in range(2)]
    scale, offset = gain.reshape(1, 1, C), shift.reshape(1, 1, C)

    def first(top, row):
        unit = (tiles_of(load(row)) - centers[top]) * rates[top]
        grad = tiles_of(load_grad(row))
        if with_swish:
            value = unit * scale + offset
            gate = 0.5 + 0.5 * jnp.tanh(0.5 * value)
            grad = grad * (gate * (1.0 + value * (1.0 - gate)))
            keep_ref[at_row(row), :] = grad.reshape(SIDE, C)
        return grad, grad * unit

    plain, scaled = over_canvas(first, 2)
    mean_plain = image_means([p * gain for p in plain], eq_ref)
    mean_scaled = image_means([s * gain for s in scaled], eq_ref)
    first_means = [pair(mean_plain, top) for top in range(2)]
    second_means = [pair(mean_scaled, top) for top in range(2)]

    def second(top, row):
        unit = (tiles_of(load(row)) - centers[top]) * rates[top]
        grad = tiles_of(keep_ref[at_row(row), :] if with_swish else load_grad(row))
        change = rates[top] * (grad * scale - first_means[top] - unit * second_means[top])
        finish(row, change.reshape(SIDE, C))

    for_rows(second)
    return sum(scaled), sum(plain)


BAND = PIX // 2 + 2 * SIDE


def row_mask(eq_ref, target, source, right):
    column = lax.broadcasted_iota(jnp.int32, (SIDE, 128), 0)

    def eq(side, other):
        return eq_ref[(2 * target + side) * 4 + 2 * source + other]

    if right == 0:
        mask = jnp.where(column < 16, eq(0, 0), eq(1, 1))
    elif right < 0:
        mask = jnp.where(column < 16, eq(0, 0), jnp.where(column == 16, eq(1, 0), eq(1, 1)))
        mask = jnp.where(column == 0, 0.0, mask)
    else:
        mask = jnp.where(column < 15, eq(0, 0), jnp.where(column == 15, eq(0, 1), eq(1, 1)))
        mask = jnp.where(column == SIDE - 1, 0.0, mask)
    return mask.astype(BF)


def fill_bands(band_ref, load, eq_ref, columns=None):
    width = band_ref.shape[2] // 3

    def put(half, place, value, masks):
        moved = [pltpu.roll(value, 1, 0), value, pltpu.roll(value, SIDE - 1, 0)]
        for index in range(3):
            part = moved[index].astype(BF)
            if masks[index] is not None:
                part = part * jnp.concatenate([masks[index]] * (width // 128), 1)
            if columns is None:
                band_ref[half, at_row(place), index * width : (index + 1) * width] = part
            else:
                for number in range(width // HALF):
                    where = pl.ds(columns(index, number), HALF)
                    band_ref[half, at_row(place), where] = part[
                        :, number * HALF : (number + 1) * HALF]

    for half in range(2):
        inner = [row_mask(eq_ref, half, half, -1), None, row_mask(eq_ref, half, half, 1)]

        def body(index, carry, half=half, inner=inner):
            put(half, index + 1, load(half * 16 + index).astype(F32), inner)
            return carry

        lax.fori_loop(0, 16, body, 0, unroll=2)
        across = [row_mask(eq_ref, half, 1 - half, right) for right in (-1, 0, 1)]
        put(half, 17 - 17 * half, load(16 - half).astype(F32), across)
        band_ref[half, 17 * half * SIDE : (17 * half + 1) * SIDE, :] = jnp.zeros(
            (SIDE, 3 * width), BF)


def half_rows(half):
    return pl.ds(pl.multiple_of(half * (PIX // 2), PIX // 2), PIX // 2)


def tap_band(band_ref, half, down):
    if isinstance(down, int):
        return band_ref[half, down * SIDE : down * SIDE + PIX // 2, :]
    return band_ref[half, pl.ds(pl.multiple_of(down * SIDE, SIDE), PIX // 2), :]


def parts_apart(index, number):
    return number * 3 * HALF + index * HALF


def swapped(core, number):
    return pl.multiple_of((core ^ number) * HALF, HALF)


def start_all(copies):
    for copy in copies:
        copy.start()
    return copies


def wait_all(copies):
    for copy in copies:
        copy.wait()


def half_copies(core, source, target, sems):
    return [start_all([
        pltpu.make_async_copy(source.at[pl.ds(3 * group, 3), pl.ds(swapped(core, part), HALF), :],
                              target.at[group, part], sems.at[group, part])
        for part in range(2)]) for group in range(3)]


def half_conv(band, weight, copies, bias, total):
    for down in range(3):
        wait_all(copies[down])

        def body(half, carry, down=down):
            at = half_rows(half)
            value = dot(tap_band(band, half, down), weight[down].reshape(6 * HALF, HALF))
            total[at, :] = value + (total[at, :] if down > 0 else bias)
            return carry

        lax.fori_loop(0, 2, body, 0)


def tap_copies(core, own_ref, peer_ref, all_ref, sems, group):
    lead = (pl.ds(3 * group, 3),)
    return weight_copies(core, own_ref, peer_ref, all_ref, sems.at[group], lead)


def weight_copies(core, own_ref, peer_ref, all_ref, sems, lead):
    copies = []
    for local in range(2):
        source = pl.ds(pl.multiple_of((core ^ local) * HALF, HALF), HALF)
        target = pl.ds(local * HALF, HALF)
        for which, ref in enumerate((own_ref, peer_ref)):
            held = pl.ds(which * HALF, HALF)
            if own_ref.shape[-1] == HALF:
                src, dst = (source, slice(None)), (target, held)
            else:
                src, dst = (slice(None), source), (held, target)
            copies.append(
                pltpu.make_async_copy(
                    ref.at[lead + src], all_ref.at[lead + dst], sems.at[2 * local + which]
                )
            )
    return copies


def params(limit):
    return pltpu.CompilerParams(vmem_limit_bytes=limit * MB)


def cost(micros):
    return pl.CostEstimate(flops=int(micros * 1.1e9), bytes_accessed=1 << 20, transcendentals=0)


def shape(rows, columns, dtype):
    return jax.ShapeDtypeStruct((rows, columns), dtype)


def in_hbm(*arrays):
    return [pltpu.with_memory_space_constraint(array, pltpu.HBM) for array in arrays]


def fetch(source, target, sem):
    copy = pltpu.make_async_copy(source, target, sem)
    copy.start()
    return copy


def both_rows(own_ref, peer_ref, row):
    return jnp.concatenate([own_ref[at_row(row), :], peer_ref[at_row(row), :]], 1).astype(F32)


def front_kernel(core_ref, eq_ref, x_hbm, xp_hbm, w_hbm, vec_ref, peer_ref, act_own_hbm, act_peer_hbm, stat_own, stat_peer, band,
                 conv_hbm, next_ref, stat2_ref, x_own, x_peer, act_own, act_peer, weight, total, sems):
    core = core_ref[0]
    first = fetch(x_hbm.at[core], x_own, sems.at[3, 0])
    second = fetch(xp_hbm.at[core], x_peer, sems.at[3, 1])
    copies = half_copies(core, w_hbm, weight, sems)
    first.wait()
    norm_forward(lambda row: x_own[at_row(row), :].astype(F32), (act_own,), stat_own, eq_ref,
                 vec_ref[0:1, :], vec_ref[1:2, :], swish)
    second.wait()
    norm_forward(lambda row: x_peer[at_row(row), :].astype(F32), (act_peer,), stat_peer, eq_ref,
                 peer_ref[0:1, :], peer_ref[1:2, :], swish)
    stores = [fetch(act_own, act_own_hbm, sems.at[4, 0]), fetch(act_peer, act_peer_hbm, sems.at[4, 1])]
    fill_bands(band, lambda row: both_rows(act_own, act_peer, row), eq_ref, parts_apart)
    half_conv(band, weight, copies, vec_ref[2:3, :], total)
    stores.append(fetch(total, conv_hbm, sems.at[3, 0]))
    norm_forward(lambda row: total[at_row(row), :], (next_ref,), stat2_ref, eq_ref, vec_ref[3:4, :],
                 vec_ref[4:5, :], swish)
    wait_all(stores)


def front_peer_kernel(core_ref, eq_ref, band, w_hbm, vec_ref, conv_hbm, next_ref, stat2_ref, weight,
                      total, sems):
    copies = half_copies(core_ref[0], w_hbm, weight, sems)
    half_conv(band, weight, copies, vec_ref[2:3, :], total)
    store = fetch(total, conv_hbm, sems.at[3, 0])
    norm_forward(lambda row: total[at_row(row), :], (next_ref,), stat2_ref, eq_ref, vec_ref[3:4, :],
                 vec_ref[4:5, :], swish)
    store.wait()


def front_call(core, eq, pixels, pixels_peer, weight, own_vectors, peer_vectors):
    half = pltpu.HBM((PIX, HALF), BF)
    return pl.pallas_call(
        front_kernel,
        out_shape=(half, half, shape(8, HALF, F32), shape(8, HALF, F32),
                   pltpu.VMEM((2, BAND, 3 * C), BF), pltpu.HBM((PIX, HALF), F32),
                   shape(PIX, HALF, BF), shape(8, HALF, F32)),
        in_specs=[SM, SM, HBM, HBM, HBM, VM, VM],
        out_specs=(HBM, HBM, VM, VM, VM, HBM, VM, VM),
        scratch_shapes=[pltpu.VMEM((PIX, HALF), BF)] * 4
        + [pltpu.VMEM((3, 2, 3, HALF, HALF), BF), pltpu.VMEM((PIX, HALF), F32),
           pltpu.SemaphoreType.DMA((5, 2))],
        name="front", compiler_params=params(14), cost_estimate=cost(9),
    )(core, eq, *in_hbm(pixels, pixels_peer, weight), own_vectors, peer_vectors)


def front_peer_call(core, eq, band, weight, vec):
    return pl.pallas_call(
        front_peer_kernel,
        out_shape=(pltpu.HBM((PIX, HALF), F32), shape(PIX, HALF, BF), shape(8, HALF, F32)),
        in_specs=[SM, SM, VM, HBM, VM], out_specs=(HBM, VM, VM),
        scratch_shapes=[pltpu.VMEM((3, 2, 3, HALF, HALF), BF), pltpu.VMEM((PIX, HALF), F32),
                        pltpu.SemaphoreType.DMA((4, 2))],
        name="front_peer", compiler_params=params(14), cost_estimate=cost(5),
    )(core, eq, band, *in_hbm(weight), vec)


def attn_kernel(core_ref, eq_ref, act_own, act_peer, own_ref, peer_ref, x_ref, xp_ref, g_own, g_peer,
                wq_o, wq_p, wk_o, wk_p, wv_o, wv_p, wp_o, wp_p, vec_ref, out_own, out_peer, gmid_hbm,
                gconv_ref, small_ref, dquery, dkey, dvalue, mixed, normed_ref, weight, gfull, query,
                keys, values, gmixed, probs, gscores, gnormed, mid_ref, taps, band, x_own, x_peer,
                stat_ref, sems):
    core = core_ref[0]
    groups = [tap_copies(core, own_ref, peer_ref, taps, sems.at[5:8], down) for down in range(3)]
    start_all(groups[0])
    extra = [fetch(x_ref.at[core], x_own, sems.at[4, 2]), fetch(xp_ref.at[core], x_peer, sems.at[4, 3])]
    fill_bands(band, lambda row: both_rows(act_own, act_peer, row), eq_ref)
    start_all(groups[1])
    start_all(groups[2])
    wait_all(extra)
    for down in range(3):
        wait_all(groups[down])
        if down == 0:
            copies = []
            for index, (own, peer) in enumerate(
                    ((wq_o, wq_p), (wk_o, wk_p), (wv_o, wv_p), (wp_o, wp_p))):
                copies += start_all(
                    weight_copies(core, own, peer, weight.at[index], sems.at[index], ()))
            copies.append(fetch(g_own.at[core], gfull.at[:, 0:HALF], sems.at[4, 0]))
            copies.append(fetch(g_peer.at[core], gfull.at[:, HALF:C], sems.at[4, 1]))

        def conv(half, carry, down=down):
            at = half_rows(half)
            value = dot(tap_band(band, half, down),
                        taps[3 * down : 3 * down + 3].reshape(3 * C, C))
            if down > 0:
                value = value + mid_ref[at, :]
            else:
                value = value + vec_ref[5:6, :] + jnp.concatenate(
                    [x_own[at, :], x_peer[at, :]], 1).astype(F32)
            mid_ref[at, :] = value
            return carry

        lax.fori_loop(0, 2, conv, 0)
    norm_forward(lambda row: mid_ref[at_row(row), :], (normed_ref,), stat_ref, eq_ref,
                 vec_ref[6:7, :], vec_ref[7:8, :], lambda v: v)
    wait_all(copies)
    normed = normed_ref[...]
    query[...] = (dot(normed, weight[0]) + vec_ref[8:9, :]).astype(BF)
    keys[...] = dot(normed, weight[1]).astype(BF)
    values[...] = (dot(normed, weight[2]) + vec_ref[9:10, :]).astype(BF)
    gmixed[...] = dot_nt(gfull[...], weight[3]).astype(BF)

    rows = 512
    spot = lax.broadcasted_iota(jnp.int32, (1, PIX), 1)
    right = (spot & (SIDE - 1)) >= 16
    low = spot >= PIX // 2

    def block(index, carry):
        start = pl.multiple_of(index * rows, rows)
        at = pl.ds(start, rows)
        half = (start >= PIX // 2).astype(jnp.int32) * 2
        bias = []
        for side in range(2):
            base = (half + side) * 4
            row = jnp.where(low, jnp.where(right, eq_ref[base + 3], eq_ref[base + 2]),
                            jnp.where(right, eq_ref[base + 1], eq_ref[base]))
            bias.append(jnp.where(row > 0.5, 0.0, -1e30).reshape(1, 1, 1, PIX))
        bias = jnp.concatenate(bias, 1)
        scores = dot_nt(query[at, :], keys[...]) * (SCALE * LOG2E)
        scores = (scores.reshape(rows // SIDE, 2, 16, PIX) + bias).reshape(rows, PIX)
        expo = jnp.exp2(scores - jnp.max(scores, axis=1, keepdims=True))
        wide = expo * (1.0 / jnp.sum(expo, axis=1, keepdims=True))
        narrow = wide.astype(BF)
        probs[at, :] = narrow
        mixed[at, :] = dot(narrow, values[...]).astype(BF)
        gprobs = dot_nt(gmixed[at, :], values[...])
        delta = jnp.sum(wide * gprobs, axis=1, keepdims=True)
        grads = (wide * (gprobs - delta)).astype(BF)
        gscores[at, :] = grads
        dquery[at, :] = (dot(grads, keys[...]) * SCALE).astype(BF)
        return carry

    lax.fori_loop(0, PIX // rows, block, 0)

    def total(value):
        return jnp.sum(value.astype(F32), axis=0, keepdims=True)

    dkey[...] = (dot_tn(gscores[...], query[...]) * SCALE).astype(BF)
    dvalue[...] = dot_tn(probs[...], gmixed[...]).astype(BF)
    gnormed[...] = (dot_nt(dquery[...], weight[0]) + dot_nt(dkey[...], weight[1])
                    + dot_nt(dvalue[...], weight[2]))
    dbq, dbv, dbp = total(dquery[...]), total(dvalue[...]), total(gfull[...])

    out = mid_ref[...] + dot(mixed[...], weight[3]) + vec_ref[10:11, :]
    out_own[...] = out[:, :HALF]
    out_peer[...] = out[:, HALF:]

    def finish(row, change):
        grad = gfull[at_row(row), :].astype(F32) + change
        gnormed[at_row(row), :] = grad
        gconv_ref[at_row(row), :] = grad.astype(BF)

    dgain, dshift = norm_backward(
        lambda row: mid_ref[at_row(row), :], lambda row: gnormed[at_row(row), :], None, stat_ref,
        eq_ref, vec_ref[6:7, :], vec_ref[7:8, :], False, finish)
    store = fetch(gnormed, gmid_hbm, sems.at[4, 3])
    small_ref[...] = jnp.concatenate(
        [dgain, dshift, dbq, dbv, dbp, total(gconv_ref[...]), dbq, dbq], 0)
    store.wait()


def attn_call(core, eq, acts, own, peer, x, g, weights, vec):
    flat = [w for pair_of in weights for w in pair_of]
    return pl.pallas_call(
        attn_kernel,
        out_shape=(shape(PIX, HALF, F32), shape(PIX, HALF, F32), pltpu.HBM((PIX, C), F32),
                   shape(PIX, C, BF), shape(8, C, F32)) + (pltpu.VMEM((PIX, C), BF),) * 5,
        in_specs=[SM, SM, VM, VM] + [HBM] * 14 + [VM],
        out_specs=(VM, VM, HBM) + (VM,) * 7,
        scratch_shapes=[pltpu.VMEM((4, C, C), BF)] + [pltpu.VMEM((PIX, C), BF)] * 5
        + [pltpu.VMEM((PIX, PIX), BF)] * 2 + [pltpu.VMEM((PIX, C), F32)] * 2
        + [pltpu.VMEM((9, C, C), BF), pltpu.VMEM((2, BAND, 3 * C), BF)]
        + [pltpu.VMEM((PIX, HALF), BF)] * 2
        + [pltpu.VMEM((8, C), F32), pltpu.SemaphoreType.DMA((8, 4))],
        name="attention", compiler_params=params(40), cost_estimate=cost(28),
    )(core, eq, *acts, *in_hbm(own, peer, *x, *g, *flat), vec)


def attn_wgrad_kernel(core_ref, normed_ref, dquery, dkey, dvalue, mixed, g_own, g_peer, dw_own,
                      dw_peer, g_mine, g_back, sems):
    core = core_ref[0]
    copies = [fetch(g_own.at[core], g_mine, sems.at[0]), fetch(g_peer.at[core], g_back, sems.at[1])]
    normed = normed_ref[...]
    for index, ref in enumerate((dquery, dkey, dvalue)):
        full = dot_tn(normed, ref[...]).astype(BF)
        for local in range(2):
            target = pl.multiple_of(index * C + (core ^ local) * HALF, HALF)
            part = full[local * HALF : (local + 1) * HALF, :]
            dw_own[pl.ds(target, HALF), :] = part[:, :HALF]
            dw_peer[pl.ds(target, HALF), :] = part[:, HALF:]
    for copy in copies:
        copy.wait()
    for local, ref in enumerate((g_mine, g_back)):
        target = pl.multiple_of(3 * C + (core ^ local) * HALF, HALF)
        part = dot_tn(mixed[...], ref[...]).astype(BF)
        dw_own[pl.ds(target, HALF), :] = part[:HALF]
        dw_peer[pl.ds(target, HALF), :] = part[HALF:]


def attn_wgrad_call(core, normed, dquery, dkey, dvalue, mixed, g):
    return pl.pallas_call(
        attn_wgrad_kernel, out_shape=(shape(4 * C, HALF, BF),) * 2,
        in_specs=[SM] + [VM] * 5 + [HBM] * 2, out_specs=(VM, VM),
        scratch_shapes=[pltpu.VMEM((PIX, HALF), BF)] * 2 + [pltpu.SemaphoreType.DMA((2,))],
        name="attention_weights", compiler_params=params(6), cost_estimate=cost(3),
    )(core, normed, dquery, dkey, dvalue, mixed, *in_hbm(*g))


def fetch_all(sources, targets, sems):
    return [fetch(source, target, sems.at[index])
            for index, (source, target) in enumerate(zip(sources, targets))]


def wgrad2_kernel(core_ref, eq_ref, *refs):
    sources, (out_ref, act_mine, act_other, grad_mine, grad_other, band, band_other, sems) = (
        refs[:4], refs[4:])
    core = core_ref[0]
    copies = fetch_all(sources, (act_mine, act_other, grad_mine, grad_other), sems)
    copies[0].wait()
    fill_bands(band, lambda row: act_mine[at_row(row), :], eq_ref.at[0])
    copies[1].wait()
    fill_bands(band_other, lambda row: act_other[at_row(row), :], eq_ref.at[1])
    for copy in copies[2:]:
        copy.wait()

    def body(down, carry):
        for local in range(2):
            full = 0.0
            for half in range(2):
                rows = slice(half * (PIX // 2), (half + 1) * (PIX // 2))
                full = full + dot_tn(tap_band(band, half, down),
                                     grad_mine[rows, local * HALF : (local + 1) * HALF])
                full = full + dot_tn(tap_band(band_other, half, down),
                                     grad_other[rows, (1 - local) * HALF : (2 - local) * HALF])
            full = full.astype(BF)
            for index in range(3):
                base = (3 * down + index) * C + (core ^ local) * HALF
                out_ref[pl.ds(pl.multiple_of(base, HALF), HALF), :] = full[
                    index * HALF : (index + 1) * HALF]
        return carry

    lax.fori_loop(0, 3, body, 0)


def wgrad2_call(core, eqs, *arrays):
    return pl.pallas_call(
        wgrad2_kernel, out_shape=shape(9 * C, HALF, BF), in_specs=[SM, SM] + [HBM] * 4,
        out_specs=VM,
        scratch_shapes=[pltpu.VMEM((PIX, HALF), BF)] * 2 + [pltpu.VMEM((PIX, C), BF)] * 2
        + [pltpu.VMEM((2, BAND, 3 * HALF), BF)] * 2 + [pltpu.SemaphoreType.DMA((4,))],
        name="wgrad2", compiler_params=params(14), cost_estimate=cost(7),
    )(core, eqs, *in_hbm(*arrays))


TAPS = 6


def wgrad1_kernel(core_ref, eq_ref, *refs):
    sources, (out_ref, tail_ref, band, band_other, act, act2, grad_mine, grad_other, sems) = (
        refs[:6], refs[6:])
    core = core_ref[0]
    copies = fetch_all(sources, (grad_mine, grad_other, act.at[:, 0:HALF], act.at[:, HALF:C],
                                 act2.at[:, 0:HALF], act2.at[:, HALF:C]), sems)
    copies[0].wait()
    fill_bands(band, lambda row: grad_mine[at_row(row), :], eq_ref.at[0])
    copies[1].wait()
    fill_bands(band_other, lambda row: grad_other[at_row(row), :], eq_ref.at[1])
    for copy in copies[2:]:
        copy.wait()

    def group(down, out, base):
        full = 0.0
        for half in range(2):
            rows = slice(half * (PIX // 2), (half + 1) * (PIX // 2))
            full = full + dot_tn(act[rows, :], tap_band(band, half, down))
            full = full + dot_tn(act2[rows, :], tap_band(band_other, half, down))
        full = full.astype(BF)
        for index in range(3):
            for local in range(2):
                where = base + (2 - index) * C + (core ^ local) * HALF
                out[pl.ds(pl.multiple_of(where, HALF), HALF), :] = full[
                    local * HALF : (local + 1) * HALF, index * HALF : (index + 1) * HALF]

    group(0, tail_ref, 0)

    def body(down, carry):
        group(down, out_ref, (2 - down) * 3 * C)
        return carry

    lax.fori_loop(1, 3, body, 0)


def wgrad1_call(core, eqs, *arrays):
    return pl.pallas_call(
        wgrad1_kernel, out_shape=(shape(TAPS * C, HALF, BF), shape((9 - TAPS) * C, HALF, BF)),
        in_specs=[SM, SM] + [HBM] * 6, out_specs=(VM, VM),
        scratch_shapes=[pltpu.VMEM((2, BAND, 3 * HALF), BF)] * 2 + [pltpu.VMEM((PIX, C), BF)] * 2
        + [pltpu.VMEM((PIX, HALF), BF)] * 2 + [pltpu.SemaphoreType.DMA((6,))],
        name="wgrad1", compiler_params=params(16), cost_estimate=cost(7),
    )(core, eqs, *in_hbm(*arrays))


def dgrad_kernel(first, core_ref, eq_ref, own_ref, peer_ref, vec_ref, *refs):
    if first:
        (grad_own, grad_peer, stat_own, stat_peer, x_hbm, xp_hbm, gmid_hbm, out_own, out_peer, small_ref, weight, patch,
         total, stat_ref, sems, x_own, x_peer, gmid_ref) = refs
        load = lambda row: both_rows(x_own, x_peer, row)
        load_grad = lambda row: both_rows(grad_own, grad_peer, row)
        sources = (x_hbm.at[core_ref[0]], xp_hbm.at[core_ref[0]], gmid_hbm)
        held = (x_own, x_peer, gmid_ref)
        gain, shift = vec_ref[0:1, :], vec_ref[1:2, :]
    else:
        (grad_ref, stat_own, stat_peer, in_own, in_peer, out_own, out_peer, small_ref, weight, patch,
         total, stat_ref, sems, mine, back) = refs
        load = lambda row: both_rows(mine, back, row)
        load_grad = lambda row: grad_ref[at_row(row), :]
        sources, held = (in_own, in_peer), (mine, back)
        gain, shift = vec_ref[3:4, :], vec_ref[4:5, :]
    stat_ref[:, :HALF] = stat_own[...]
    stat_ref[:, HALF:] = stat_peer[...]
    copies = [tap_copies(core_ref[0], own_ref, peer_ref, weight, sems, 2 - down)
              for down in range(3)]
    for group in copies:
        for copy in group:
            copy.start()
    later = fetch_all(sources, held, sems.at[3])
    fill_bands(patch, load_grad, eq_ref)
    for down in range(3):
        for copy in copies[down]:
            copy.wait()

        def body(half, carry, down=down):
            value = total[half_rows(half), :] if down > 0 else 0.0
            for t in range(3):
                value = value + dot_nt(tap_band(patch, half, down)[:, t * C : (t + 1) * C],
                                       weight[8 - (3 * down + t)])
            total[half_rows(half), :] = value
            return carry

        lax.fori_loop(0, 2, body, 0)
    for copy in later:
        copy.wait()

    def finish(row, change):
        at = at_row(row)
        if first:
            change = change + gmid_ref[at, :]
        out_own[at, :] = change[:, :HALF].astype(out_own.dtype)
        out_peer[at, :] = change[:, HALF:].astype(out_peer.dtype)

    dgain, dshift = norm_backward(load, lambda row: total[at_row(row), :], total, stat_ref, eq_ref,
                                  gain, shift, True, finish)
    bias = [jnp.sum(ref[...].astype(F32), axis=0, keepdims=True) for ref in (out_own, out_peer)]
    bias = jnp.concatenate(bias, 1)
    small_ref[...] = jnp.concatenate([dgain, dshift, bias] + [dgain] * 5, 0)


def dgrad_call(core, eq, grad, own, peer, vec, stats, source, gmid=None):
    first = gmid is not None
    extra = (*source, gmid) if first else source
    held = [pltpu.VMEM((PIX, HALF), BF if first else F32)] * 2
    held += [pltpu.VMEM((PIX, C), F32)] if first else []
    outs = (shape(PIX, HALF, F32 if first else BF),) * 2
    return pl.pallas_call(
        functools.partial(dgrad_kernel, first),
        out_shape=outs + (shape(8, C, F32),),
        in_specs=[SM, SM, HBM, HBM, VM] + [VM] * (len(grad) + len(stats)) + [HBM] * len(extra),
        out_specs=(VM,) * 3,
        scratch_shapes=[pltpu.VMEM((9, C, C), BF), pltpu.VMEM((2, BAND, 3 * C), BF),
                        pltpu.VMEM((PIX, C), F32), pltpu.VMEM((8, C), F32),
                        pltpu.SemaphoreType.DMA((4, 4))] + held,
        name="dgrad1" if first else "dgrad2", compiler_params=params(16), cost_estimate=cost(10),
    )(core, eq, *in_hbm(own, peer), vec, *grad, *stats, *in_hbm(*extra))


EVERY, TIED, SMALL_FROM = "asrf", 9, 0
ORDERS = {
    "second": ((2, 0, 1), (0, 1, 2)),
    "attn": ((1, 2, 0), (1, 2, 0)),
    "first": ((2, 0, 1), (0, 1, 2)),
    "rest": ((1, 2, 0), (1, 2, 0)),
}


def orders_of(kind, size):
    bits = size.bit_length() - 1
    return [[*order, *range(3, bits)] for order in ORDERS[kind]]


def exchange(array, orders, stage, size):
    moves = [((d, c), (d ^ (1 << orders[c][stage]), c)) for d in range(size) for c in range(2)]
    return lax.ppermute(array, ("dp", "chan"), [(a[0] * 2 + a[1], b[0] * 2 + b[1]) for a, b in moves])


def side_of(orders, stage):
    bit = jnp.where(lax.axis_index("chan") == 0, orders[0][stage], orders[1][stage])
    return (lax.axis_index("dp") >> bit) & 1


def side_base(orders):
    base = 0
    for stage in range(len(orders[0])):
        base = base * 2 + side_of(orders, stage)
    return base


class Chain:
    def __init__(self, part, kind, size):
        self.value, self.size, self.orders, self.step = part, size, orders_of(kind, size), 0
        self.stages, self.rows = len(self.orders[0]), part.shape[0]

    def advance(self):
        stage = self.step if self.step < self.stages else 2 * self.stages - 1 - self.step
        if self.step < self.stages:
            half = self.value.shape[0] // 2
            side = side_of(self.orders, stage)
            send = lax.dynamic_slice_in_dim(self.value, (1 - side) * half, half, 0)
            keep = lax.dynamic_slice_in_dim(self.value, side * half, half, 0)
            self.value = keep + exchange(send, self.orders, stage, self.size)
        else:
            back = exchange(self.value, self.orders, stage, self.size)
            self.value = jnp.concatenate([self.value, back], 0) if stage > 0 else (self.value, back)
        self.step += 1


def together(chains, *values):
    held = lax.optimization_barrier(([c.value for c in chains], values))
    for chain, value in zip(chains, held[0]):
        chain.value = value
    return held[1]


def after(value, *others):
    return lax.optimization_barrier((value, *others))[0]


def spread_kernel(plan, base_ref, *refs):
    count = len(plan)
    ins, out_hbm, wide, sems = refs[:count], refs[-2 * count - 1], refs[-2 * count : -count], refs[-count:]
    copies = []
    for index, (start, first, rows) in enumerate(plan):
        wide[index][...] = ins[index][...].astype(F32)
        for block in range(ins[index].shape[0] // rows):
            row = start + ((block + first) ^ base_ref[index]) * rows
            copies.append(fetch(
                wide[index].at[block * rows : (block + 1) * rows, :],
                out_hbm.at[pl.ds(pl.multiple_of(row, rows & -rows), rows), :],
                sems[index].at[block]))
    wait_all(copies)


def spread(parts, rows, token, into=None):
    plan = [(start, first, chain.rows // chain.size) for _, chain, start, first in parts]
    arrays = [part[0] for part in parts]
    base = jnp.stack([side_base(part[1].orders) for part in parts]).astype(jnp.int32)
    held = () if into is None else (into,)
    return pl.pallas_call(
        functools.partial(spread_kernel, plan), out_shape=pltpu.HBM((rows, HALF), F32),
        in_specs=[SM] + [VM] * len(arrays) + [HBM] * len(held), out_specs=HBM,
        input_output_aliases={} if into is None else {1 + len(arrays): 0},
        scratch_shapes=[pltpu.VMEM(array.shape, F32) for array in arrays]
        + [pltpu.SemaphoreType.DMA((array.shape[0] // one[2],)) for array, one in zip(arrays, plan)],
        compiler_params=params(14), name="spread", cost_estimate=cost(2),
    )(after(base, token), *arrays, *held)


def second_target(row):
    return 0, row // C * HALF + row % HALF, slice(row // HALF % 2 * HALF, (row // HALF % 2 + 1) * HALF)


def attn_target(row):
    if row < 3 * C:
        return row // C, row % C, slice(0, HALF)
    row -= 3 * C
    return 3, row % HALF, slice(row // HALF * HALF, (row // HALF + 1) * HALF)


def place_kernel(size, targets, base_ref, *refs):
    ins, outs, held = refs[: 2 * len(targets)], refs[2 * len(targets) : -1], refs[-1]
    start = 0
    for index, target in enumerate(targets):
        part, part2 = ins[2 * index : 2 * index + 2]
        half = part.shape[0]
        held[start : start + half, :] = part[...]
        held[start + half : start + 2 * half, :] = part2[...]
        rows = 2 * half // size
        piece = math.gcd(rows, HALF)
        for row in range(0, 2 * half, piece):
            source = ((row // rows) ^ base_ref[index]) * rows + row % rows + start
            which, at, columns = target(row)
            outs[which][at : at + piece, columns] = held[
                pl.ds(pl.multiple_of(source, piece), piece), :].astype(F32)
        start += 2 * half


def place(chains, targets, shapes, token):
    parts = [part for chain in chains for part in chain.value]
    rows = sum(part.shape[0] for part in parts)
    base = jnp.stack([side_base(chain.orders) for chain in chains]).astype(jnp.int32)
    return pl.pallas_call(
        functools.partial(place_kernel, chains[0].size, targets),
        out_shape=tuple(shape(*one, F32) for one in shapes), in_specs=[SM] + [VM] * len(parts),
        out_specs=(VM,) * len(shapes), scratch_shapes=[pltpu.VMEM((rows, HALF), BF)],
        compiler_params=params(12), name="place", cost_estimate=cost(2),
    )(after(base, token), *parts)


def swap(array):
    return lax.ppermute(array, "chan", [(0, 1), (1, 0)])


def shards(pixels, tile_ids, first_gain, first_shift, first_conv, first_bias, second_gain,
           second_shift, second_conv, second_bias, attn_gain, attn_shift, query_weight,
           query_bias, key_weight, value_weight, value_bias, proj_weight, proj_bias, cotangent,
           *, size):
    index = lax.axis_index("chan")
    core = index.reshape(1).astype(jnp.int32)
    tiles = tile_ids.reshape(2, 2, 16, 2, 16)[:, :, 0, :, 0].reshape(2, 4)
    eqs = (tiles[:, :, None] == tiles[:, None, :]).astype(F32).reshape(2, 16)
    eqs = jnp.where(index == 0, eqs, eqs[::-1])
    own_vectors = jnp.stack([first_gain, first_shift, first_bias, second_gain, second_shift,
                             second_bias, attn_gain, attn_shift, query_bias, value_bias, proj_bias])
    pixels_peer = swap(pixels)
    pixels_peer, own_vectors, eqs = lax.optimization_barrier((pixels_peer, own_vectors, eqs))
    eq = eqs[0]
    peer_vectors = swap(own_vectors)
    first_conv, peer_vectors, pixels_peer = lax.optimization_barrier(
        (first_conv, peer_vectors, pixels_peer))
    first_peer = swap(first_conv)
    weights = lax.optimization_barrier(
        (query_weight, key_weight, value_weight, proj_weight, peer_vectors))[:4]
    weights_peer = [swap(array) for array in weights]
    vectors = jnp.concatenate([own_vectors, peer_vectors], 1)
    x = (pixels, pixels_peer)
    act_own, act_peer, stat_own, stat_peer, band, conv1_own, act2_own, stat2_own = front_call(
        core, eq, *x, first_conv, own_vectors, peer_vectors)
    first_peer, act2_own, act_own, act_peer, second_conv, cotangent, *weights_peer = (
        lax.optimization_barrier((first_peer, act2_own, act_own, act_peer, second_conv, cotangent,
                                  *weights_peer)))
    second_peer, g_peer = swap(second_conv), swap(cotangent)
    act_other = (swap(act_peer), swap(act_own))
    conv1_peer, act2_peer, stat2_peer = front_peer_call(core, eq, band, first_peer, peer_vectors)
    act2_peer, second_peer, g_peer = lax.optimization_barrier((act2_peer, second_peer, g_peer))
    g = (cotangent, g_peer)
    act2_other = swap(act2_peer)
    out_own, out_peer, gmid, gconv2, small3, *parts, normed = attn_call(
        core, eq, (act2_own, act2_peer), second_conv, second_peer, x, g,
        list(zip(weights, weights_peer)), vectors)
    gconv2, act2_other, *act_other = lax.optimization_barrier((gconv2, act2_other, *act_other))
    gconv2_other = swap(gconv2)
    dattn, dattn_peer = attn_wgrad_call(core, normed, *parts, g)
    dattn, gconv2, gconv2_other = lax.optimization_barrier((dattn, gconv2, gconv2_other))
    attn_other = swap(dattn_peer)
    part = wgrad2_call(core, eqs, act2_own, act2_other, gconv2, gconv2_other)
    attn_other, part = lax.optimization_barrier((attn_other, part))
    second, attn_sum = Chain(part, "second", size), Chain(dattn + attn_other, "attn", size)
    (gconv2,) = together([second, attn_sum], gconv2)

    for chain in (attn_sum, second):
        chain.advance()
    gconv1_own, gconv1_peer, small2 = dgrad_call(
        core, eq, (gconv2,), second_conv, second_peer, vectors, (stat2_own, stat2_peer),
        (conv1_own, conv1_peer))
    gconv1_other = swap(gconv1_peer)
    gconv1_own, gconv1_other = together([second, attn_sum], gconv1_own, gconv1_other)

    for chain in (attn_sum, second):
        chain.advance()
    part, tail = wgrad1_call(core, eqs, gconv1_own, gconv1_other, act_own, act_peer, *act_other)
    first, rest = Chain(part, "first", size), Chain(tail, "rest", size)
    (gconv1_own,) = together([second, attn_sum, first, rest], gconv1_own)

    known = {"a": attn_sum, "s": second, "r": rest, "f": first}
    every = [known[name] for name in EVERY]
    for chain in every:
        chain.advance()
    pix_own, pix_peer, small1 = dgrad_call(core, eq, (gconv1_own, gconv1_peer), first_conv,
                                           first_peer, vectors, (stat_own, stat_peer), x, gmid)
    small = jnp.concatenate([small1, small2, small3], 0)
    pix_peer, out_peer, small = together(every, pix_peer, out_peer, small)

    small = small[:, :HALF] + swap(small[:, HALF:])
    pix_back = swap(pix_peer)
    out_back = swap(out_peer)
    bits = size.bit_length() - 1
    turn, bit = 0, 0
    token = core
    while any(chain.step < 2 * bits for chain in every):
        for chain in every:
            if chain.step < 2 * bits:
                chain.advance()
                if turn < TIED:
                    (token,) = together([chain], token)
        if turn >= SMALL_FROM and bit < bits:
            small = small + lax.ppermute(
                small, "dp", [(i, i ^ (1 << bit)) for i in range(size)])
            small, token = lax.optimization_barrier((small, token))
            bit += 1
        turn += 1
    (sums2,) = place([second], [second_target], [(9 * HALF, C)], core)
    sums3 = place([attn_sum], [attn_target], [(C, HALF), (C, HALF), (C, HALF), (HALF, C)], core)
    mine, back = first.value
    half = size // 2
    sums1 = spread([(rest.value[0], rest, TAPS * C, 0), (mine, first, 0, 0)], 9 * C, core)
    sums1 = spread([(rest.value[1], rest, TAPS * C, half), (back, first, 0, half)], 9 * C, token, sums1)

    def unboth(own, back):
        return jnp.where(index == 0, jnp.stack([own, back]), jnp.stack([back, own]))

    return (
        unboth(out_own, out_back), unboth(pix_own, pix_back), small[0], small[1],
        sums1.reshape(9, C, HALF), small[10], small[8], small[9], sums2.reshape(9, HALF, C),
        small[21], small[16], small[17], sums3[0], small[18], sums3[1], sums3[2], small[19],
        sums3[3], small[20],
    )


def solution(mesh):
    chan = P("chan")
    rows = P("dp", None, "chan")
    return jax.shard_map(
        functools.partial(shards, size=mesh.shape["dp"]),
        mesh=mesh,
        in_specs=(
            rows, P("dp", None), chan, chan, P(None, None, "chan"), chan, chan, chan,
            P(None, "chan", None), chan, chan, chan, P(None, "chan"), chan, P(None, "chan"),
            P(None, "chan"), chan, P("chan", None), chan, rows,
        ),
        out_specs=(
            rows, rows, chan, chan, P(None, None, "chan"), chan, chan, chan,
            P(None, "chan", None), chan, chan, chan, P(None, "chan"), chan, P(None, "chan"),
            P(None, "chan"), chan, P("chan", None), chan,
        ),
        check_vma=False,
    )
```

```python
import functools
import math
import jax
import jax.numpy as jnp
from jax import lax
from jax.experimental import pallas as pl
from jax.experimental.pallas import tpu as pltpu
from jax.sharding import PartitionSpec as P

C = 512
HALF = 256
GROUP = 16
SIDE = 32
PIX = 1024
EPSILON = 1e-06
BF = jnp.bfloat16
F32 = jnp.float32
MB = 1024 * 1024
VM = pl.BlockSpec(memory_space=pltpu.VMEM)
SM = pl.BlockSpec(memory_space=pltpu.SMEM)
HBM = pl.BlockSpec(memory_space=pltpu.HBM)
SCALE = C ** (-0.5)
LOG2E = 1.4426950408889634


def dot(first, second):
    return jnp.dot(first, second, preferred_element_type=F32)


def dot_nt(first, second):
    return lax.dot_general(first, second, (((1,), (1,)), ((), ())), preferred_element_type=F32)


def dot_tn(first, second):
    return lax.dot_general(first, second, (((0,), (0,)), ((), ())), preferred_element_type=F32)


def at_row(row):
    return pl.ds(pl.multiple_of(row * SIDE, SIDE), SIDE)


def group_sums(rows):
    full = jnp.concatenate(rows, 0)
    width = full.shape[1]
    lane = lax.broadcasted_iota(jnp.int32, full.shape, 1)
    for step in (1, 2, 4, 8):
        full = full + jnp.where(
            (lane & step) == 0, pltpu.roll(full, width - step, 1), pltpu.roll(full, step, 1)
        )
    return [full[i : i + 1] for i in range(len(rows))]


def image_means(sums, eq_ref):
    rows = []
    for i in range(4):
        total, count = 0.0, 0.0
        for j in range(4):
            total = total + eq_ref[4 * i + j] * sums[j]
            count = count + eq_ref[4 * i + j]
        rows.append(total / (count * float(256 * GROUP)))
    return group_sums(rows)


def tiles_of(rows):
    return rows.reshape(2, 16, rows.shape[-1])


def pair(rows, top):
    return jnp.concatenate([rows[2 * top + side].reshape(1, 1, -1) for side in range(2)], 0)


def over_canvas(step, count, width=C, unroll=2):
    found = [[] for _ in range(count)]
    for top in range(2):
        zero = tuple(jnp.zeros((2, 16, width), F32) for _ in range(count))

        def body(index, carry, top=top):
            return tuple(a + b for a, b in zip(carry, step(top, top * 16 + index)))

        totals = lax.fori_loop(0, 16, body, zero, unroll=unroll)
        for n in range(count):
            columns = jnp.sum(totals[n], axis=1)
            found[n] += [columns[0:1], columns[1:2]]
    return found


def for_rows(step, unroll=2):
    for top in range(2):

        def body(index, carry, top=top):
            step(top, top * 16 + index)
            return carry

        lax.fori_loop(0, 16, body, 0, unroll=unroll)


def norm_stats(load, eq_ref, width):
    (sums,) = over_canvas(lambda top, row: (tiles_of(load(row)),), 1, width)
    means = image_means(sums, eq_ref)
    centers = [pair(means, top) for top in range(2)]

    def square(top, row):
        off = tiles_of(load(row)) - centers[top]
        return (off * off,)

    (squares,) = over_canvas(square, 1, width)
    rstds = [lax.rsqrt(v + EPSILON) for v in image_means(squares, eq_ref)]
    return means, rstds


def swish(value):
    half = 0.5 * value
    return half + half * jnp.tanh(half)


def norm_forward(load, out_refs, stat_ref, eq_ref, gain, shift, act):
    width = gain.shape[-1]
    means, rstds = norm_stats(load, eq_ref, width)
    stat_ref[...] = jnp.concatenate(means + rstds, 0)
    centers = [pair(means, top) for top in range(2)]
    slopes = [pair([r * gain for r in rstds], top) for top in range(2)]
    offset = shift.reshape(1, 1, width)

    def step(top, row):
        value = (tiles_of(load(row)) - centers[top]) * slopes[top] + offset
        value = act(value).reshape(SIDE, width).astype(BF)
        held = width // len(out_refs)
        for index, ref in enumerate(out_refs):
            ref[at_row(row), :] = value[:, index * held : (index + 1) * held]

    for_rows(step)


def norm_backward(load, load_grad, keep_ref, stat_ref, eq_ref, gain, shift, with_swish, finish):
    stats = stat_ref[...]
    means = [stats[i : i + 1] for i in range(4)]
    rstds = [stats[4 + i : 5 + i] for i in range(4)]
    centers = [pair(means, top) for top in range(2)]
    rates = [pair(rstds, top) for top in range(2)]
    scale, offset = gain.reshape(1, 1, C), shift.reshape(1, 1, C)

    def first(top, row):
        unit = (tiles_of(load(row)) - centers[top]) * rates[top]
        grad = tiles_of(load_grad(row))
        if with_swish:
            value = unit * scale + offset
            gate = 0.5 + 0.5 * jnp.tanh(0.5 * value)
            grad = grad * (gate * (1.0 + value * (1.0 - gate)))
            keep_ref[at_row(row), :] = grad.reshape(SIDE, C)
        return grad, grad * unit

    plain, scaled = over_canvas(first, 2)
    mean_plain = image_means([p * gain for p in plain], eq_ref)
    mean_scaled = image_means([s * gain for s in scaled], eq_ref)
    first_means = [pair(mean_plain, top) for top in range(2)]
    second_means = [pair(mean_scaled, top) for top in range(2)]

    def second(top, row):
        unit = (tiles_of(load(row)) - centers[top]) * rates[top]
        grad = tiles_of(keep_ref[at_row(row), :] if with_swish else load_grad(row))
        change = rates[top] * (grad * scale - first_means[top] - unit * second_means[top])
        finish(row, change.reshape(SIDE, C))

    for_rows(second)
    return sum(scaled), sum(plain)


BAND = PIX // 2 + 2 * SIDE


def row_mask(eq_ref, target, source, right):
    column = lax.broadcasted_iota(jnp.int32, (SIDE, 128), 0)

    def eq(side, other):
        return eq_ref[(2 * target + side) * 4 + 2 * source + other]

    if right == 0:
        mask = jnp.where(column < 16, eq(0, 0), eq(1, 1))
    elif right < 0:
        mask = jnp.where(column < 16, eq(0, 0), jnp.where(column == 16, eq(1, 0), eq(1, 1)))
        mask = jnp.where(column == 0, 0.0, mask)
    else:
        mask = jnp.where(column < 15, eq(0, 0), jnp.where(column == 15, eq(0, 1), eq(1, 1)))
        mask = jnp.where(column == SIDE - 1, 0.0, mask)
    return mask.astype(BF)


def fill_bands(band_ref, load, eq_ref, columns=None):
    width = band_ref.shape[2] // 3

    def put(half, place, value, masks):
        moved = [pltpu.roll(value, 1, 0), value, pltpu.roll(value, SIDE - 1, 0)]
        for index in range(3):
            part = moved[index].astype(BF)
            if masks[index] is not None:
                part = part * jnp.concatenate([masks[index]] * (width // 128), 1)
            if columns is None:
                band_ref[half, at_row(place), index * width : (index + 1) * width] = part
            else:
                for number in range(width // HALF):
                    where = pl.ds(columns(index, number), HALF)
                    band_ref[half, at_row(place), where] = part[
                        :, number * HALF : (number + 1) * HALF]

    for half in range(2):
        inner = [row_mask(eq_ref, half, half, -1), None, row_mask(eq_ref, half, half, 1)]

        def body(index, carry, half=half, inner=inner):
            put(half, index + 1, load(half * 16 + index).astype(F32), inner)
            return carry

        lax.fori_loop(0, 16, body, 0, unroll=2)
        across = [row_mask(eq_ref, half, 1 - half, right) for right in (-1, 0, 1)]
        put(half, 17 - 17 * half, load(16 - half).astype(F32), across)
        band_ref[half, 17 * half * SIDE : (17 * half + 1) * SIDE, :] = jnp.zeros(
            (SIDE, 3 * width), BF)


def half_rows(half):
    return pl.ds(pl.multiple_of(half * (PIX // 2), PIX // 2), PIX // 2)


def tap_band(band_ref, half, down):
    if isinstance(down, int):
        return band_ref[half, down * SIDE : down * SIDE + PIX // 2, :]
    return band_ref[half, pl.ds(pl.multiple_of(down * SIDE, SIDE), PIX // 2), :]


def parts_apart(index, number):
    return number * 3 * HALF + index * HALF


def swapped(core, number):
    return pl.multiple_of((core ^ number) * HALF, HALF)


def start_all(copies):
    for copy in copies:
        copy.start()
    return copies


def wait_all(copies):
    for copy in copies:
        copy.wait()


def half_copies(core, source, target, sems):
    return [start_all([
        pltpu.make_async_copy(source.at[pl.ds(3 * group, 3), pl.ds(swapped(core, part), HALF), :],
                              target.at[group, part], sems.at[group, part])
        for part in range(2)]) for group in range(3)]


def half_conv(band, weight, copies, bias, total):
    for down in range(3):
        wait_all(copies[down])

        def body(half, carry, down=down):
            at = half_rows(half)
            value = dot(tap_band(band, half, down), weight[down].reshape(6 * HALF, HALF))
            total[at, :] = value + (total[at, :] if down > 0 else bias)
            return carry

        lax.fori_loop(0, 2, body, 0)


def tap_copies(core, own_ref, peer_ref, all_ref, sems, group):
    lead = (pl.ds(3 * group, 3),)
    return weight_copies(core, own_ref, peer_ref, all_ref, sems.at[group], lead)


def weight_copies(core, own_ref, peer_ref, all_ref, sems, lead):
    copies = []
    for local in range(2):
        source = pl.ds(pl.multiple_of((core ^ local) * HALF, HALF), HALF)
        target = pl.ds(local * HALF, HALF)
        for which, ref in enumerate((own_ref, peer_ref)):
            held = pl.ds(which * HALF, HALF)
            if own_ref.shape[-1] == HALF:
                src, dst = (source, slice(None)), (target, held)
            else:
                src, dst = (slice(None), source), (held, target)
            copies.append(
                pltpu.make_async_copy(
                    ref.at[lead + src], all_ref.at[lead + dst], sems.at[2 * local + which]
                )
            )
    return copies


def params(limit):
    return pltpu.CompilerParams(vmem_limit_bytes=limit * MB)


def cost(micros):
    return pl.CostEstimate(flops=int(micros * 1.1e9), bytes_accessed=1 << 20, transcendentals=0)


def shape(rows, columns, dtype):
    return jax.ShapeDtypeStruct((rows, columns), dtype)


def in_hbm(*arrays):
    return [pltpu.with_memory_space_constraint(array, pltpu.HBM) for array in arrays]


def fetch(source, target, sem):
    copy = pltpu.make_async_copy(source, target, sem)
    copy.start()
    return copy


def both_rows(own_ref, peer_ref, row):
    return jnp.concatenate([own_ref[at_row(row), :], peer_ref[at_row(row), :]], 1).astype(F32)


def front_kernel(core_ref, eq_ref, x_hbm, xp_hbm, w_hbm, vec_ref, peer_ref, act_own_hbm, act_peer_hbm, stat_own, stat_peer, band,
                 conv_hbm, next_ref, stat2_ref, x_own, x_peer, act_own, act_peer, weight, total, sems):
    core = core_ref[0]
    first = fetch(x_hbm.at[core], x_own, sems.at[3, 0])
    second = fetch(xp_hbm.at[core], x_peer, sems.at[3, 1])
    copies = half_copies(core, w_hbm, weight, sems)
    first.wait()
    norm_forward(lambda row: x_own[at_row(row), :].astype(F32), (act_own,), stat_own, eq_ref,
                 vec_ref[0:1, :], vec_ref[1:2, :], swish)
    second.wait()
    norm_forward(lambda row: x_peer[at_row(row), :].astype(F32), (act_peer,), stat_peer, eq_ref,
                 peer_ref[0:1, :], peer_ref[1:2, :], swish)
    stores = [fetch(act_own, act_own_hbm, sems.at[4, 0]), fetch(act_peer, act_peer_hbm, sems.at[4, 1])]
    fill_bands(band, lambda row: both_rows(act_own, act_peer, row), eq_ref, parts_apart)
    half_conv(band, weight, copies, vec_ref[2:3, :], total)
    stores.append(fetch(total, conv_hbm, sems.at[3, 0]))
    norm_forward(lambda row: total[at_row(row), :], (next_ref,), stat2_ref, eq_ref, vec_ref[3:4, :],
                 vec_ref[4:5, :], swish)
    wait_all(stores)


def front_peer_kernel(core_ref, eq_ref, band, w_hbm, vec_ref, conv_hbm, next_ref, stat2_ref, weight,
                      total, sems):
    copies = half_copies(core_ref[0], w_hbm, weight, sems)
    half_conv(band, weight, copies, vec_ref[2:3, :], total)
    store = fetch(total, conv_hbm, sems.at[3, 0])
    norm_forward(lambda row: total[at_row(row), :], (next_ref,), stat2_ref, eq_ref, vec_ref[3:4, :],
                 vec_ref[4:5, :], swish)
    store.wait()


def front_call(core, eq, pixels, pixels_peer, weight, own_vectors, peer_vectors):
    half = pltpu.HBM((PIX, HALF), BF)
    return pl.pallas_call(
        front_kernel,
        out_shape=(half, half, shape(8, HALF, F32), shape(8, HALF, F32),
                   pltpu.VMEM((2, BAND, 3 * C), BF), pltpu.HBM((PIX, HALF), F32),
                   shape(PIX, HALF, BF), shape(8, HALF, F32)),
        in_specs=[SM, SM, HBM, HBM, HBM, VM, VM],
        out_specs=(HBM, HBM, VM, VM, VM, HBM, VM, VM),
        scratch_shapes=[pltpu.VMEM((PIX, HALF), BF)] * 4
        + [pltpu.VMEM((3, 2, 3, HALF, HALF), BF), pltpu.VMEM((PIX, HALF), F32),
           pltpu.SemaphoreType.DMA((5, 2))],
        name="front", compiler_params=params(14), cost_estimate=cost(9),
    )(core, eq, *in_hbm(pixels, pixels_peer, weight), own_vectors, peer_vectors)


def front_peer_call(core, eq, band, weight, vec):
    return pl.pallas_call(
        front_peer_kernel,
        out_shape=(pltpu.HBM((PIX, HALF), F32), shape(PIX, HALF, BF), shape(8, HALF, F32)),
        in_specs=[SM, SM, VM, HBM, VM], out_specs=(HBM, VM, VM),
        scratch_shapes=[pltpu.VMEM((3, 2, 3, HALF, HALF), BF), pltpu.VMEM((PIX, HALF), F32),
                        pltpu.SemaphoreType.DMA((4, 2))],
        name="front_peer", compiler_params=params(14), cost_estimate=cost(5),
    )(core, eq, band, *in_hbm(weight), vec)


def attn_kernel(core_ref, eq_ref, act_own, act_peer, own_ref, peer_ref, x_ref, xp_ref, g_own, g_peer,
                wq_o, wq_p, wk_o, wk_p, wv_o, wv_p, wp_o, wp_p, vec_ref, out_own, out_peer, gmid_hbm,
                gconv_ref, small_ref, dquery, dkey, dvalue, mixed, normed_ref, weight, gfull, query,
                keys, values, gmixed, probs, gscores, gnormed, mid_ref, taps, band, x_own, x_peer,
                stat_ref, sems):
    core = core_ref[0]
    groups = [tap_copies(core, own_ref, peer_ref, taps, sems.at[5:8], down) for down in range(3)]
    start_all(groups[0])
    extra = [fetch(x_ref.at[core], x_own, sems.at[4, 2]), fetch(xp_ref.at[core], x_peer, sems.at[4, 3])]
    fill_bands(band, lambda row: both_rows(act_own, act_peer, row), eq_ref)
    start_all(groups[1])
    start_all(groups[2])
    wait_all(extra)
    for down in range(3):
        wait_all(groups[down])
        if down == 0:
            copies = []
            for index, (own, peer) in enumerate(
                    ((wq_o, wq_p), (wk_o, wk_p), (wv_o, wv_p), (wp_o, wp_p))):
                copies += start_all(
                    weight_copies(core, own, peer, weight.at[index], sems.at[index], ()))
            copies.append(fetch(g_own.at[core], gfull.at[:, 0:HALF], sems.at[4, 0]))
            copies.append(fetch(g_peer.at[core], gfull.at[:, HALF:C], sems.at[4, 1]))

        def conv(half, carry, down=down):
            at = half_rows(half)
            value = dot(tap_band(band, half, down),
                        taps[3 * down : 3 * down + 3].reshape(3 * C, C))
            if down > 0:
                value = value + mid_ref[at, :]
            else:
                value = value + vec_ref[5:6, :] + jnp.concatenate(
                    [x_own[at, :], x_peer[at, :]], 1).astype(F32)
            mid_ref[at, :] = value
            return carry

        lax.fori_loop(0, 2, conv, 0)
    norm_forward(lambda row: mid_ref[at_row(row), :], (normed_ref,), stat_ref, eq_ref,
                 vec_ref[6:7, :], vec_ref[7:8, :], lambda v: v)
    wait_all(copies)
    normed = normed_ref[...]
    query[...] = (dot(normed, weight[0]) + vec_ref[8:9, :]).astype(BF)
    keys[...] = dot(normed, weight[1]).astype(BF)
    values[...] = (dot(normed, weight[2]) + vec_ref[9:10, :]).astype(BF)
    gmixed[...] = dot_nt(gfull[...], weight[3]).astype(BF)

    rows = 512
    spot = lax.broadcasted_iota(jnp.int32, (1, PIX), 1)
    right = (spot & (SIDE - 1)) >= 16
    low = spot >= PIX // 2

    def block(index, carry):
        start = pl.multiple_of(index * rows, rows)
        at = pl.ds(start, rows)
        half = (start >= PIX // 2).astype(jnp.int32) * 2
        bias = []
        for side in range(2):
            base = (half + side) * 4
            row = jnp.where(low, jnp.where(right, eq_ref[base + 3], eq_ref[base + 2]),
                            jnp.where(right, eq_ref[base + 1], eq_ref[base]))
            bias.append(jnp.where(row > 0.5, 0.0, -1e30).reshape(1, 1, 1, PIX))
        bias = jnp.concatenate(bias, 1)
        scores = dot_nt(query[at, :], keys[...]) * (SCALE * LOG2E)
        scores = (scores.reshape(rows // SIDE, 2, 16, PIX) + bias).reshape(rows, PIX)
        expo = jnp.exp2(scores - jnp.max(scores, axis=1, keepdims=True))
        wide = expo * (1.0 / jnp.sum(expo, axis=1, keepdims=True))
        narrow = wide.astype(BF)
        probs[at, :] = narrow
        mixed[at, :] = dot(narrow, values[...]).astype(BF)
        gprobs = dot_nt(gmixed[at, :], values[...])
        delta = jnp.sum(wide * gprobs, axis=1, keepdims=True)
        grads = (wide * (gprobs - delta)).astype(BF)
        gscores[at, :] = grads
        dquery[at, :] = (dot(grads, keys[...]) * SCALE).astype(BF)
        return carry

    lax.fori_loop(0, PIX // rows, block, 0)

    def total(value):
        return jnp.sum(value.astype(F32), axis=0, keepdims=True)

    dkey[...] = (dot_tn(gscores[...], query[...]) * SCALE).astype(BF)
    dvalue[...] = dot_tn(probs[...], gmixed[...]).astype(BF)
    gnormed[...] = (dot_nt(dquery[...], weight[0]) + dot_nt(dkey[...], weight[1])
                    + dot_nt(dvalue[...], weight[2]))
    dbq, dbv, dbp = total(dquery[...]), total(dvalue[...]), total(gfull[...])

    out = mid_ref[...] + dot(mixed[...], weight[3]) + vec_ref[10:11, :]
    out_own[...] = out[:, :HALF]
    out_peer[...] = out[:, HALF:]

    def finish(row, change):
        grad = gfull[at_row(row), :].astype(F32) + change
        gnormed[at_row(row), :] = grad
        gconv_ref[at_row(row), :] = grad.astype(BF)

    dgain, dshift = norm_backward(
        lambda row: mid_ref[at_row(row), :], lambda row: gnormed[at_row(row), :], None, stat_ref,
        eq_ref, vec_ref[6:7, :], vec_ref[7:8, :], False, finish)
    store = fetch(gnormed, gmid_hbm, sems.at[4, 3])
    small_ref[...] = jnp.concatenate(
        [dgain, dshift, dbq, dbv, dbp, total(gconv_ref[...]), dbq, dbq], 0)
    store.wait()


def attn_call(core, eq, acts, own, peer, x, g, weights, vec):
    flat = [w for pair_of in weights for w in pair_of]
    return pl.pallas_call(
        attn_kernel,
        out_shape=(shape(PIX, HALF, F32), shape(PIX, HALF, F32), pltpu.HBM((PIX, C), F32),
                   shape(PIX, C, BF), shape(8, C, F32)) + (pltpu.VMEM((PIX, C), BF),) * 5,
        in_specs=[SM, SM, VM, VM] + [HBM] * 14 + [VM],
        out_specs=(VM, VM, HBM) + (VM,) * 7,
        scratch_shapes=[pltpu.VMEM((4, C, C), BF)] + [pltpu.VMEM((PIX, C), BF)] * 5
        + [pltpu.VMEM((PIX, PIX), BF)] * 2 + [pltpu.VMEM((PIX, C), F32)] * 2
        + [pltpu.VMEM((9, C, C), BF), pltpu.VMEM((2, BAND, 3 * C), BF)]
        + [pltpu.VMEM((PIX, HALF), BF)] * 2
        + [pltpu.VMEM((8, C), F32), pltpu.SemaphoreType.DMA((8, 4))],
        name="attention", compiler_params=params(40), cost_estimate=cost(28),
    )(core, eq, *acts, *in_hbm(own, peer, *x, *g, *flat), vec)


def attn_wgrad_kernel(core_ref, normed_ref, dquery, dkey, dvalue, mixed, g_own, g_peer, dw_own,
                      dw_peer, g_mine, g_back, sems):
    core = core_ref[0]
    copies = [fetch(g_own.at[core], g_mine, sems.at[0]), fetch(g_peer.at[core], g_back, sems.at[1])]
    normed = normed_ref[...]
    for index, ref in enumerate((dquery, dkey, dvalue)):
        full = dot_tn(normed, ref[...]).astype(BF)
        for local in range(2):
            target = pl.multiple_of(index * C + (core ^ local) * HALF, HALF)
            part = full[local * HALF : (local + 1) * HALF, :]
            dw_own[pl.ds(target, HALF), :] = part[:, :HALF]
            dw_peer[pl.ds(target, HALF), :] = part[:, HALF:]
    for copy in copies:
        copy.wait()
    for local, ref in enumerate((g_mine, g_back)):
        target = pl.multiple_of(3 * C + (core ^ local) * HALF, HALF)
        part = dot_tn(mixed[...], ref[...]).astype(BF)
        dw_own[pl.ds(target, HALF), :] = part[:HALF]
        dw_peer[pl.ds(target, HALF), :] = part[HALF:]


def attn_wgrad_call(core, normed, dquery, dkey, dvalue, mixed, g):
    return pl.pallas_call(
        attn_wgrad_kernel, out_shape=(shape(4 * C, HALF, BF),) * 2,
        in_specs=[SM] + [VM] * 5 + [HBM] * 2, out_specs=(VM, VM),
        scratch_shapes=[pltpu.VMEM((PIX, HALF), BF)] * 2 + [pltpu.SemaphoreType.DMA((2,))],
        name="attention_weights", compiler_params=params(6), cost_estimate=cost(3),
    )(core, normed, dquery, dkey, dvalue, mixed, *in_hbm(*g))


def fetch_all(sources, targets, sems):
    return [fetch(source, target, sems.at[index])
            for index, (source, target) in enumerate(zip(sources, targets))]


def wgrad2_kernel(core_ref, eq_ref, *refs):
    sources, (out_ref, act_mine, act_other, grad_mine, grad_other, band, band_other, sems) = (
        refs[:4], refs[4:])
    core = core_ref[0]
    copies = fetch_all(sources, (act_mine, act_other, grad_mine, grad_other), sems)
    copies[0].wait()
    fill_bands(band, lambda row: act_mine[at_row(row), :], eq_ref.at[0])
    copies[1].wait()
    fill_bands(band_other, lambda row: act_other[at_row(row), :], eq_ref.at[1])
    for copy in copies[2:]:
        copy.wait()

    def body(down, carry):
        for local in range(2):
            full = 0.0
            for half in range(2):
                rows = slice(half * (PIX // 2), (half + 1) * (PIX // 2))
                full = full + dot_tn(tap_band(band, half, down),
                                     grad_mine[rows, local * HALF : (local + 1) * HALF])
                full = full + dot_tn(tap_band(band_other, half, down),
                                     grad_other[rows, (1 - local) * HALF : (2 - local) * HALF])
            full = full.astype(BF)
            for index in range(3):
                base = (3 * down + index) * C + (core ^ local) * HALF
                out_ref[pl.ds(pl.multiple_of(base, HALF), HALF), :] = full[
                    index * HALF : (index + 1) * HALF]
        return carry

    lax.fori_loop(0, 3, body, 0)


def wgrad2_call(core, eqs, *arrays):
    return pl.pallas_call(
        wgrad2_kernel, out_shape=shape(9 * C, HALF, BF), in_specs=[SM, SM] + [HBM] * 4,
        out_specs=VM,
        scratch_shapes=[pltpu.VMEM((PIX, HALF), BF)] * 2 + [pltpu.VMEM((PIX, C), BF)] * 2
        + [pltpu.VMEM((2, BAND, 3 * HALF), BF)] * 2 + [pltpu.SemaphoreType.DMA((4,))],
        name="wgrad2", compiler_params=params(14), cost_estimate=cost(7),
    )(core, eqs, *in_hbm(*arrays))


TAPS = 6


def wgrad1_kernel(core_ref, eq_ref, *refs):
    sources, (out_ref, tail_ref, band, band_other, act, act2, grad_mine, grad_other, sems) = (
        refs[:6], refs[6:])
    core = core_ref[0]
    copies = fetch_all(sources, (grad_mine, grad_other, act.at[:, 0:HALF], act.at[:, HALF:C],
                                 act2.at[:, 0:HALF], act2.at[:, HALF:C]), sems)
    copies[0].wait()
    fill_bands(band, lambda row: grad_mine[at_row(row), :], eq_ref.at[0])
    copies[1].wait()
    fill_bands(band_other, lambda row: grad_other[at_row(row), :], eq_ref.at[1])
    for copy in copies[2:]:
        copy.wait()

    def group(down, out, base):
        full = 0.0
        for half in range(2):
            rows = slice(half * (PIX // 2), (half + 1) * (PIX // 2))
            full = full + dot_tn(act[rows, :], tap_band(band, half, down))
            full = full + dot_tn(act2[rows, :], tap_band(band_other, half, down))
        full = full.astype(BF)
        for index in range(3):
            for local in range(2):
                where = base + (2 - index) * C + (core ^ local) * HALF
                out[pl.ds(pl.multiple_of(where, HALF), HALF), :] = full[
                    local * HALF : (local + 1) * HALF, index * HALF : (index + 1) * HALF]

    group(0, tail_ref, 0)

    def body(down, carry):
        group(down, out_ref, (2 - down) * 3 * C)
        return carry

    lax.fori_loop(1, 3, body, 0)


def wgrad1_call(core, eqs, *arrays):
    return pl.pallas_call(
        wgrad1_kernel, out_shape=(shape(TAPS * C, HALF, BF), shape((9 - TAPS) * C, HALF, BF)),
        in_specs=[SM, SM] + [HBM] * 6, out_specs=(VM, VM),
        scratch_shapes=[pltpu.VMEM((2, BAND, 3 * HALF), BF)] * 2 + [pltpu.VMEM((PIX, C), BF)] * 2
        + [pltpu.VMEM((PIX, HALF), BF)] * 2 + [pltpu.SemaphoreType.DMA((6,))],
        name="wgrad1", compiler_params=params(16), cost_estimate=cost(7),
    )(core, eqs, *in_hbm(*arrays))


def dgrad_kernel(first, core_ref, eq_ref, own_ref, peer_ref, vec_ref, *refs):
    if first:
        (grad_own, grad_peer, stat_own, stat_peer, x_hbm, xp_hbm, gmid_hbm, out_own, out_peer, small_ref, weight, patch,
         total, stat_ref, sems, x_own, x_peer, gmid_ref) = refs
        load = lambda row: both_rows(x_own, x_peer, row)
        load_grad = lambda row: both_rows(grad_own, grad_peer, row)
        sources = (x_hbm.at[core_ref[0]], xp_hbm.at[core_ref[0]], gmid_hbm)
        held = (x_own, x_peer, gmid_ref)
        gain, shift = vec_ref[0:1, :], vec_ref[1:2, :]
    else:
        (grad_ref, stat_own, stat_peer, in_own, in_peer, out_own, out_peer, small_ref, weight, patch,
         total, stat_ref, sems, mine, back) = refs
        load = lambda row: both_rows(mine, back, row)
        load_grad = lambda row: grad_ref[at_row(row), :]
        sources, held = (in_own, in_peer), (mine, back)
        gain, shift = vec_ref[3:4, :], vec_ref[4:5, :]
    stat_ref[:, :HALF] = stat_own[...]
    stat_ref[:, HALF:] = stat_peer[...]
    copies = [tap_copies(core_ref[0], own_ref, peer_ref, weight, sems, 2 - down)
              for down in range(3)]
    for group in copies:
        for copy in group:
            copy.start()
    later = fetch_all(sources, held, sems.at[3])
    fill_bands(patch, load_grad, eq_ref)
    for down in range(3):
        for copy in copies[down]:
            copy.wait()

        def body(half, carry, down=down):
            value = total[half_rows(half), :] if down > 0 else 0.0
            for t in range(3):
                value = value + dot_nt(tap_band(patch, half, down)[:, t * C : (t + 1) * C],
                                       weight[8 - (3 * down + t)])
            total[half_rows(half), :] = value
            return carry

        lax.fori_loop(0, 2, body, 0)
    for copy in later:
        copy.wait()

    def finish(row, change):
        at = at_row(row)
        if first:
            change = change + gmid_ref[at, :]
        out_own[at, :] = change[:, :HALF].astype(out_own.dtype)
        out_peer[at, :] = change[:, HALF:].astype(out_peer.dtype)

    dgain, dshift = norm_backward(load, lambda row: total[at_row(row), :], total, stat_ref, eq_ref,
                                  gain, shift, True, finish)
    bias = [jnp.sum(ref[...].astype(F32), axis=0, keepdims=True) for ref in (out_own, out_peer)]
    bias = jnp.concatenate(bias, 1)
    small_ref[...] = jnp.concatenate([dgain, dshift, bias] + [dgain] * 5, 0)


def dgrad_call(core, eq, grad, own, peer, vec, stats, source, gmid=None):
    first = gmid is not None
    extra = (*source, gmid) if first else source
    held = [pltpu.VMEM((PIX, HALF), BF if first else F32)] * 2
    held += [pltpu.VMEM((PIX, C), F32)] if first else []
    outs = (shape(PIX, HALF, F32 if first else BF),) * 2
    return pl.pallas_call(
        functools.partial(dgrad_kernel, first),
        out_shape=outs + (shape(8, C, F32),),
        in_specs=[SM, SM, HBM, HBM, VM] + [VM] * (len(grad) + len(stats)) + [HBM] * len(extra),
        out_specs=(VM,) * 3,
        scratch_shapes=[pltpu.VMEM((9, C, C), BF), pltpu.VMEM((2, BAND, 3 * C), BF),
                        pltpu.VMEM((PIX, C), F32), pltpu.VMEM((8, C), F32),
                        pltpu.SemaphoreType.DMA((4, 4))] + held,
        name="dgrad1" if first else "dgrad2", compiler_params=params(16), cost_estimate=cost(10),
    )(core, eq, *in_hbm(own, peer), vec, *grad, *stats, *in_hbm(*extra))


EVERY, TIED, SMALL_FROM = "asrf", 9, 0
ORDERS = {
    "second": ((0, 2, 1), (2, 1, 0)),
    "attn": ((1, 0, 2), (1, 2, 0)),
    "first": ((0, 2, 1), (1, 0, 2)),
    "rest": ((2, 1, 0), (2, 1, 0)),
}


def orders_of(kind, size):
    bits = size.bit_length() - 1
    return [[*order, *range(3, bits)] for order in ORDERS[kind]]


def exchange(array, orders, stage, size):
    moves = [((d, c), (d ^ (1 << orders[c][stage]), c)) for d in range(size) for c in range(2)]
    return lax.ppermute(array, ("dp", "chan"), [(a[0] * 2 + a[1], b[0] * 2 + b[1]) for a, b in moves])


def side_of(orders, stage):
    bit = jnp.where(lax.axis_index("chan") == 0, orders[0][stage], orders[1][stage])
    return (lax.axis_index("dp") >> bit) & 1


def side_base(orders):
    base = 0
    for stage in range(len(orders[0])):
        base = base * 2 + side_of(orders, stage)
    return base


class Chain:
    def __init__(self, part, kind, size):
        self.value, self.size, self.orders, self.step = part, size, orders_of(kind, size), 0
        self.stages, self.rows = len(self.orders[0]), part.shape[0]

    def advance(self):
        stage = self.step if self.step < self.stages else 2 * self.stages - 1 - self.step
        if self.step < self.stages:
            half = self.value.shape[0] // 2
            side = side_of(self.orders, stage)
            send = lax.dynamic_slice_in_dim(self.value, (1 - side) * half, half, 0)
            keep = lax.dynamic_slice_in_dim(self.value, side * half, half, 0)
            self.value = keep + exchange(send, self.orders, stage, self.size)
        else:
            back = exchange(self.value, self.orders, stage, self.size)
            self.value = jnp.concatenate([self.value, back], 0) if stage > 0 else (self.value, back)
        self.step += 1


def together(chains, *values):
    held = lax.optimization_barrier(([c.value for c in chains], values))
    for chain, value in zip(chains, held[0]):
        chain.value = value
    return held[1]


def after(value, *others):
    return lax.optimization_barrier((value, *others))[0]


def spread_kernel(plan, base_ref, *refs):
    count = len(plan)
    ins, out_hbm, wide, sems = refs[:count], refs[-2 * count - 1], refs[-2 * count : -count], refs[-count:]
    copies = []
    for index, (start, first, rows) in enumerate(plan):
        wide[index][...] = ins[index][...].astype(F32)
        for block in range(ins[index].shape[0] // rows):
            row = start + ((block + first) ^ base_ref[index]) * rows
            copies.append(fetch(
                wide[index].at[block * rows : (block + 1) * rows, :],
                out_hbm.at[pl.ds(pl.multiple_of(row, rows & -rows), rows), :],
                sems[index].at[block]))
    wait_all(copies)


def spread(parts, rows, token, into=None):
    plan = [(start, first, chain.rows // chain.size) for _, chain, start, first in parts]
    arrays = [part[0] for part in parts]
    base = jnp.stack([side_base(part[1].orders) for part in parts]).astype(jnp.int32)
    held = () if into is None else (into,)
    return pl.pallas_call(
        functools.partial(spread_kernel, plan), out_shape=pltpu.HBM((rows, HALF), F32),
        in_specs=[SM] + [VM] * len(arrays) + [HBM] * len(held), out_specs=HBM,
        input_output_aliases={} if into is None else {1 + len(arrays): 0},
        scratch_shapes=[pltpu.VMEM(array.shape, F32) for array in arrays]
        + [pltpu.SemaphoreType.DMA((array.shape[0] // one[2],)) for array, one in zip(arrays, plan)],
        compiler_params=params(14), name="spread", cost_estimate=cost(2),
    )(after(base, token), *arrays, *held)


def second_target(row):
    return 0, row // C * HALF + row % HALF, slice(row // HALF % 2 * HALF, (row // HALF % 2 + 1) * HALF)


def attn_target(row):
    if row < 3 * C:
        return row // C, row % C, slice(0, HALF)
    row -= 3 * C
    return 3, row % HALF, slice(row // HALF * HALF, (row // HALF + 1) * HALF)


def place_kernel(size, targets, base_ref, *refs):
    ins, outs, held = refs[: 2 * len(targets)], refs[2 * len(targets) : -1], refs[-1]
    start = 0
    for index, target in enumerate(targets):
        part, part2 = ins[2 * index : 2 * index + 2]
        half = part.shape[0]
        held[start : start + half, :] = part[...]
        held[start + half : start + 2 * half, :] = part2[...]
        rows = 2 * half // size
        piece = math.gcd(rows, HALF)
        for row in range(0, 2 * half, piece):
            source = ((row // rows) ^ base_ref[index]) * rows + row % rows + start
            which, at, columns = target(row)
            outs[which][at : at + piece, columns] = held[
                pl.ds(pl.multiple_of(source, piece), piece), :].astype(F32)
        start += 2 * half


def place(chains, targets, shapes, token):
    parts = [part for chain in chains for part in chain.value]
    rows = sum(part.shape[0] for part in parts)
    base = jnp.stack([side_base(chain.orders) for chain in chains]).astype(jnp.int32)
    return pl.pallas_call(
        functools.partial(place_kernel, chains[0].size, targets),
        out_shape=tuple(shape(*one, F32) for one in shapes), in_specs=[SM] + [VM] * len(parts),
        out_specs=(VM,) * len(shapes), scratch_shapes=[pltpu.VMEM((rows, HALF), BF)],
        compiler_params=params(12), name="place", cost_estimate=cost(2),
    )(after(base, token), *parts)


def swap(array):
    return lax.ppermute(array, "chan", [(0, 1), (1, 0)])


def shards(pixels, tile_ids, first_gain, first_shift, first_conv, first_bias, second_gain,
           second_shift, second_conv, second_bias, attn_gain, attn_shift, query_weight,
           query_bias, key_weight, value_weight, value_bias, proj_weight, proj_bias, cotangent,
           *, size):
    index = lax.axis_index("chan")
    core = index.reshape(1).astype(jnp.int32)
    tiles = tile_ids.reshape(2, 2, 16, 2, 16)[:, :, 0, :, 0].reshape(2, 4)
    eqs = (tiles[:, :, None] == tiles[:, None, :]).astype(F32).reshape(2, 16)
    eqs = jnp.where(index == 0, eqs, eqs[::-1])
    own_vectors = jnp.stack([first_gain, first_shift, first_bias, second_gain, second_shift,
                             second_bias, attn_gain, attn_shift, query_bias, value_bias, proj_bias])
    pixels_peer = swap(pixels)
    pixels_peer, own_vectors, eqs = lax.optimization_barrier((pixels_peer, own_vectors, eqs))
    eq = eqs[0]
    peer_vectors = swap(own_vectors)
    first_conv, peer_vectors, pixels_peer = lax.optimization_barrier(
        (first_conv, peer_vectors, pixels_peer))
    first_peer = swap(first_conv)
    weights = lax.optimization_barrier(
        (query_weight, key_weight, value_weight, proj_weight, peer_vectors))[:4]
    weights_peer = [swap(array) for array in weights]
    vectors = jnp.concatenate([own_vectors, peer_vectors], 1)
    x = (pixels, pixels_peer)
    act_own, act_peer, stat_own, stat_peer, band, conv1_own, act2_own, stat2_own = front_call(
        core, eq, *x, first_conv, own_vectors, peer_vectors)
    first_peer, act2_own, act_own, act_peer, second_conv, cotangent, *weights_peer = (
        lax.optimization_barrier((first_peer, act2_own, act_own, act_peer, second_conv, cotangent,
                                  *weights_peer)))
    second_peer, g_peer = swap(second_conv), swap(cotangent)
    act_other = (swap(act_peer), swap(act_own))
    conv1_peer, act2_peer, stat2_peer = front_peer_call(core, eq, band, first_peer, peer_vectors)
    act2_peer, second_peer, g_peer = lax.optimization_barrier((act2_peer, second_peer, g_peer))
    g = (cotangent, g_peer)
    act2_other = swap(act2_peer)
    out_own, out_peer, gmid, gconv2, small3, *parts, normed = attn_call(
        core, eq, (act2_own, act2_peer), second_conv, second_peer, x, g,
        list(zip(weights, weights_peer)), vectors)
    gconv2, act2_other, *act_other = lax.optimization_barrier((gconv2, act2_other, *act_other))
    gconv2_other = swap(gconv2)
    dattn, dattn_peer = attn_wgrad_call(core, normed, *parts, g)
    dattn, gconv2, gconv2_other = lax.optimization_barrier((dattn, gconv2, gconv2_other))
    attn_other = swap(dattn_peer)
    part = wgrad2_call(core, eqs, act2_own, act2_other, gconv2, gconv2_other)
    attn_other, part = lax.optimization_barrier((attn_other, part))
    second, attn_sum = Chain(part, "second", size), Chain(dattn + attn_other, "attn", size)
    (gconv2,) = together([second, attn_sum], gconv2)

    for chain in (attn_sum, second):
        chain.advance()
    gconv1_own, gconv1_peer, small2 = dgrad_call(
        core, eq, (gconv2,), second_conv, second_peer, vectors, (stat2_own, stat2_peer),
        (conv1_own, conv1_peer))
    gconv1_other = swap(gconv1_peer)
    gconv1_own, gconv1_other = together([second, attn_sum], gconv1_own, gconv1_other)

    for chain in (attn_sum, second):
        chain.advance()
    part, tail = wgrad1_call(core, eqs, gconv1_own, gconv1_other, act_own, act_peer, *act_other)
    first, rest = Chain(part, "first", size), Chain(tail, "rest", size)
    (gconv1_own,) = together([second, attn_sum, first, rest], gconv1_own)

    known = {"a": attn_sum, "s": second, "r": rest, "f": first}
    every = [known[name] for name in EVERY]
    for chain in every:
        chain.advance()
    pix_own, pix_peer, small1 = dgrad_call(core, eq, (gconv1_own, gconv1_peer), first_conv,
                                           first_peer, vectors, (stat_own, stat_peer), x, gmid)
    small = jnp.concatenate([small1, small2, small3], 0)
    pix_peer, out_peer, small = together(every, pix_peer, out_peer, small)

    small = small[:, :HALF] + swap(small[:, HALF:])
    pix_back = swap(pix_peer)
    out_back = swap(out_peer)
    bits = size.bit_length() - 1
    turn, bit = 0, 0
    token = core
    while any(chain.step < 2 * bits for chain in every):
        for chain in every:
            if chain.step < 2 * bits:
                chain.advance()
                if turn < TIED:
                    (token,) = together([chain], token)
        if turn >= SMALL_FROM and bit < bits:
            small = small + lax.ppermute(
                small, "dp", [(i, i ^ (1 << bit)) for i in range(size)])
            small, token = lax.optimization_barrier((small, token))
            bit += 1
        turn += 1
    (sums2,) = place([second], [second_target], [(9 * HALF, C)], core)
    sums3 = place([attn_sum], [attn_target], [(C, HALF), (C, HALF), (C, HALF), (HALF, C)], core)
    mine, back = first.value
    half = size // 2
    sums1 = spread([(rest.value[0], rest, TAPS * C, 0), (mine, first, 0, 0)], 9 * C, core)
    sums1 = spread([(rest.value[1], rest, TAPS * C, half), (back, first, 0, half)], 9 * C, token, sums1)

    def unboth(own, back):
        return jnp.where(index == 0, jnp.stack([own, back]), jnp.stack([back, own]))

    return (
        unboth(out_own, out_back), unboth(pix_own, pix_back), small[0], small[1],
        sums1.reshape(9, C, HALF), small[10], small[8], small[9], sums2.reshape(9, HALF, C),
        small[21], small[16], small[17], sums3[0], small[18], sums3[1], sums3[2], small[19],
        sums3[3], small[20],
    )


def solution(mesh):
    chan = P("chan")
    rows = P("dp", None, "chan")
    return jax.shard_map(
        functools.partial(shards, size=mesh.shape["dp"]),
        mesh=mesh,
        in_specs=(
            rows, P("dp", None), chan, chan, P(None, None, "chan"), chan, chan, chan,
            P(None, "chan", None), chan, chan, chan, P(None, "chan"), chan, P(None, "chan"),
            P(None, "chan"), chan, P("chan", None), chan, rows,
        ),
        out_specs=(
            rows, rows, chan, chan, P(None, None, "chan"), chan, chan, chan,
            P(None, "chan", None), chan, chan, chan, P(None, "chan"), chan, P(None, "chan"),
            P(None, "chan"), chan, P("chan", None), chan,
        ),
        check_vma=False,
    )
```

```python
import functools
import math
import jax
import jax.numpy as jnp
from jax import lax
from jax.experimental import pallas as pl
from jax.experimental.pallas import tpu as pltpu
from jax.sharding import PartitionSpec as P

C = 512
HALF = 256
GROUP = 16
SIDE = 32
PIX = 1024
EPSILON = 1e-06
BF = jnp.bfloat16
F32 = jnp.float32
MB = 1024 * 1024
VM = pl.BlockSpec(memory_space=pltpu.VMEM)
SM = pl.BlockSpec(memory_space=pltpu.SMEM)
HBM = pl.BlockSpec(memory_space=pltpu.HBM)
SCALE = C ** (-0.5)
LOG2E = 1.4426950408889634


def dot(first, second):
    return jnp.dot(first, second, preferred_element_type=F32)


def dot_nt(first, second):
    return lax.dot_general(first, second, (((1,), (1,)), ((), ())), preferred_element_type=F32)


def dot_tn(first, second):
    return lax.dot_general(first, second, (((0,), (0,)), ((), ())), preferred_element_type=F32)


def at_row(row):
    return pl.ds(pl.multiple_of(row * SIDE, SIDE), SIDE)


def group_sums(rows):
    full = jnp.concatenate(rows, 0)
    width = full.shape[1]
    lane = lax.broadcasted_iota(jnp.int32, full.shape, 1)
    for step in (1, 2, 4, 8):
        full = full + jnp.where(
            (lane & step) == 0, pltpu.roll(full, width - step, 1), pltpu.roll(full, step, 1)
        )
    return [full[i : i + 1] for i in range(len(rows))]


def image_means(sums, eq_ref):
    rows = []
    for i in range(4):
        total, count = 0.0, 0.0
        for j in range(4):
            total = total + eq_ref[4 * i + j] * sums[j]
            count = count + eq_ref[4 * i + j]
        rows.append(total / (count * float(256 * GROUP)))
    return group_sums(rows)


def tiles_of(rows):
    return rows.reshape(2, 16, rows.shape[-1])


def pair(rows, top):
    return jnp.concatenate([rows[2 * top + side].reshape(1, 1, -1) for side in range(2)], 0)


def over_canvas(step, count, width=C, unroll=2):
    found = [[] for _ in range(count)]
    for top in range(2):
        zero = tuple(jnp.zeros((2, 16, width), F32) for _ in range(count))

        def body(index, carry, top=top):
            return tuple(a + b for a, b in zip(carry, step(top, top * 16 + index)))

        totals = lax.fori_loop(0, 16, body, zero, unroll=unroll)
        for n in range(count):
            columns = jnp.sum(totals[n], axis=1)
            found[n] += [columns[0:1], columns[1:2]]
    return found


def for_rows(step, unroll=2):
    for top in range(2):

        def body(index, carry, top=top):
            step(top, top * 16 + index)
            return carry

        lax.fori_loop(0, 16, body, 0, unroll=unroll)


def norm_stats(load, eq_ref, width):
    (sums,) = over_canvas(lambda top, row: (tiles_of(load(row)),), 1, width)
    means = image_means(sums, eq_ref)
    centers = [pair(means, top) for top in range(2)]

    def square(top, row):
        off = tiles_of(load(row)) - centers[top]
        return (off * off,)

    (squares,) = over_canvas(square, 1, width)
    rstds = [lax.rsqrt(v + EPSILON) for v in image_means(squares, eq_ref)]
    return means, rstds


def swish(value):
    half = 0.5 * value
    return half + half * jnp.tanh(half)


def norm_forward(load, out_refs, stat_ref, eq_ref, gain, shift, act):
    width = gain.shape[-1]
    means, rstds = norm_stats(load, eq_ref, width)
    stat_ref[...] = jnp.concatenate(means + rstds, 0)
    centers = [pair(means, top) for top in range(2)]
    slopes = [pair([r * gain for r in rstds], top) for top in range(2)]
    offset = shift.reshape(1, 1, width)

    def step(top, row):
        value = (tiles_of(load(row)) - centers[top]) * slopes[top] + offset
        value = act(value).reshape(SIDE, width).astype(BF)
        held = width // len(out_refs)
        for index, ref in enumerate(out_refs):
            ref[at_row(row), :] = value[:, index * held : (index + 1) * held]

    for_rows(step)


def norm_backward(load, load_grad, keep_ref, stat_ref, eq_ref, gain, shift, with_swish, finish):
    stats = stat_ref[...]
    means = [stats[i : i + 1] for i in range(4)]
    rstds = [stats[4 + i : 5 + i] for i in range(4)]
    centers = [pair(means, top) for top in range(2)]
    rates = [pair(rstds, top) for top in range(2)]
    scale, offset = gain.reshape(1, 1, C), shift.reshape(1, 1, C)

    def first(top, row):
        unit = (tiles_of(load(row)) - centers[top]) * rates[top]
        grad = tiles_of(load_grad(row))
        if with_swish:
            value = unit * scale + offset
            gate = 0.5 + 0.5 * jnp.tanh(0.5 * value)
            grad = grad * (gate * (1.0 + value * (1.0 - gate)))
            keep_ref[at_row(row), :] = grad.reshape(SIDE, C)
        return grad, grad * unit

    plain, scaled = over_canvas(first, 2)
    mean_plain = image_means([p * gain for p in plain], eq_ref)
    mean_scaled = image_means([s * gain for s in scaled], eq_ref)
    first_means = [pair(mean_plain, top) for top in range(2)]
    second_means = [pair(mean_scaled, top) for top in range(2)]

    def second(top, row):
        unit = (tiles_of(load(row)) - centers[top]) * rates[top]
        grad = tiles_of(keep_ref[at_row(row), :] if with_swish else load_grad(row))
        change = rates[top] * (grad * scale - first_means[top] - unit * second_means[top])
        finish(row, change.reshape(SIDE, C))

    for_rows(second)
    return sum(scaled), sum(plain)


BAND = PIX // 2 + 2 * SIDE


def row_mask(eq_ref, target, source, right):
    column = lax.broadcasted_iota(jnp.int32, (SIDE, 128), 0)

    def eq(side, other):
        return eq_ref[(2 * target + side) * 4 + 2 * source + other]

    if right == 0:
        mask = jnp.where(column < 16, eq(0, 0), eq(1, 1))
    elif right < 0:
        mask = jnp.where(column < 16, eq(0, 0), jnp.where(column == 16, eq(1, 0), eq(1, 1)))
        mask = jnp.where(column == 0, 0.0, mask)
    else:
        mask = jnp.where(column < 15, eq(0, 0), jnp.where(column == 15, eq(0, 1), eq(1, 1)))
        mask = jnp.where(column == SIDE - 1, 0.0, mask)
    return mask.astype(BF)


def fill_bands(band_ref, load, eq_ref, columns=None):
    width = band_ref.shape[2] // 3

    def put(half, place, value, masks):
        moved = [pltpu.roll(value, 1, 0), value, pltpu.roll(value, SIDE - 1, 0)]
        for index in range(3):
            part = moved[index].astype(BF)
            if masks[index] is not None:
                part = part * jnp.concatenate([masks[index]] * (width // 128), 1)
            if columns is None:
                band_ref[half, at_row(place), index * width : (index + 1) * width] = part
            else:
                for number in range(width // HALF):
                    where = pl.ds(columns(index, number), HALF)
                    band_ref[half, at_row(place), where] = part[
                        :, number * HALF : (number + 1) * HALF]

    for half in range(2):
        inner = [row_mask(eq_ref, half, half, -1), None, row_mask(eq_ref, half, half, 1)]

        def body(index, carry, half=half, inner=inner):
            put(half, index + 1, load(half * 16 + index).astype(F32), inner)
            return carry

        lax.fori_loop(0, 16, body, 0, unroll=2)
        across = [row_mask(eq_ref, half, 1 - half, right) for right in (-1, 0, 1)]
        put(half, 17 - 17 * half, load(16 - half).astype(F32), across)
        band_ref[half, 17 * half * SIDE : (17 * half + 1) * SIDE, :] = jnp.zeros(
            (SIDE, 3 * width), BF)


def half_rows(half):
    return pl.ds(pl.multiple_of(half * (PIX // 2), PIX // 2), PIX // 2)


def tap_band(band_ref, half, down):
    if isinstance(down, int):
        return band_ref[half, down * SIDE : down * SIDE + PIX // 2, :]
    return band_ref[half, pl.ds(pl.multiple_of(down * SIDE, SIDE), PIX // 2), :]


def parts_apart(index, number):
    return number * 3 * HALF + index * HALF


def swapped(core, number):
    return pl.multiple_of((core ^ number) * HALF, HALF)


def start_all(copies):
    for copy in copies:
        copy.start()
    return copies


def wait_all(copies):
    for copy in copies:
        copy.wait()


def half_copies(core, source, target, sems):
    return [start_all([
        pltpu.make_async_copy(source.at[pl.ds(3 * group, 3), pl.ds(swapped(core, part), HALF), :],
                              target.at[group, part], sems.at[group, part])
        for part in range(2)]) for group in range(3)]


def half_conv(band, weight, copies, bias, total):
    for down in range(3):
        wait_all(copies[down])

        def body(half, carry, down=down):
            at = half_rows(half)
            value = dot(tap_band(band, half, down), weight[down].reshape(6 * HALF, HALF))
            total[at, :] = value + (total[at, :] if down > 0 else bias)
            return carry

        lax.fori_loop(0, 2, body, 0)


def tap_copies(core, own_ref, peer_ref, all_ref, sems, group):
    lead = (pl.ds(3 * group, 3),)
    return weight_copies(core, own_ref, peer_ref, all_ref, sems.at[group], lead)


def weight_copies(core, own_ref, peer_ref, all_ref, sems, lead):
    copies = []
    for local in range(2):
        source = pl.ds(pl.multiple_of((core ^ local) * HALF, HALF), HALF)
        target = pl.ds(local * HALF, HALF)
        for which, ref in enumerate((own_ref, peer_ref)):
            held = pl.ds(which * HALF, HALF)
            if own_ref.shape[-1] == HALF:
                src, dst = (source, slice(None)), (target, held)
            else:
                src, dst = (slice(None), source), (held, target)
            copies.append(
                pltpu.make_async_copy(
                    ref.at[lead + src], all_ref.at[lead + dst], sems.at[2 * local + which]
                )
            )
    return copies


def params(limit):
    return pltpu.CompilerParams(vmem_limit_bytes=limit * MB)


def cost(micros):
    return pl.CostEstimate(flops=int(micros * 1.1e9), bytes_accessed=1 << 20, transcendentals=0)


def shape(rows, columns, dtype):
    return jax.ShapeDtypeStruct((rows, columns), dtype)


def in_hbm(*arrays):
    return [pltpu.with_memory_space_constraint(array, pltpu.HBM) for array in arrays]


def fetch(source, target, sem):
    copy = pltpu.make_async_copy(source, target, sem)
    copy.start()
    return copy


def both_rows(own_ref, peer_ref, row):
    return jnp.concatenate([own_ref[at_row(row), :], peer_ref[at_row(row), :]], 1).astype(F32)


def front_kernel(core_ref, eq_ref, x_hbm, xp_hbm, w_hbm, vec_ref, peer_ref, act_own_hbm, act_peer_hbm, stat_own, stat_peer, band,
                 conv_hbm, next_ref, stat2_ref, x_own, x_peer, act_own, act_peer, weight, total, sems):
    core = core_ref[0]
    first = fetch(x_hbm.at[core], x_own, sems.at[3, 0])
    second = fetch(xp_hbm.at[core], x_peer, sems.at[3, 1])
    copies = half_copies(core, w_hbm, weight, sems)
    first.wait()
    norm_forward(lambda row: x_own[at_row(row), :].astype(F32), (act_own,), stat_own, eq_ref,
                 vec_ref[0:1, :], vec_ref[1:2, :], swish)
    second.wait()
    norm_forward(lambda row: x_peer[at_row(row), :].astype(F32), (act_peer,), stat_peer, eq_ref,
                 peer_ref[0:1, :], peer_ref[1:2, :], swish)
    stores = [fetch(act_own, act_own_hbm, sems.at[4, 0]), fetch(act_peer, act_peer_hbm, sems.at[4, 1])]
    fill_bands(band, lambda row: both_rows(act_own, act_peer, row), eq_ref, parts_apart)
    half_conv(band, weight, copies, vec_ref[2:3, :], total)
    stores.append(fetch(total, conv_hbm, sems.at[3, 0]))
    norm_forward(lambda row: total[at_row(row), :], (next_ref,), stat2_ref, eq_ref, vec_ref[3:4, :],
                 vec_ref[4:5, :], swish)
    wait_all(stores)


def front_peer_kernel(core_ref, eq_ref, band, w_hbm, vec_ref, conv_hbm, next_ref, stat2_ref, weight,
                      total, sems):
    copies = half_copies(core_ref[0], w_hbm, weight, sems)
    half_conv(band, weight, copies, vec_ref[2:3, :], total)
    store = fetch(total, conv_hbm, sems.at[3, 0])
    norm_forward(lambda row: total[at_row(row), :], (next_ref,), stat2_ref, eq_ref, vec_ref[3:4, :],
                 vec_ref[4:5, :], swish)
    store.wait()


def front_call(core, eq, pixels, pixels_peer, weight, own_vectors, peer_vectors):
    half = pltpu.HBM((PIX, HALF), BF)
    return pl.pallas_call(
        front_kernel,
        out_shape=(half, half, shape(8, HALF, F32), shape(8, HALF, F32),
                   pltpu.VMEM((2, BAND, 3 * C), BF), pltpu.HBM((PIX, HALF), F32),
                   shape(PIX, HALF, BF), shape(8, HALF, F32)),
        in_specs=[SM, SM, HBM, HBM, HBM, VM, VM],
        out_specs=(HBM, HBM, VM, VM, VM, HBM, VM, VM),
        scratch_shapes=[pltpu.VMEM((PIX, HALF), BF)] * 4
        + [pltpu.VMEM((3, 2, 3, HALF, HALF), BF), pltpu.VMEM((PIX, HALF), F32),
           pltpu.SemaphoreType.DMA((5, 2))],
        name="front", compiler_params=params(14), cost_estimate=cost(9),
    )(core, eq, *in_hbm(pixels, pixels_peer, weight), own_vectors, peer_vectors)


def front_peer_call(core, eq, band, weight, vec):
    return pl.pallas_call(
        front_peer_kernel,
        out_shape=(pltpu.HBM((PIX, HALF), F32), shape(PIX, HALF, BF), shape(8, HALF, F32)),
        in_specs=[SM, SM, VM, HBM, VM], out_specs=(HBM, VM, VM),
        scratch_shapes=[pltpu.VMEM((3, 2, 3, HALF, HALF), BF), pltpu.VMEM((PIX, HALF), F32),
                        pltpu.SemaphoreType.DMA((4, 2))],
        name="front_peer", compiler_params=params(14), cost_estimate=cost(5),
    )(core, eq, band, *in_hbm(weight), vec)


def attn_kernel(core_ref, eq_ref, act_own, act_peer, own_ref, peer_ref, x_ref, xp_ref, g_own, g_peer,
                wq_o, wq_p, wk_o, wk_p, wv_o, wv_p, wp_o, wp_p, vec_ref, out_own, out_peer, gmid_hbm,
                gconv_ref, small_ref, dquery, dkey, dvalue, mixed, normed_ref, weight, gfull, query,
                keys, values, gmixed, probs, gscores, gnormed, mid_ref, taps, band, x_own, x_peer,
                stat_ref, sems):
    core = core_ref[0]
    groups = [tap_copies(core, own_ref, peer_ref, taps, sems.at[5:8], down) for down in range(3)]
    start_all(groups[0])
    extra = [fetch(x_ref.at[core], x_own, sems.at[4, 2]), fetch(xp_ref.at[core], x_peer, sems.at[4, 3])]
    fill_bands(band, lambda row: both_rows(act_own, act_peer, row), eq_ref)
    start_all(groups[1])
    start_all(groups[2])
    wait_all(extra)
    for down in range(3):
        wait_all(groups[down])
        if down == 0:
            copies = []
            for index, (own, peer) in enumerate(
                    ((wq_o, wq_p), (wk_o, wk_p), (wv_o, wv_p), (wp_o, wp_p))):
                copies += start_all(
                    weight_copies(core, own, peer, weight.at[index], sems.at[index], ()))
            copies.append(fetch(g_own.at[core], gfull.at[:, 0:HALF], sems.at[4, 0]))
            copies.append(fetch(g_peer.at[core], gfull.at[:, HALF:C], sems.at[4, 1]))

        def conv(half, carry, down=down):
            at = half_rows(half)
            value = dot(tap_band(band, half, down),
                        taps[3 * down : 3 * down + 3].reshape(3 * C, C))
            if down > 0:
                value = value + mid_ref[at, :]
            else:
                value = value + vec_ref[5:6, :] + jnp.concatenate(
                    [x_own[at, :], x_peer[at, :]], 1).astype(F32)
            mid_ref[at, :] = value
            return carry

        lax.fori_loop(0, 2, conv, 0)
    norm_forward(lambda row: mid_ref[at_row(row), :], (normed_ref,), stat_ref, eq_ref,
                 vec_ref[6:7, :], vec_ref[7:8, :], lambda v: v)
    wait_all(copies)
    normed = normed_ref[...]
    query[...] = (dot(normed, weight[0]) + vec_ref[8:9, :]).astype(BF)
    keys[...] = dot(normed, weight[1]).astype(BF)
    values[...] = (dot(normed, weight[2]) + vec_ref[9:10, :]).astype(BF)
    gmixed[...] = dot_nt(gfull[...], weight[3]).astype(BF)

    rows = 512
    spot = lax.broadcasted_iota(jnp.int32, (1, PIX), 1)
    right = (spot & (SIDE - 1)) >= 16
    low = spot >= PIX // 2

    def block(index, carry):
        start = pl.multiple_of(index * rows, rows)
        at = pl.ds(start, rows)
        half = (start >= PIX // 2).astype(jnp.int32) * 2
        bias = []
        for side in range(2):
            base = (half + side) * 4
            row = jnp.where(low, jnp.where(right, eq_ref[base + 3], eq_ref[base + 2]),
                            jnp.where(right, eq_ref[base + 1], eq_ref[base]))
            bias.append(jnp.where(row > 0.5, 0.0, -1e30).reshape(1, 1, 1, PIX))
        bias = jnp.concatenate(bias, 1)
        scores = dot_nt(query[at, :], keys[...]) * (SCALE * LOG2E)
        scores = (scores.reshape(rows // SIDE, 2, 16, PIX) + bias).reshape(rows, PIX)
        expo = jnp.exp2(scores - jnp.max(scores, axis=1, keepdims=True))
        wide = expo * (1.0 / jnp.sum(expo, axis=1, keepdims=True))
        narrow = wide.astype(BF)
        probs[at, :] = narrow
        mixed[at, :] = dot(narrow, values[...]).astype(BF)
        gprobs = dot_nt(gmixed[at, :], values[...])
        delta = jnp.sum(wide * gprobs, axis=1, keepdims=True)
        grads = (wide * (gprobs - delta)).astype(BF)
        gscores[at, :] = grads
        dquery[at, :] = (dot(grads, keys[...]) * SCALE).astype(BF)
        return carry

    lax.fori_loop(0, PIX // rows, block, 0)

    def total(value):
        return jnp.sum(value.astype(F32), axis=0, keepdims=True)

    dkey[...] = (dot_tn(gscores[...], query[...]) * SCALE).astype(BF)
    dvalue[...] = dot_tn(probs[...], gmixed[...]).astype(BF)
    gnormed[...] = (dot_nt(dquery[...], weight[0]) + dot_nt(dkey[...], weight[1])
                    + dot_nt(dvalue[...], weight[2]))
    dbq, dbv, dbp = total(dquery[...]), total(dvalue[...]), total(gfull[...])

    out = mid_ref[...] + dot(mixed[...], weight[3]) + vec_ref[10:11, :]
    out_own[...] = out[:, :HALF]
    out_peer[...] = out[:, HALF:]

    def finish(row, change):
        grad = gfull[at_row(row), :].astype(F32) + change
        gnormed[at_row(row), :] = grad
        gconv_ref[at_row(row), :] = grad.astype(BF)

    dgain, dshift = norm_backward(
        lambda row: mid_ref[at_row(row), :], lambda row: gnormed[at_row(row), :], None, stat_ref,
        eq_ref, vec_ref[6:7, :], vec_ref[7:8, :], False, finish)
    store = fetch(gnormed, gmid_hbm, sems.at[4, 3])
    small_ref[...] = jnp.concatenate(
        [dgain, dshift, dbq, dbv, dbp, total(gconv_ref[...]), dbq, dbq], 0)
    store.wait()


def attn_call(core, eq, acts, own, peer, x, g, weights, vec):
    flat = [w for pair_of in weights for w in pair_of]
    return pl.pallas_call(
        attn_kernel,
        out_shape=(shape(PIX, HALF, F32), shape(PIX, HALF, F32), pltpu.HBM((PIX, C), F32),
                   shape(PIX, C, BF), shape(8, C, F32)) + (pltpu.VMEM((PIX, C), BF),) * 5,
        in_specs=[SM, SM, VM, VM] + [HBM] * 14 + [VM],
        out_specs=(VM, VM, HBM) + (VM,) * 7,
        scratch_shapes=[pltpu.VMEM((4, C, C), BF)] + [pltpu.VMEM((PIX, C), BF)] * 5
        + [pltpu.VMEM((PIX, PIX), BF)] * 2 + [pltpu.VMEM((PIX, C), F32)] * 2
        + [pltpu.VMEM((9, C, C), BF), pltpu.VMEM((2, BAND, 3 * C), BF)]
        + [pltpu.VMEM((PIX, HALF), BF)] * 2
        + [pltpu.VMEM((8, C), F32), pltpu.SemaphoreType.DMA((8, 4))],
        name="attention", compiler_params=params(40), cost_estimate=cost(28),
    )(core, eq, *acts, *in_hbm(own, peer, *x, *g, *flat), vec)


def attn_wgrad_kernel(core_ref, normed_ref, dquery, dkey, dvalue, mixed, g_own, g_peer, dw_own,
                      dw_peer, g_mine, g_back, sems):
    core = core_ref[0]
    copies = [fetch(g_own.at[core], g_mine, sems.at[0]), fetch(g_peer.at[core], g_back, sems.at[1])]
    normed = normed_ref[...]
    for index, ref in enumerate((dquery, dkey, dvalue)):
        full = dot_tn(normed, ref[...]).astype(BF)
        for local in range(2):
            target = pl.multiple_of(index * C + (core ^ local) * HALF, HALF)
            part = full[local * HALF : (local + 1) * HALF, :]
            dw_own[pl.ds(target, HALF), :] = part[:, :HALF]
            dw_peer[pl.ds(target, HALF), :] = part[:, HALF:]
    for copy in copies:
        copy.wait()
    for local, ref in enumerate((g_mine, g_back)):
        target = pl.multiple_of(3 * C + (core ^ local) * HALF, HALF)
        part = dot_tn(mixed[...], ref[...]).astype(BF)
        dw_own[pl.ds(target, HALF), :] = part[:HALF]
        dw_peer[pl.ds(target, HALF), :] = part[HALF:]


def attn_wgrad_call(core, normed, dquery, dkey, dvalue, mixed, g):
    return pl.pallas_call(
        attn_wgrad_kernel, out_shape=(shape(4 * C, HALF, BF),) * 2,
        in_specs=[SM] + [VM] * 5 + [HBM] * 2, out_specs=(VM, VM),
        scratch_shapes=[pltpu.VMEM((PIX, HALF), BF)] * 2 + [pltpu.SemaphoreType.DMA((2,))],
        name="attention_weights", compiler_params=params(6), cost_estimate=cost(3),
    )(core, normed, dquery, dkey, dvalue, mixed, *in_hbm(*g))


def fetch_all(sources, targets, sems):
    return [fetch(source, target, sems.at[index])
            for index, (source, target) in enumerate(zip(sources, targets))]


def wgrad2_kernel(core_ref, eq_ref, *refs):
    sources, (out_ref, act_mine, act_other, grad_mine, grad_other, band, band_other, sems) = (
        refs[:4], refs[4:])
    core = core_ref[0]
    copies = fetch_all(sources, (act_mine, act_other, grad_mine, grad_other), sems)
    copies[0].wait()
    fill_bands(band, lambda row: act_mine[at_row(row), :], eq_ref.at[0])
    copies[1].wait()
    fill_bands(band_other, lambda row: act_other[at_row(row), :], eq_ref.at[1])
    for copy in copies[2:]:
        copy.wait()

    def body(down, carry):
        for local in range(2):
            full = 0.0
            for half in range(2):
                rows = slice(half * (PIX // 2), (half + 1) * (PIX // 2))
                full = full + dot_tn(tap_band(band, half, down),
                                     grad_mine[rows, local * HALF : (local + 1) * HALF])
                full = full + dot_tn(tap_band(band_other, half, down),
                                     grad_other[rows, (1 - local) * HALF : (2 - local) * HALF])
            full = full.astype(BF)
            for index in range(3):
                base = (3 * down + index) * C + (core ^ local) * HALF
                out_ref[pl.ds(pl.multiple_of(base, HALF), HALF), :] = full[
                    index * HALF : (index + 1) * HALF]
        return carry

    lax.fori_loop(0, 3, body, 0)


def wgrad2_call(core, eqs, *arrays):
    return pl.pallas_call(
        wgrad2_kernel, out_shape=shape(9 * C, HALF, BF), in_specs=[SM, SM] + [HBM] * 4,
        out_specs=VM,
        scratch_shapes=[pltpu.VMEM((PIX, HALF), BF)] * 2 + [pltpu.VMEM((PIX, C), BF)] * 2
        + [pltpu.VMEM((2, BAND, 3 * HALF), BF)] * 2 + [pltpu.SemaphoreType.DMA((4,))],
        name="wgrad2", compiler_params=params(14), cost_estimate=cost(7),
    )(core, eqs, *in_hbm(*arrays))


TAPS = 6


def wgrad1_kernel(core_ref, eq_ref, *refs):
    sources, (out_ref, tail_ref, band, band_other, act, act2, grad_mine, grad_other, sems) = (
        refs[:6], refs[6:])
    core = core_ref[0]
    copies = fetch_all(sources, (grad_mine, grad_other, act.at[:, 0:HALF], act.at[:, HALF:C],
                                 act2.at[:, 0:HALF], act2.at[:, HALF:C]), sems)
    copies[0].wait()
    fill_bands(band, lambda row: grad_mine[at_row(row), :], eq_ref.at[0])
    copies[1].wait()
    fill_bands(band_other, lambda row: grad_other[at_row(row), :], eq_ref.at[1])
    for copy in copies[2:]:
        copy.wait()

    def group(down, out, base):
        full = 0.0
        for half in range(2):
            rows = slice(half * (PIX // 2), (half + 1) * (PIX // 2))
            full = full + dot_tn(act[rows, :], tap_band(band, half, down))
            full = full + dot_tn(act2[rows, :], tap_band(band_other, half, down))
        full = full.astype(BF)
        for index in range(3):
            for local in range(2):
                where = base + (2 - index) * C + (core ^ local) * HALF
                out[pl.ds(pl.multiple_of(where, HALF), HALF), :] = full[
                    local * HALF : (local + 1) * HALF, index * HALF : (index + 1) * HALF]

    group(0, tail_ref, 0)

    def body(down, carry):
        group(down, out_ref, (2 - down) * 3 * C)
        return carry

    lax.fori_loop(1, 3, body, 0)


def wgrad1_call(core, eqs, *arrays):
    return pl.pallas_call(
        wgrad1_kernel, out_shape=(shape(TAPS * C, HALF, BF), shape((9 - TAPS) * C, HALF, BF)),
        in_specs=[SM, SM] + [HBM] * 6, out_specs=(VM, VM),
        scratch_shapes=[pltpu.VMEM((2, BAND, 3 * HALF), BF)] * 2 + [pltpu.VMEM((PIX, C), BF)] * 2
        + [pltpu.VMEM((PIX, HALF), BF)] * 2 + [pltpu.SemaphoreType.DMA((6,))],
        name="wgrad1", compiler_params=params(16), cost_estimate=cost(7),
    )(core, eqs, *in_hbm(*arrays))


def dgrad_kernel(first, core_ref, eq_ref, own_ref, peer_ref, vec_ref, *refs):
    if first:
        (grad_own, grad_peer, stat_own, stat_peer, x_hbm, xp_hbm, gmid_hbm, out_own, out_peer, small_ref, weight, patch,
         total, stat_ref, sems, x_own, x_peer, gmid_ref) = refs
        load = lambda row: both_rows(x_own, x_peer, row)
        load_grad = lambda row: both_rows(grad_own, grad_peer, row)
        sources = (x_hbm.at[core_ref[0]], xp_hbm.at[core_ref[0]], gmid_hbm)
        held = (x_own, x_peer, gmid_ref)
        gain, shift = vec_ref[0:1, :], vec_ref[1:2, :]
    else:
        (grad_ref, stat_own, stat_peer, in_own, in_peer, out_own, out_peer, small_ref, weight, patch,
         total, stat_ref, sems, mine, back) = refs
        load = lambda row: both_rows(mine, back, row)
        load_grad = lambda row: grad_ref[at_row(row), :]
        sources, held = (in_own, in_peer), (mine, back)
        gain, shift = vec_ref[3:4, :], vec_ref[4:5, :]
    stat_ref[:, :HALF] = stat_own[...]
    stat_ref[:, HALF:] = stat_peer[...]
    copies = [tap_copies(core_ref[0], own_ref, peer_ref, weight, sems, 2 - down)
              for down in range(3)]
    for group in copies:
        for copy in group:
            copy.start()
    later = fetch_all(sources, held, sems.at[3])
    fill_bands(patch, load_grad, eq_ref)
    for down in range(3):
        for copy in copies[down]:
            copy.wait()

        def body(half, carry, down=down):
            value = total[half_rows(half), :] if down > 0 else 0.0
            for t in range(3):
                value = value + dot_nt(tap_band(patch, half, down)[:, t * C : (t + 1) * C],
                                       weight[8 - (3 * down + t)])
            total[half_rows(half), :] = value
            return carry

        lax.fori_loop(0, 2, body, 0)
    for copy in later:
        copy.wait()

    def finish(row, change):
        at = at_row(row)
        if first:
            change = change + gmid_ref[at, :]
        out_own[at, :] = change[:, :HALF].astype(out_own.dtype)
        out_peer[at, :] = change[:, HALF:].astype(out_peer.dtype)

    dgain, dshift = norm_backward(load, lambda row: total[at_row(row), :], total, stat_ref, eq_ref,
                                  gain, shift, True, finish)
    bias = [jnp.sum(ref[...].astype(F32), axis=0, keepdims=True) for ref in (out_own, out_peer)]
    bias = jnp.concatenate(bias, 1)
    small_ref[...] = jnp.concatenate([dgain, dshift, bias] + [dgain] * 5, 0)


def dgrad_call(core, eq, grad, own, peer, vec, stats, source, gmid=None):
    first = gmid is not None
    extra = (*source, gmid) if first else source
    held = [pltpu.VMEM((PIX, HALF), BF if first else F32)] * 2
    held += [pltpu.VMEM((PIX, C), F32)] if first else []
    outs = (shape(PIX, HALF, F32 if first else BF),) * 2
    return pl.pallas_call(
        functools.partial(dgrad_kernel, first),
        out_shape=outs + (shape(8, C, F32),),
        in_specs=[SM, SM, HBM, HBM, VM] + [VM] * (len(grad) + len(stats)) + [HBM] * len(extra),
        out_specs=(VM,) * 3,
        scratch_shapes=[pltpu.VMEM((9, C, C), BF), pltpu.VMEM((2, BAND, 3 * C), BF),
                        pltpu.VMEM((PIX, C), F32), pltpu.VMEM((8, C), F32),
                        pltpu.SemaphoreType.DMA((4, 4))] + held,
        name="dgrad1" if first else "dgrad2", compiler_params=params(16), cost_estimate=cost(10),
    )(core, eq, *in_hbm(own, peer), vec, *grad, *stats, *in_hbm(*extra))


EVERY, TIED, SMALL_FROM = "asrf", 9, 0
ORDERS = {
    "second": ((2, 0, 1), (0, 1, 2)),
    "attn": ((1, 2, 0), (1, 2, 0)),
    "first": ((0, 1, 2), (2, 0, 1)),
    "rest": ((1, 2, 0), (1, 2, 0)),
}


def orders_of(kind, size):
    bits = size.bit_length() - 1
    return [[*order, *range(3, bits)] for order in ORDERS[kind]]


def exchange(array, orders, stage, size):
    moves = [((d, c), (d ^ (1 << orders[c][stage]), c)) for d in range(size) for c in range(2)]
    return lax.ppermute(array, ("dp", "chan"), [(a[0] * 2 + a[1], b[0] * 2 + b[1]) for a, b in moves])


def side_of(orders, stage):
    bit = jnp.where(lax.axis_index("chan") == 0, orders[0][stage], orders[1][stage])
    return (lax.axis_index("dp") >> bit) & 1


def side_base(orders):
    base = 0
    for stage in range(len(orders[0])):
        base = base * 2 + side_of(orders, stage)
    return base


class Chain:
    def __init__(self, part, kind, size):
        self.value, self.size, self.orders, self.step = part, size, orders_of(kind, size), 0
        self.stages, self.rows = len(self.orders[0]), part.shape[0]

    def advance(self):
        stage = self.step if self.step < self.stages else 2 * self.stages - 1 - self.step
        if self.step < self.stages:
            half = self.value.shape[0] // 2
            side = side_of(self.orders, stage)
            send = lax.dynamic_slice_in_dim(self.value, (1 - side) * half, half, 0)
            keep = lax.dynamic_slice_in_dim(self.value, side * half, half, 0)
            self.value = keep + exchange(send, self.orders, stage, self.size)
        else:
            back = exchange(self.value, self.orders, stage, self.size)
            self.value = jnp.concatenate([self.value, back], 0) if stage > 0 else (self.value, back)
        self.step += 1


def together(chains, *values):
    held = lax.optimization_barrier(([c.value for c in chains], values))
    for chain, value in zip(chains, held[0]):
        chain.value = value
    return held[1]


def after(value, *others):
    return lax.optimization_barrier((value, *others))[0]


def spread_kernel(plan, base_ref, *refs):
    count = len(plan)
    ins, out_hbm, wide, sems = refs[:count], refs[-2 * count - 1], refs[-2 * count : -count], refs[-count:]
    copies = []
    for index, (start, first, rows) in enumerate(plan):
        wide[index][...] = ins[index][...].astype(F32)
        for block in range(ins[index].shape[0] // rows):
            row = start + ((block + first) ^ base_ref[index]) * rows
            copies.append(fetch(
                wide[index].at[block * rows : (block + 1) * rows, :],
                out_hbm.at[pl.ds(pl.multiple_of(row, rows & -rows), rows), :],
                sems[index].at[block]))
    wait_all(copies)


def spread(parts, rows, token, into=None):
    plan = [(start, first, chain.rows // chain.size) for _, chain, start, first in parts]
    arrays = [part[0] for part in parts]
    base = jnp.stack([side_base(part[1].orders) for part in parts]).astype(jnp.int32)
    held = () if into is None else (into,)
    return pl.pallas_call(
        functools.partial(spread_kernel, plan), out_shape=pltpu.HBM((rows, HALF), F32),
        in_specs=[SM] + [VM] * len(arrays) + [HBM] * len(held), out_specs=HBM,
        input_output_aliases={} if into is None else {1 + len(arrays): 0},
        scratch_shapes=[pltpu.VMEM(array.shape, F32) for array in arrays]
        + [pltpu.SemaphoreType.DMA((array.shape[0] // one[2],)) for array, one in zip(arrays, plan)],
        compiler_params=params(14), name="spread", cost_estimate=cost(2),
    )(after(base, token), *arrays, *held)


def second_target(row):
    return 0, row // C * HALF + row % HALF, slice(row // HALF % 2 * HALF, (row // HALF % 2 + 1) * HALF)


def attn_target(row):
    if row < 3 * C:
        return row // C, row % C, slice(0, HALF)
    row -= 3 * C
    return 3, row % HALF, slice(row // HALF * HALF, (row // HALF + 1) * HALF)


def place_kernel(size, targets, base_ref, *refs):
    ins, outs, held = refs[: 2 * len(targets)], refs[2 * len(targets) : -1], refs[-1]
    start = 0
    for index, target in enumerate(targets):
        part, part2 = ins[2 * index : 2 * index + 2]
        half = part.shape[0]
        held[start : start + half, :] = part[...]
        held[start + half : start + 2 * half, :] = part2[...]
        rows = 2 * half // size
        piece = math.gcd(rows, HALF)
        for row in range(0, 2 * half, piece):
            source = ((row // rows) ^ base_ref[index]) * rows + row % rows + start
            which, at, columns = target(row)
            outs[which][at : at + piece, columns] = held[
                pl.ds(pl.multiple_of(source, piece), piece), :].astype(F32)
        start += 2 * half


def place(chains, targets, shapes, token):
    parts = [part for chain in chains for part in chain.value]
    rows = sum(part.shape[0] for part in parts)
    base = jnp.stack([side_base(chain.orders) for chain in chains]).astype(jnp.int32)
    return pl.pallas_call(
        functools.partial(place_kernel, chains[0].size, targets),
        out_shape=tuple(shape(*one, F32) for one in shapes), in_specs=[SM] + [VM] * len(parts),
        out_specs=(VM,) * len(shapes), scratch_shapes=[pltpu.VMEM((rows, HALF), BF)],
        compiler_params=params(12), name="place", cost_estimate=cost(2),
    )(after(base, token), *parts)


def swap(array):
    return lax.ppermute(array, "chan", [(0, 1), (1, 0)])


def shards(pixels, tile_ids, first_gain, first_shift, first_conv, first_bias, second_gain,
           second_shift, second_conv, second_bias, attn_gain, attn_shift, query_weight,
           query_bias, key_weight, value_weight, value_bias, proj_weight, proj_bias, cotangent,
           *, size):
    index = lax.axis_index("chan")
    core = index.reshape(1).astype(jnp.int32)
    tiles = tile_ids.reshape(2, 2, 16, 2, 16)[:, :, 0, :, 0].reshape(2, 4)
    eqs = (tiles[:, :, None] == tiles[:, None, :]).astype(F32).reshape(2, 16)
    eqs = jnp.where(index == 0, eqs, eqs[::-1])
    own_vectors = jnp.stack([first_gain, first_shift, first_bias, second_gain, second_shift,
                             second_bias, attn_gain, attn_shift, query_bias, value_bias, proj_bias])
    pixels_peer = swap(pixels)
    pixels_peer, own_vectors, eqs = lax.optimization_barrier((pixels_peer, own_vectors, eqs))
    eq = eqs[0]
    peer_vectors = swap(own_vectors)
    first_conv, peer_vectors, pixels_peer = lax.optimization_barrier(
        (first_conv, peer_vectors, pixels_peer))
    first_peer = swap(first_conv)
    weights = lax.optimization_barrier(
        (query_weight, key_weight, value_weight, proj_weight, peer_vectors))[:4]
    weights_peer = [swap(array) for array in weights]
    vectors = jnp.concatenate([own_vectors, peer_vectors], 1)
    x = (pixels, pixels_peer)
    act_own, act_peer, stat_own, stat_peer, band, conv1_own, act2_own, stat2_own = front_call(
        core, eq, *x, first_conv, own_vectors, peer_vectors)
    first_peer, act2_own, act_own, act_peer, second_conv, cotangent, *weights_peer = (
        lax.optimization_barrier((first_peer, act2_own, act_own, act_peer, second_conv, cotangent,
                                  *weights_peer)))
    second_peer, g_peer = swap(second_conv), swap(cotangent)
    act_other = (swap(act_peer), swap(act_own))
    conv1_peer, act2_peer, stat2_peer = front_peer_call(core, eq, band, first_peer, peer_vectors)
    act2_peer, second_peer, g_peer = lax.optimization_barrier((act2_peer, second_peer, g_peer))
    g = (cotangent, g_peer)
    act2_other = swap(act2_peer)
    out_own, out_peer, gmid, gconv2, small3, *parts, normed = attn_call(
        core, eq, (act2_own, act2_peer), second_conv, second_peer, x, g,
        list(zip(weights, weights_peer)), vectors)
    gconv2, act2_other, *act_other = lax.optimization_barrier((gconv2, act2_other, *act_other))
    gconv2_other = swap(gconv2)
    dattn, dattn_peer = attn_wgrad_call(core, normed, *parts, g)
    dattn, gconv2, gconv2_other = lax.optimization_barrier((dattn, gconv2, gconv2_other))
    attn_other = swap(dattn_peer)
    part = wgrad2_call(core, eqs, act2_own, act2_other, gconv2, gconv2_other)
    attn_other, part = lax.optimization_barrier((attn_other, part))
    second, attn_sum = Chain(part, "second", size), Chain(dattn + attn_other, "attn", size)
    (gconv2,) = together([second, attn_sum], gconv2)

    for chain in (attn_sum, second):
        chain.advance()
    gconv1_own, gconv1_peer, small2 = dgrad_call(
        core, eq, (gconv2,), second_conv, second_peer, vectors, (stat2_own, stat2_peer),
        (conv1_own, conv1_peer))
    gconv1_other = swap(gconv1_peer)
    gconv1_own, gconv1_other = together([second, attn_sum], gconv1_own, gconv1_other)

    for chain in (attn_sum, second):
        chain.advance()
    part, tail = wgrad1_call(core, eqs, gconv1_own, gconv1_other, act_own, act_peer, *act_other)
    first, rest = Chain(part, "first", size), Chain(tail, "rest", size)
    (gconv1_own,) = together([second, attn_sum, first, rest], gconv1_own)

    known = {"a": attn_sum, "s": second, "r": rest, "f": first}
    every = [known[name] for name in EVERY]
    for chain in every:
        chain.advance()
    pix_own, pix_peer, small1 = dgrad_call(core, eq, (gconv1_own, gconv1_peer), first_conv,
                                           first_peer, vectors, (stat_own, stat_peer), x, gmid)
    small = jnp.concatenate([small1, small2, small3], 0)
    pix_peer, out_peer, small = together(every, pix_peer, out_peer, small)

    small = small[:, :HALF] + swap(small[:, HALF:])
    pix_back = swap(pix_peer)
    out_back = swap(out_peer)
    bits = size.bit_length() - 1
    turn, bit = 0, 0
    token = core
    while any(chain.step < 2 * bits for chain in every):
        for chain in every:
            if chain.step < 2 * bits:
                chain.advance()
                if turn < TIED:
                    (token,) = together([chain], token)
        if turn >= SMALL_FROM and bit < bits:
            small = small + lax.ppermute(
                small, "dp", [(i, i ^ (1 << bit)) for i in range(size)])
            small, token = lax.optimization_barrier((small, token))
            bit += 1
        turn += 1
    (sums2,) = place([second], [second_target], [(9 * HALF, C)], core)
    sums3 = place([attn_sum], [attn_target], [(C, HALF), (C, HALF), (C, HALF), (HALF, C)], core)
    mine, back = first.value
    half = size // 2
    sums1 = spread([(rest.value[0], rest, TAPS * C, 0), (mine, first, 0, 0)], 9 * C, core)
    sums1 = spread([(rest.value[1], rest, TAPS * C, half), (back, first, 0, half)], 9 * C, token, sums1)

    def unboth(own, back):
        return jnp.where(index == 0, jnp.stack([own, back]), jnp.stack([back, own]))

    return (
        unboth(out_own, out_back), unboth(pix_own, pix_back), small[0], small[1],
        sums1.reshape(9, C, HALF), small[10], small[8], small[9], sums2.reshape(9, HALF, C),
        small[21], small[16], small[17], sums3[0], small[18], sums3[1], sums3[2], small[19],
        sums3[3], small[20],
    )


def solution(mesh):
    chan = P("chan")
    rows = P("dp", None, "chan")
    return jax.shard_map(
        functools.partial(shards, size=mesh.shape["dp"]),
        mesh=mesh,
        in_specs=(
            rows, P("dp", None), chan, chan, P(None, None, "chan"), chan, chan, chan,
            P(None, "chan", None), chan, chan, chan, P(None, "chan"), chan, P(None, "chan"),
            P(None, "chan"), chan, P("chan", None), chan, rows,
        ),
        out_specs=(
            rows, rows, chan, chan, P(None, None, "chan"), chan, chan, chan,
            P(None, "chan", None), chan, chan, chan, P(None, "chan"), chan, P(None, "chan"),
            P(None, "chan"), chan, P("chan", None), chan,
        ),
        check_vma=False,
    )
```
